32 devices in a mesh: section: 2 (over core), dp: 4 (over z), mp: 4 (over y, x).
Axes of the slice: x: 2, y: 2, z: 4, core: 2. Of those that a mesh axis runs over, the one named last changes fastest.
Arguments:
- tokens: bfloat16 [2, 8192, 1024], P(None, ('dp', 'mp')), may hold values from -6 to 6
- layout: int32 [2, 4], P(None, 'dp'), may hold values from 1 to 2, as said below
- cotangent: float32 [2, 8192, 1024], P(None, ('dp', 'mp')), may hold values from -6 to 6
- attn_gain: float32 [2, 1024], P('section'), may hold values from 0.5 to 1.5
- query_weight: bfloat16 [2, 1024, 1024], P('section', None, 'mp'), may hold values from -0.1875 to 0.1875
- key_weight: bfloat16 [2, 1024, 1024], P('section', None, 'mp'), may hold values from -0.1875 to 0.1875
- value_weight: bfloat16 [2, 1024, 1024], P('section', None, 'mp'), may hold values from -0.1875 to 0.1875
- out_weight: bfloat16 [2, 1024, 1024], P('section', 'mp'), may hold values from -1.5 to 1.5
- ffn_gain: float32 [2, 1024], P('section'), may hold values from 0.5 to 1.5
- gate_weight: bfloat16 [2, 1024, 2816], P('section', None, 'mp'), may hold values from -0.1875 to 0.1875
- up_weight: bfloat16 [2, 1024, 2816], P('section', None, 'mp'), may hold values from -0.1875 to 0.1875
- down_weight: bfloat16 [2, 2816, 1024], P('section', 'mp'), may hold values from -0.109375 to 0.109375
Outputs:
- layer_out: bfloat16 [2, 2, 8192, 1024], P('section', None, ('dp', 'mp'))
- input_grads: float32 [2, 2, 8192, 1024], P('section', None, ('dp', 'mp'))
- first_values: bfloat16 [2, 8192, 1024], P(None, 'dp', 'mp')
- value_norms: float32 [2, 16], replicated
- attn_gain_grad: float32 [2, 1024], P('section')
- query_grad: float32 [2, 1024, 1024], P('section', None, 'mp')
- key_grad: float32 [2, 1024, 1024], P('section', None, 'mp')
- value_grad: float32 [2, 1024, 1024], P('section', None, 'mp')
- out_grad: float32 [2, 1024, 1024], P('section', 'mp')
- ffn_gain_grad: float32 [2, 1024], P('section')
- gate_grad: float32 [2, 1024, 2816], P('section', None, 'mp')
- up_grad: float32 [2, 1024, 2816], P('section', None, 'mp')
- down_grad: float32 [2, 2816, 1024], P('section', 'mp')
The draws below stay inside these ranges and needn't reach their ends.
Inputs may be any that keep to these rules, and one draw needn't show every extreme that they name: layout[m, d] is 1 or 2; for each data index d, 1 of the micro-batches hold 1.
All inputs are finite; a program needn't handle non-finite values.
Results may differ from the reference program's by a relative error of at most 0.028.
Values may be sent and summed in bfloat16 or wider, within the bound.
No kernel may reach another device: no remote copies, remote signals or barrier semaphores. Data moves between devices by JAX's collectives and lax.ppermute only.
A program may use at most 384 MiB of HBM per device.

```python
import jax
import jax.numpy as jnp
from jax import lax

D = 1024
HEAD_DIM = 64
FF = 2816
PACK = 2048
MICRO = 2
ROWS = 8192
N_DP = 4


def draw_layout(key, part):
    column_keys = jax.random.split(jax.random.fold_in(key, 7), N_DP)
    orders = jax.vmap(lambda column_key: jax.random.permutation(column_key, jnp.arange(MICRO, dtype=jnp.int32)))(column_keys)
    return jnp.where(orders.T < MICRO // 2, 1, 2).astype(jnp.int32)


def shard_levels(rng, shape, cuts, least, high):
    level, own = 1.0, jax.random.fold_in(rng, 6)
    for axis_at, parts in cuts:
        steps = jnp.exp(jax.random.uniform(jax.random.fold_in(own, axis_at), (parts,), jnp.float32, least / len(cuts), high / len(cuts)))
        level = level * jnp.repeat(steps, shape[axis_at] // parts).reshape([-1 if axis == axis_at else 1 for axis in range(len(shape))])
    return level


def gaussian(own_key, shape, width, most, pieces=(), held_as=jnp.bfloat16):
    result = width * jax.random.normal(own_key, shape, jnp.float32)
    if pieces:
        result = result * shard_levels(own_key, shape, pieces, -0.22, 0.18)
    return jnp.clip(result, -most, most).astype(held_as)


def setup_inputs(seed: int = 0) -> dict:
    splits = jax.random.split(jax.random.key(seed), 13)
    tokens = gaussian(splits[0], (MICRO, ROWS, D), 1.0, 6.0, ((1, 16),))
    layout = draw_layout(jax.random.fold_in(splits[12], 71), 0)
    cotangent = gaussian(splits[2], (MICRO, ROWS, D), 1.0, 6.0, ((1, 16),), jnp.float32)
    attn_gain = jnp.clip(1.0 + 0.1 * jax.random.normal(splits[3], (2, D), jnp.float32), 0.5, 1.5)
    query_weight = gaussian(splits[4], (2, D, D), D ** -0.5, 0.1875, ((0, 2), (2, 4)))
    key_weight = gaussian(splits[5], (2, D, D), D ** -0.5, 0.1875, ((0, 2), (2, 4)))
    value_weight = gaussian(splits[6], (2, D, D), D ** -0.5, 0.1875, ((0, 2), (2, 4)))
    out_weight = gaussian(splits[7], (2, D, D), (D // 64) ** -0.5, 1.5, ((0, 2), (1, 4)))
    ffn_gain = jnp.clip(1.0 + 0.1 * jax.random.normal(splits[8], (2, D), jnp.float32), 0.5, 1.5)
    gate_weight = gaussian(splits[9], (2, D, FF), D ** -0.5, 0.1875, ((0, 2), (2, 4)))
    up_weight = gaussian(splits[10], (2, D, FF), D ** -0.5, 0.1875, ((0, 2), (2, 4)))
    down_weight = gaussian(splits[11], (2, FF, D), FF ** -0.5, 0.109375, ((0, 2), (1, 4)))
    return dict(tokens=tokens, layout=layout, cotangent=cotangent, attn_gain=attn_gain, query_weight=query_weight, key_weight=key_weight, value_weight=value_weight, out_weight=out_weight, ffn_gain=ffn_gain, gate_weight=gate_weight, up_weight=up_weight, down_weight=down_weight)


@jax.custom_vjp
def low(v):
    return lax.optimization_barrier(v.astype(jnp.bfloat16)).astype(jnp.float32)

@jax.custom_vjp
def low_back(v):
    return v

def low_keep(v):
    return (low(v), None)

def low_pass(kept, grad):
    return (grad,)

def back_keep(v):
    return (v, None)

def back_low(kept, grad):
    return (low(grad),)
low.defvjp(low_keep, low_pass)
low_back.defvjp(back_keep, back_low)

def matmul(left, right):
    return jnp.einsum('rpd,df->rpf', left, right, precision=lax.Precision.HIGHEST)

def normalize(rows_in, gain):
    return rows_in * lax.rsqrt(lax.optimization_barrier(jnp.mean(rows_in * rows_in, axis=-1, keepdims=True)) + 1e-05) * gain

def rotary(seq_rows, seg_len):
    positions = (jnp.arange(seq_rows, dtype=jnp.int32) % seg_len).astype(jnp.float32)
    inverse_freq = 10000.0 ** (-(jnp.arange(HEAD_DIM // 2, dtype=jnp.float32) * 2.0 / HEAD_DIM))
    angles = positions[:, None] * inverse_freq[None, :]
    return (jnp.cos(angles)[:, None, :], jnp.sin(angles)[:, None, :])

def rotate(tensor, cosine, sine_part):
    half_dim = tensor.shape[-1] // 2
    first_half = tensor[..., :half_dim]
    second_half = tensor[..., half_dim:]
    return jnp.concatenate([first_half * cosine - second_half * sine_part, first_half * sine_part + second_half * cosine], axis=-1)

def allowed_mask(seq_rows, seg_len):
    token_index = jnp.arange(seq_rows, dtype=jnp.int32)
    causal = token_index[None, :] <= token_index[:, None]
    same_seq = token_index[:, None] // seg_len == token_index[None, :] // seg_len
    return causal & same_seq

def attend_row(items):
    query_raw, key_raw, mixed, seg_len = items
    seq_rows = query_raw.shape[0]
    cosine, sine_part = rotary(seq_rows, seg_len)
    queries = low(rotate(query_raw, cosine, sine_part))
    keys_rot = low(rotate(key_raw, cosine, sine_part))
    scores = jnp.einsum('qhd,khd->hqk', queries, keys_rot, precision=lax.Precision.HIGHEST) * HEAD_DIM ** (-0.5)
    scores = low_back(jnp.where(allowed_mask(seq_rows, seg_len)[None], scores, -1e+30))
    row_top = lax.optimization_barrier(jnp.max(scores, axis=-1, keepdims=True))
    expo = jnp.exp(scores - row_top)
    probabilities = expo / lax.optimization_barrier(jnp.sum(expo, axis=-1, keepdims=True))
    return jnp.einsum('hqk,khd->qhd', low(probabilities), mixed, precision=lax.Precision.HIGHEST)

def layer_pass(state_rows, params, layer_index, first_in, seq_lengths):
    attn_gain, query_weight, key_weight, value_weight, out_weight, ffn_gain, gate_weight, up_weight, down_weight = [each_param[layer_index] for each_param in params]
    batch_rows, seq_rows, model_width = state_rows.shape
    normed = low(normalize(state_rows, attn_gain))
    query_raw = low_back(matmul(normed, query_weight))
    key_raw = low_back(matmul(normed, key_weight))
    value_raw = low_back(matmul(normed, value_weight))
    if first_in is None:
        mixed = low(value_raw)
    else:
        mixed = low(0.5 * value_raw + 0.5 * low_back(first_in))
    head_shape = (batch_rows, seq_rows, model_width // HEAD_DIM, HEAD_DIM)
    attended = lax.map(jax.checkpoint(attend_row), (query_raw.reshape(head_shape), key_raw.reshape(head_shape), mixed.reshape(head_shape), seq_lengths))
    attended = low_back(low(attended.reshape(batch_rows, seq_rows, model_width)))
    middle = state_rows + low_back(matmul(attended, out_weight))
    normed_ffn = low(normalize(middle, ffn_gain))
    gate_proj = low_back(matmul(normed_ffn, gate_weight))
    up_proj = low_back(matmul(normed_ffn, up_weight))
    activated = low(jax.nn.silu(gate_proj) * up_proj)
    return (middle + low_back(matmul(activated, down_weight)), mixed)

def forward(tokens_f32, h1_offset, params, seq_lengths):
    first_out, first_values = layer_pass(tokens_f32, params, 0, None, seq_lengths)
    second_in = low_back(low(first_out)) + h1_offset
    second_out, unused = layer_pass(second_in, params, 1, first_values, seq_lengths)
    return (second_out, (first_out, first_values))

def reference(tokens, layout, cotangent, attn_gain, query_weight, key_weight, value_weight, out_weight, ffn_gain, gate_weight, up_weight, down_weight):
    micro_count, tok_rows, model_width = tokens.shape
    pack_count = tok_rows // PACK
    tokens_f32 = tokens.astype(jnp.float32).reshape(micro_count * pack_count, PACK, model_width)
    seq_lengths = (PACK // layout).astype(jnp.int32).reshape(micro_count * pack_count)
    params = tuple((each_param.astype(jnp.float32) for each_param in (attn_gain, query_weight, key_weight, value_weight, out_weight, ffn_gain, gate_weight, up_weight, down_weight)))
    h1_offset = jnp.zeros_like(tokens_f32)

    def wrapped(tokens_in, offset_in, params_in):
        return forward(tokens_in, offset_in, params_in, seq_lengths)
    second_out, back_fn, aux_items = jax.vjp(wrapped, tokens_f32, h1_offset, params, has_aux=True)
    first_out, first_values = aux_items
    grad_tokens, grad_offset, grad_params = back_fn(cotangent.astype(jnp.float32).reshape(second_out.shape))
    full_shape = (micro_count, tok_rows, model_width)
    layer_out = jnp.stack([first_out.reshape(full_shape), second_out.reshape(full_shape)]).astype(jnp.bfloat16)
    input_grads = jnp.stack([grad_tokens.reshape(full_shape), grad_offset.reshape(full_shape)])
    first_shaped = first_values.reshape(micro_count, pack_count, PACK, model_width // HEAD_DIM, HEAD_DIM)
    value_norms = lax.optimization_barrier(jnp.sum(first_shaped * first_shaped, axis=(1, 2, 4)))
    return (layer_out, input_grads, first_values.reshape(full_shape).astype(jnp.bfloat16), value_norms, grad_params[0], grad_params[1], grad_params[2], grad_params[3], grad_params[4], grad_params[5], grad_params[6], grad_params[7], grad_params[8])
```

```python
import functools

import jax
import jax.numpy as jnp
from jax import lax
from jax.experimental import pallas as pl
from jax.experimental.pallas import tpu as pltpu
from jax.sharding import PartitionSpec as P

HEAD_DIM = 64
HALF = HEAD_DIM // 2
EPS = 1e-05
SCALE = HEAD_DIM**-0.5
F32 = jnp.float32
BF16 = jnp.bfloat16
VMEM_BYTES = 56 * 1024 * 1024

NT = (((1,), (1,)), ((), ()))
NN = (((1,), (0,)), ((), ()))
TN = (((0,), (0,)), ((), ()))


def mm(left, right, dims=NN):
    return lax.dot_general(left, right, dims, preferred_element_type=F32)


def swap_halves(tensor):
    width = tensor.shape[1]
    if width % 128 == 0:
        lane = lax.broadcasted_iota(jnp.int32, tensor.shape, 1)
        ahead = pltpu.roll(tensor, width - HALF, 1)
        behind = pltpu.roll(tensor, HALF, 1)
        return jnp.where(lane % HEAD_DIM < HALF, ahead, behind)
    return jnp.concatenate([tensor[:, HALF:], tensor[:, :HALF]], axis=1)


def qkv_kernel(second, group, x_ref, w_ref, cos_ref, sin_ref, *refs):
    if second:
        first_ref, q_ref, k_ref, v_ref = refs
    else:
        q_ref, k_ref, v_ref = refs
    width = q_ref.shape[1]
    acc = mm(x_ref[...], w_ref[...])
    cosine, sine = cos_ref[...], sin_ref[...]
    for at in range(0, width, group):
        part = acc[:, at : at + group]
        turned = part * cosine + swap_halves(part) * sine
        q_ref[:, at : at + group] = (turned * SCALE).astype(BF16)
        part = acc[:, width + at : width + at + group]
        turned = part * cosine + swap_halves(part) * sine
        k_ref[:, at : at + group] = turned.astype(BF16)
    value = acc[:, 2 * width :]
    if second:
        value = 0.5 * value + 0.5 * first_ref[...].astype(F32)
    v_ref[...] = value.astype(BF16)


def project_qkv(normed, weight, cosine, sine, first):
    rows, model = normed.shape
    width = weight.shape[1] // 3
    group = min(width, 128)
    block = min(512, rows)
    second = first is not None
    row_spec = pl.BlockSpec((block, width), lambda i: (i, 0))
    in_specs = [
        pl.BlockSpec((block, model), lambda i: (i, 0)),
        pl.BlockSpec((model, 3 * width), lambda i: (0, 0)),
        pl.BlockSpec((block, group), lambda i: (i, 0)),
        pl.BlockSpec((block, group), lambda i: (i, 0)),
    ]
    args = [normed, weight, cosine, sine]
    if second:
        in_specs.append(row_spec)
        args.append(first)
    shape = jax.ShapeDtypeStruct((rows, width), BF16)
    return pl.pallas_call(
        functools.partial(qkv_kernel, second, group),
        grid=(rows // block,),
        in_specs=in_specs,
        out_specs=[row_spec] * 3,
        out_shape=[shape] * 3,
        compiler_params=pltpu.CompilerParams(vmem_limit_bytes=VMEM_BYTES),
        name="qkv_rope",
    )(*args)


def head_lanes(value, head, group):
    per = group // HEAD_DIM
    if per == 1:
        return value
    lane = lax.broadcasted_iota(jnp.int32, value.shape, 1)
    return jnp.where(lane // HEAD_DIM == head % per, value, jnp.zeros_like(value))


def attend_kernel(block, group, len_ref, q_ref, k_ref, v_ref, o_ref, lse_ref, acc_ref, top_ref, sum_ref):
    width = q_ref.shape[1]
    heads = width // HEAD_DIM
    per = group // HEAD_DIM
    step = pl.program_id(0)
    seg_len = len_ref[0]
    first = (step * block // seg_len) * (seg_len // block)
    q_heads = []
    for head in range(heads):
        at = head // per * group
        q_heads.append(head_lanes(q_ref[:, at : at + group], head, group))

    def one(col, masked, start):
        rows = pl.ds(pl.multiple_of(col * block, block), block)
        for pair in range(heads // per):
            at = pair * group
            keys = k_ref[rows, at : at + group]
            values = v_ref[rows, at : at + group]
            total = None
            shrink = None
            for sub in range(per):
                head = pair * per + sub
                scores = mm(q_heads[head], keys, NT)
                if masked:
                    r = lax.broadcasted_iota(jnp.int32, scores.shape, 0)
                    c = lax.broadcasted_iota(jnp.int32, scores.shape, 1)
                    scores = jnp.where(c <= r, scores, -1e30)
                top = jnp.max(scores, axis=1, keepdims=True)
                if not start:
                    old = top_ref[:, head : head + 1]
                    top = jnp.maximum(top, old)
                probs = jnp.exp(scores - top)
                count = jnp.sum(probs, axis=1, keepdims=True)
                if not start:
                    scale = jnp.exp(old - top)
                    count = count + sum_ref[:, head : head + 1] * scale
                    wide = jnp.broadcast_to(scale, (block, group))
                    if shrink is None:
                        shrink = wide
                    else:
                        lane = lax.broadcasted_iota(jnp.int32, wide.shape, 1)
                        shrink = jnp.where(lane // HEAD_DIM == sub, wide, shrink)
                top_ref[:, head : head + 1] = top
                sum_ref[:, head : head + 1] = count
                part = mm(probs.astype(BF16), head_lanes(values, head, group))
                total = part if total is None else total + part
            if start:
                acc_ref[:, at : at + group] = total
            else:
                acc_ref[:, at : at + group] = acc_ref[:, at : at + group] * shrink + total

    one(step, True, True)

    @pl.loop(first, step)
    def _(col):
        one(col, False, False)

    lane = lax.broadcasted_iota(jnp.int32, (block, 128), 1)
    columns = jnp.zeros((block, 128), F32)
    for head in range(heads):
        value = top_ref[:, head : head + 1] + jnp.log(sum_ref[:, head : head + 1])
        columns = jnp.where(lane == head, value, columns)
    lse_ref[...] = columns.T[: lse_ref.shape[0]]
    for pair in range(heads // per):
        at = pair * group
        over = None
        for sub in range(per):
            head = pair * per + sub
            wide = jnp.broadcast_to(1.0 / sum_ref[:, head : head + 1], (block, group))
            if over is None:
                over = wide
            else:
                sub_lane = lax.broadcasted_iota(jnp.int32, wide.shape, 1)
                over = jnp.where(sub_lane // HEAD_DIM == sub, wide, over)
        o_ref[:, at : at + group] = (acc_ref[:, at : at + group] * over).astype(BF16)


def attend(queries, keys, values, seg_len):
    rows, width = queries.shape
    group = min(width, 128)
    heads = width // HEAD_DIM
    block = min(512, rows // 2)
    whole = pl.BlockSpec((rows, width), lambda i, n: (0, 0))
    return pl.pallas_call(
        functools.partial(attend_kernel, block, group),
        grid_spec=pltpu.PrefetchScalarGridSpec(
            num_scalar_prefetch=1,
            grid=(rows // block,),
            in_specs=[pl.BlockSpec((block, width), lambda i, n: (i, 0)), whole, whole],
            out_specs=[
                pl.BlockSpec((block, width), lambda i, n: (i, 0)),
                pl.BlockSpec((heads, block), lambda i, n: (0, i)),
            ],
            scratch_shapes=[
                pltpu.VMEM((block, width), F32),
                pltpu.VMEM((block, 128), F32),
                pltpu.VMEM((block, 128), F32),
            ],
        ),
        out_shape=[
            jax.ShapeDtypeStruct((rows, width), BF16),
            jax.ShapeDtypeStruct((heads, rows), F32),
        ],
        compiler_params=pltpu.CompilerParams(vmem_limit_bytes=VMEM_BYTES),
        name="attend",
    )(seg_len, queries, keys, values)


def attend_back_kernel(second, block, group, len_ref, q_ref, k_ref, v_ref, o_ref, do_ref, lse_ref, cos_ref, sin_ref, *refs):
    if second:
        out_ref, dq_ref, dk_ref, dv_ref, delta_ref = refs
    else:
        first_ref, out_ref, dq_ref, dk_ref, dv_ref, delta_ref = refs
    rows, width = q_ref.shape
    heads = width // HEAD_DIM
    per = group // HEAD_DIM
    step = pl.program_id(0)
    steps = rows // block
    seg_len = len_ref[0]
    per_seg = seg_len // block
    last = (step // per_seg + 1) * per_seg

    @pl.when(step == 0)
    def _():
        dq_ref[...] = jnp.zeros_like(dq_ref)
        head = lax.broadcasted_iota(jnp.int32, (8, width), 0)
        lane = lax.broadcasted_iota(jnp.int32, (8, width), 1)
        pick = jnp.where(lane // HEAD_DIM == head, 1.0, 0.0).astype(F32)
        for at in range(0, rows, block):
            prod = do_ref[at : at + block, :].astype(F32) * o_ref[at : at + block, :].astype(F32)
            delta_ref[:, at : at + block] = lax.dot_general(
                pick, prod, NT, precision=lax.Precision.HIGHEST, preferred_element_type=F32
            )

    key_rows = pl.ds(pl.multiple_of(step * block, block), block)

    def one(row, masked):
        query_rows = pl.ds(pl.multiple_of(row * block, block), block)
        for pair in range(heads // per):
            at = pair * group
            keys = k_ref[key_rows, at : at + group]
            values = v_ref[key_rows, at : at + group]
            queries = q_ref[query_rows, at : at + group]
            grads = do_ref[query_rows, at : at + group]
            dq = dk = dv = None
            for sub in range(per):
                head = pair * per + sub
                q_one = head_lanes(queries, head, group)
                do_one = head_lanes(grads, head, group)
                scores = mm(keys, q_one, NT)
                probs = jnp.exp(scores - lse_ref[head : head + 1, query_rows])
                if masked:
                    r = lax.broadcasted_iota(jnp.int32, scores.shape, 0)
                    c = lax.broadcasted_iota(jnp.int32, scores.shape, 1)
                    probs = jnp.where(r <= c, probs, 0.0)
                g_probs = mm(values, do_one, NT)
                g_scores = (probs * (g_probs - delta_ref[head : head + 1, query_rows])).astype(BF16)
                dv_one = mm(probs.astype(BF16), do_one)
                dk_one = mm(g_scores, q_one)
                dq_one = mm(g_scores, head_lanes(keys, head, group), TN)
                dq = dq_one if dq is None else dq + dq_one
                dk = dk_one if dk is None else dk + dk_one
                dv = dv_one if dv is None else dv + dv_one
            dq_ref[query_rows, at : at + group] += dq
            if masked:
                dk_ref[:, at : at + group] = dk
                dv_ref[:, at : at + group] = dv
            else:
                dk_ref[:, at : at + group] += dk
                dv_ref[:, at : at + group] += dv

    one(step, True)

    @pl.loop(step + 1, last)
    def _(row):
        one(row, False)

    def turn_back(value, at_rows):
        return value * cos_ref[at_rows, :] - swap_halves(value) * sin_ref[at_rows, :]

    for at in range(0, width, group):
        out_ref[key_rows, width + at : width + at + group] = turn_back(dk_ref[:, at : at + group], key_rows).astype(BF16)
        out_ref[key_rows, at : at + group] = turn_back(dq_ref[key_rows, at : at + group] * SCALE, key_rows).astype(BF16)
    if second:
        g_value = 0.5 * dv_ref[...]
    else:
        g_value = dv_ref[...] + first_ref[key_rows, :].astype(F32)
    out_ref[key_rows, 2 * width :] = g_value.astype(BF16)


def attend_back(queries, keys, values, attended, grads, lse, cosine, sine, g_first, seg_len):
    rows, width = queries.shape
    group = min(width, 128)
    heads = width // HEAD_DIM
    block = min(512, rows // 2)
    second = g_first is None
    whole = pl.BlockSpec((rows, width), lambda i, n: (0, 0))
    table = pl.BlockSpec((rows, group), lambda i, n: (0, 0))
    in_specs = [whole] * 5 + [pl.BlockSpec((heads, rows), lambda i, n: (0, 0)), table, table]
    args = [queries, keys, values, attended, grads, lse, cosine, sine]
    if not second:
        in_specs.append(whole)
        args.append(g_first)
    return pl.pallas_call(
        functools.partial(attend_back_kernel, second, block, group),
        grid_spec=pltpu.PrefetchScalarGridSpec(
            num_scalar_prefetch=1,
            grid=(rows // block,),
            in_specs=in_specs,
            out_specs=pl.BlockSpec((rows, 3 * width), lambda i, n: (0, 0)),
            scratch_shapes=[
                pltpu.VMEM((rows, width), F32),
                pltpu.VMEM((block, width), F32),
                pltpu.VMEM((block, width), F32),
                pltpu.VMEM((8, rows), F32),
            ],
        ),
        out_shape=jax.ShapeDtypeStruct((rows, 3 * width), BF16),
        compiler_params=pltpu.CompilerParams(vmem_limit_bytes=VMEM_BYTES),
        name="attend_back",
    )(seg_len, *args)


def normalize(rows_in, gain):
    scale = lax.rsqrt(jnp.mean(rows_in * rows_in, axis=-1, keepdims=True) + EPS)
    return rows_in * scale * gain


def normalize_back(rows_in, gain, grad):
    scale = lax.rsqrt(jnp.mean(rows_in * rows_in, axis=-1, keepdims=True) + EPS)
    gained = grad * gain
    inner = jnp.mean(gained * rows_in, axis=-1, keepdims=True)
    g_rows = scale * (gained - rows_in * (scale * scale * inner))
    return g_rows, jnp.sum(grad * (rows_in * scale), axis=0)


def rotary_tables(rows, seg_len, lanes):
    positions = (jnp.arange(rows, dtype=jnp.int32) % seg_len).astype(F32)
    inverse_freq = 10000.0 ** (-(jnp.arange(HALF, dtype=F32) * 2.0 / HEAD_DIM))
    angles = positions[:, None] * inverse_freq[None, :]
    cosine, sine = jnp.cos(angles), jnp.sin(angles)
    cosine = jnp.concatenate([cosine, cosine] * (lanes // HEAD_DIM), axis=1)
    sine = jnp.concatenate([-sine, sine] * (lanes // HEAD_DIM), axis=1)
    return cosine, sine


def swap_cores(value):
    return lax.ppermute(value, "section", [(0, 1), (1, 0)])


def pick_half(value, which, axis=0):
    size = value.shape[axis] // 2
    return lax.dynamic_slice_in_dim(value, which * size, size, axis)


def shards(
    tokens,
    layout,
    cotangent,
    attn_gain,
    query_weight,
    key_weight,
    value_weight,
    out_weight,
    ffn_gain,
    gate_weight,
    up_weight,
    down_weight,
):
    core = lax.axis_index("section")
    is_low = core == 0
    micro_count, tok_rows, model = tokens.shape
    mp = lax.axis_size("mp")
    seq_rows = tok_rows * mp
    width = query_weight.shape[2]
    hidden = gate_weight.shape[2]
    hid_half = hidden // 2
    out_half = width // 2
    group = min(width, 128)

    def in_order(own, other):
        return jnp.where(is_low, own, other), jnp.where(is_low, other, own)

    inputs = lax.dynamic_index_in_dim(tokens, core, 0, keepdims=False)
    g_top = lax.dynamic_index_in_dim(cotangent, core, 0, keepdims=False)
    pack_layout = lax.dynamic_index_in_dim(layout[:, 0], core, 0, keepdims=False)
    seg_len = (seq_rows // pack_layout).astype(jnp.int32)
    seg_arg = seg_len.reshape(1)
    cosine, sine = rotary_tables(seq_rows, seg_len, group)

    own_qkv = jnp.concatenate([query_weight[0], key_weight[0], value_weight[0]], axis=1)
    qkv_weights = in_order(own_qkv, swap_cores(own_qkv))
    gains = jnp.concatenate([attn_gain, ffn_gain], axis=0)
    gain_first, gain_second = in_order(gains, swap_cores(gains))
    halves = jnp.concatenate(
        [
            gate_weight[0].T.reshape(2, hid_half, model),
            up_weight[0].T.reshape(2, hid_half, model),
            down_weight[0].reshape(2, hid_half, model),
            out_weight[0].reshape(2, out_half, model),
        ],
        axis=1,
    )
    kept = lax.dynamic_index_in_dim(halves, core, 0, keepdims=False)
    sent = lax.dynamic_index_in_dim(halves, 1 - core, 0, keepdims=False)
    packs = in_order(kept, swap_cores(sent))
    pack_rows = packs[0].shape[0]

    def unpack(pack):
        parts = pack.reshape(mp, pack_rows, model)
        gate_t = parts[:, :hid_half].reshape(mp * hid_half, model)
        up_t = parts[:, hid_half : 2 * hid_half].reshape(mp * hid_half, model)
        down = parts[:, 2 * hid_half : 3 * hid_half].reshape(mp * hid_half, model)
        return gate_t, up_t, down, parts[:, 3 * hid_half :]

    def gathered(pack):
        own = lax.all_gather(pack, "mp", axis=0, tiled=True)
        other = swap_cores(own)
        own, other = unpack(own), unpack(other)
        low, high = in_order(own[3], other[3])
        out_full = jnp.concatenate([low, high], axis=1).reshape(mp * width, model)
        return own[:3], other[:3], out_full

    layers = []
    for layer in range(2):
        gain_pair = (gain_first, gain_second)[layer]
        own, other, out_full = gathered(packs[layer])
        layers.append((gain_pair[0], gain_pair[1], qkv_weights[layer], own, other, out_full))

    def to_owners(value):
        blocks = value.reshape(mp, tok_rows, width)
        moved = lax.all_to_all(blocks, "mp", 0, 0)
        return jnp.transpose(moved, (1, 0, 2)).reshape(tok_rows, mp * width)

    def to_heads(value):
        blocks = jnp.transpose(value.reshape(tok_rows, mp, width), (1, 0, 2))
        return lax.all_to_all(blocks, "mp", 0, 0).reshape(seq_rows, width)

    def forward(rows_low, first, weights):
        gain_a, gain_f, qkv_w, own, other, out_full = weights
        state = rows_low.astype(F32)
        normed = normalize(state, gain_a).astype(BF16)
        normed_all = lax.all_gather(normed, "mp", axis=0, tiled=True)
        queries, keys, values = project_qkv(normed_all, qkv_w, cosine, sine, first)
        attended, lse = attend(queries, keys, values, seg_arg)
        att_rows = to_owners(attended)
        middle = state + mm(att_rows, out_full)
        normed_ffn = normalize(middle, gain_f).astype(BF16)
        result = middle
        inner = []
        for gate_t, up_t, down in (own, other):
            gate = mm(normed_ffn, gate_t, NT)
            up = mm(normed_ffn, up_t, NT)
            activated = (jax.nn.silu(gate) * up).astype(BF16)
            result = result + mm(activated, down)
            inner.append((gate, up, activated))
        kept_items = (state, normed_all, queries, keys, values, attended, lse, att_rows, middle, normed_ffn, inner)
        return result.astype(BF16), values, kept_items

    def backward(g_result, g_first, weights, kept_items):
        gain_a, gain_f, qkv_w, own, other, out_full = weights
        state, normed_all, queries, keys, values, attended, lse, att_rows, middle, normed_ffn, inner = kept_items
        g_branch = g_result.astype(BF16)
        g_normed = None
        g_inner = []
        for (gate, up, activated), (gate_t, up_t, down) in zip(inner, (own, other)):
            g_act = mm(g_branch, down, NT)
            sig = jax.nn.sigmoid(gate)
            g_up = (g_act * (gate * sig)).astype(BF16)
            g_gate = (g_act * up * (sig * (1.0 + gate * (1.0 - sig)))).astype(BF16)
            part = mm(g_gate, gate_t) + mm(g_up, up_t)
            g_normed = part if g_normed is None else g_normed + part
            g_inner.append((g_gate, g_up, activated))
        g_norm, g_gain_f = normalize_back(middle, gain_f, g_normed)
        g_middle = g_result + g_norm
        g_mid_low = g_middle.astype(BF16)
        g_att = to_heads(mm(g_mid_low, out_full, NT).astype(BF16))
        g_qkv = attend_back(queries, keys, values, attended, g_att, lse, cosine, sine, g_first, seg_arg)
        g_normed_part = mm(g_qkv, qkv_w, NT).astype(BF16)
        g_normed_attn = lax.psum_scatter(g_normed_part, "mp", scatter_dimension=0, tiled=True).astype(F32)
        g_norm, g_gain_a = normalize_back(state, gain_a, g_normed_attn)
        g_inputs = g_middle + g_norm

        sent_rows = jnp.concatenate(list(g_inner[1]) + [normed_ffn, g_branch], axis=1)
        got = swap_cores(sent_rows)
        hid_all = mp * hid_half
        got_gate, got_up, got_act = (got[:, i * hid_all : (i + 1) * hid_all] for i in range(3))
        got_normed = got[:, 3 * hid_all : 3 * hid_all + model]
        got_branch = got[:, 3 * hid_all + model :]
        gate_grad = mm(g_inner[0][0], normed_ffn, TN) + mm(got_gate, got_normed, TN)
        up_grad = mm(g_inner[0][1], normed_ffn, TN) + mm(got_up, got_normed, TN)
        down_grad = mm(g_inner[0][2], g_branch, TN) + mm(got_act, got_branch, TN)
        out_grad = mm(att_rows, g_mid_low, TN).astype(BF16).reshape(mp, 2, out_half, model)
        out_kept = lax.dynamic_index_in_dim(out_grad, core, 1, keepdims=False)
        out_sent = lax.dynamic_index_in_dim(out_grad, 1 - core, 1, keepdims=False)
        out_grad = out_kept.astype(F32) + swap_cores(out_sent).astype(F32)
        grads = jnp.concatenate(
            [
                gate_grad.astype(BF16).reshape(mp, hid_half, model),
                up_grad.astype(BF16).reshape(mp, hid_half, model),
                down_grad.astype(BF16).reshape(mp, hid_half, model),
                out_grad.astype(BF16),
            ],
            axis=1,
        ).reshape(mp * pack_rows, model)
        grads = lax.psum_scatter(grads, "mp", scatter_dimension=0, tiled=True)
        grads = lax.psum(grads, "dp")
        qkv_grad = mm(normed_all, g_qkv, TN).astype(BF16)
        qkv_grad = pick_half(qkv_grad, core).astype(F32) + swap_cores(pick_half(qkv_grad, 1 - core)).astype(F32)
        qkv_grad = lax.psum(qkv_grad.astype(BF16), "dp")
        return g_inputs, g_qkv[:, 2 * width :], (grads, qkv_grad, g_gain_a, g_gain_f)

    h_first, first_values, kept_first = forward(inputs, None, layers[0])
    h_second, unused, kept_second = forward(h_first, first_values, layers[1])
    g_second, g_first, grads_second = backward(g_top, None, layers[1], kept_second)
    g_tokens, unused, grads_first = backward(g_second.astype(BF16).astype(F32), g_first, layers[0], kept_first)

    def by_layer(low, high, wire):
        mine = jnp.where(is_low, low, high)
        theirs = swap_cores(jnp.where(is_low, high, low).astype(wire)).astype(mine.dtype)
        return in_order(mine, theirs)

    layer_out = jnp.stack(by_layer(h_first, h_second, BF16))
    input_grads = jnp.stack(by_layer(g_tokens, g_second, BF16))
    all_first = jnp.stack(in_order(first_values, swap_cores(first_values)))

    grads_low, grads_high = by_layer(grads_first[0], grads_second[0], BF16)
    qkv_low, qkv_high = by_layer(grads_first[1], grads_second[1], BF16)

    def joined(start, size):
        return jnp.concatenate([grads_low[start : start + size], grads_high[start : start + size]], axis=0).astype(F32)

    gate_grad = joined(0, hid_half).T
    up_grad = joined(hid_half, hid_half).T
    down_grad = joined(2 * hid_half, hid_half)
    out_grad = joined(3 * hid_half, out_half)
    qkv_grad = jnp.concatenate([qkv_low, qkv_high], axis=0).astype(F32)

    heads_here = width // HEAD_DIM
    first_f32 = first_values.astype(F32).reshape(seq_rows, heads_here, HEAD_DIM)
    squares = jnp.sum(first_f32 * first_f32, axis=(0, 2))
    placed = lax.dynamic_update_slice(
        jnp.zeros((micro_count, heads_here * mp), F32),
        squares[None],
        (core, lax.axis_index("mp") * heads_here),
    )
    gain_grads = jnp.stack([grads_first[2], grads_second[2], grads_first[3], grads_second[3]])
    gain_grads, value_norms = lax.psum((gain_grads, placed), ("section", "dp", "mp"))
    attn_gain_grad = lax.dynamic_slice_in_dim(gain_grads, core, 1, 0)
    ffn_gain_grad = lax.dynamic_slice_in_dim(gain_grads, 2 + core, 1, 0)
    return (
        layer_out[None],
        input_grads[None],
        all_first,
        value_norms,
        attn_gain_grad,
        qkv_grad[:, :width][None],
        qkv_grad[:, width : 2 * width][None],
        qkv_grad[:, 2 * width :][None],
        out_grad[None],
        ffn_gain_grad,
        gate_grad[None],
        up_grad[None],
        down_grad[None],
    )


def solution(mesh):
    in_specs = (
        P(None, ("dp", "mp"), None),
        P(None, "dp"),
        P(None, ("dp", "mp"), None),
        P("section", None),
        P("section", None, "mp"),
        P("section", None, "mp"),
        P("section", None, "mp"),
        P("section", "mp", None),
        P("section", None),
        P("section", None, "mp"),
        P("section", None, "mp"),
        P("section", "mp", None),
    )
    out_specs = (
        P("section", None, ("dp", "mp"), None),
        P("section", None, ("dp", "mp"), None),
        P(None, "dp", "mp"),
        P(),
        P("section", None),
        P("section", None, "mp"),
        P("section", None, "mp"),
        P("section", None, "mp"),
        P("section", "mp", None),
        P("section", None),
        P("section", None, "mp"),
        P("section", None, "mp"),
        P("section", "mp", None),
    )
    return jax.shard_map(shards, mesh=mesh, in_specs=in_specs, out_specs=out_specs, check_vma=False)
```

```python
import functools

import jax
import jax.numpy as jnp
from jax import lax
from jax.experimental import pallas as pl
from jax.experimental.pallas import tpu as pltpu
from jax.sharding import PartitionSpec as P

HEAD_DIM = 64
HALF = HEAD_DIM // 2
EPS = 1e-05
SCALE = HEAD_DIM**-0.5
F32 = jnp.float32
BF16 = jnp.bfloat16
VMEM_BYTES = 56 * 1024 * 1024

NT = (((1,), (1,)), ((), ()))
NN = (((1,), (0,)), ((), ()))
TN = (((0,), (0,)), ((), ()))


def cost(micros):
    return pl.CostEstimate(flops=int(micros * 1.15e9), transcendentals=0, bytes_accessed=1 << 20)


def mm(left, right, dims=NN):
    return lax.dot_general(left, right, dims, preferred_element_type=F32)


def swap_halves(tensor):
    width = tensor.shape[1]
    if width % 128 == 0:
        lane = lax.broadcasted_iota(jnp.int32, tensor.shape, 1)
        ahead = pltpu.roll(tensor, width - HALF, 1)
        behind = pltpu.roll(tensor, HALF, 1)
        return jnp.where(lane % HEAD_DIM < HALF, ahead, behind)
    return jnp.concatenate([tensor[:, HALF:], tensor[:, :HALF]], axis=1)


def qkv_kernel(second, group, parts, fresh, place_ref, *refs):
    piece_refs, refs = refs[:parts], refs[parts:]
    w_ref, cos_ref, sin_ref = refs[:3]
    refs = refs[3:]
    if second:
        first_ref, refs = refs[0], refs[1:]
    if not fresh:
        refs = refs[3:]
    q_ref, k_ref, v_ref = refs
    width = q_ref.shape[1]
    rows = piece_refs[0][...]
    if parts == 2:
        rows = jnp.where(pl.program_id(0) == 0, rows, piece_refs[1][...])
    acc = mm(rows, w_ref[...])
    cosine, sine = cos_ref[...], sin_ref[...]
    for at in range(0, width, group):
        part = acc[:, at : at + group]
        turned = part * cosine + swap_halves(part) * sine
        q_ref[:, at : at + group] = (turned * SCALE).astype(BF16)
        part = acc[:, width + at : width + at + group]
        turned = part * cosine + swap_halves(part) * sine
        k_ref[:, at : at + group] = turned.astype(BF16)
    value = acc[:, 2 * width :]
    if second:
        value = 0.5 * value + 0.5 * first_ref[...].astype(F32)
    v_ref[...] = value.astype(BF16)


def project_qkv(pieces, place, weight, cosine, sine, first, held):
    rows, model = cosine.shape[0], weight.shape[0]
    width = weight.shape[1] // 3
    group = min(width, 128)
    chunk = sum(piece.shape[0] for piece in pieces)
    parts = len(pieces)
    block = pieces[0].shape[0] if parts == 2 else min(512, chunk)
    steps = chunk // block
    second = first is not None
    fresh = held is None

    def at_place(i, place_ref):
        return (place_ref[0] * steps + i, 0)

    row_spec = pl.BlockSpec((block, width), at_place)
    if parts == 2:
        piece_specs = [pl.BlockSpec((block, model), lambda i, p: (0, 0))] * 2
    else:
        piece_specs = [pl.BlockSpec((block, model), lambda i, p: (i, 0))]
    in_specs = piece_specs + [
        pl.BlockSpec((model, 3 * width), lambda i, p: (0, 0)),
        pl.BlockSpec((block, group), at_place),
        pl.BlockSpec((block, group), at_place),
    ]
    args = [*pieces, weight, cosine, sine]
    if second:
        in_specs.append(row_spec)
        args.append(first)
    aliases = {}
    if not fresh:
        aliases = {1 + len(args) + i: i for i in range(3)}
        in_specs += [pl.BlockSpec(memory_space=pl.ANY)] * 3
        args += list(held)
    shape = jax.ShapeDtypeStruct((rows, width), BF16)
    return pl.pallas_call(
        functools.partial(qkv_kernel, second, group, parts, fresh),
        grid_spec=pltpu.PrefetchScalarGridSpec(
            num_scalar_prefetch=1,
            grid=(steps,),
            in_specs=in_specs,
            out_specs=[row_spec] * 3,
        ),
        out_shape=[shape] * 3,
        input_output_aliases=aliases,
        compiler_params=pltpu.CompilerParams(vmem_limit_bytes=VMEM_BYTES),
        cost_estimate=cost(4),
        name="qkv_rope",
    )(place, *args)


def head_lanes(value, head, group):
    per = group // HEAD_DIM
    if per == 1:
        return value
    lane = lax.broadcasted_iota(jnp.int32, value.shape, 1)
    return jnp.where(lane // HEAD_DIM == head % per, value, jnp.zeros_like(value))


def attend_kernel(block, group, parts, info_ref, q_ref, k_ref, v_ref, *refs):
    o_refs, refs = refs[:parts], refs[parts:]
    lse_ref, vt_ref, acc_ref, top_ref, sum_ref, all_ref = refs
    rows, width = k_ref.shape
    heads = width // HEAD_DIM
    per = group // HEAD_DIM
    chunk = rows // parts
    small = min(block, chunk)
    step = pl.program_id(0)
    seg_len = info_ref[0]
    place = info_ref[1]

    @pl.when(step == 0)
    def _():
        for at in range(0, rows, small):
            vt_ref[:, at : at + small] = v_ref[at : at + small, :].astype(F32).T.astype(BF16)

    q_heads = []
    for head in range(heads):
        at = head // per * group
        q_heads.append(head_lanes(q_ref[:, at : at + group], head, group))

    def one(col, masked):
        key_rows = pl.ds(pl.multiple_of(col * block, block), block)
        for head in range(heads):
            at = head // per * group
            own = slice(head * HEAD_DIM, (head + 1) * HEAD_DIM)
            scores = mm(k_ref[key_rows, at : at + group], q_heads[head], NT)
            if masked:
                r = lax.broadcasted_iota(jnp.int32, scores.shape, 0)
                c = lax.broadcasted_iota(jnp.int32, scores.shape, 1)
                scores = jnp.where(r <= c, scores, -1e30)
            top = jnp.max(scores, axis=0, keepdims=True)
            if not masked:
                old = top_ref[head : head + 1, :]
                top = jnp.maximum(top, old)
            probs = jnp.exp(scores - top)
            count = jnp.sum(probs, axis=0, keepdims=True)
            total = mm(vt_ref[own, key_rows], probs.astype(BF16))
            if not masked:
                shrink = jnp.exp(old - top)
                count = count + sum_ref[head : head + 1, :] * shrink
                total = total + acc_ref[own, :] * shrink
            acc_ref[own, :] = total
            top_ref[head : head + 1, :] = top
            sum_ref[head : head + 1, :] = count

    one(step, True)

    @pl.loop(step * block // seg_len * (seg_len // block), step)
    def _(col):
        one(col, False)

    lse_ref[...] = top_ref[:heads, :] + jnp.log(sum_ref[:heads, :])
    for head in range(heads):
        own = slice(head * HEAD_DIM, (head + 1) * HEAD_DIM)
        acc_ref[own, :] = acc_ref[own, :] * (1.0 / sum_ref[head : head + 1, :])
    for at in range(0, block, small):
        turned = acc_ref[:, at : at + small].T.astype(BF16)
        if parts == 1:
            target = step * block + at
        else:
            target = jnp.bitwise_xor(step * (block // chunk) + at // chunk, place) * chunk + at % chunk
        all_ref[pl.ds(pl.multiple_of(target, small), small), :] = turned

    @pl.when(step == pl.num_programs(0) - 1)
    def _():
        for part in range(parts):
            o_refs[part][...] = all_ref[part * chunk : (part + 1) * chunk, :]


def attend(queries, keys, values, info, parts):
    rows, width = queries.shape
    group = min(width, 128)
    heads = width // HEAD_DIM
    block = rows // 2
    chunk = rows // parts
    whole = pl.BlockSpec((rows, width), lambda i, n: (0, 0))
    results = pl.pallas_call(
        functools.partial(attend_kernel, block, group, parts),
        grid_spec=pltpu.PrefetchScalarGridSpec(
            num_scalar_prefetch=1,
            grid=(rows // block,),
            in_specs=[pl.BlockSpec((block, width), lambda i, n: (i, 0)), whole, whole],
            out_specs=[pl.BlockSpec((chunk, width), lambda i, n: (0, 0))] * parts
            + [pl.BlockSpec((heads, block), lambda i, n: (0, i))],
            scratch_shapes=[
                pltpu.VMEM((width, rows), BF16),
                pltpu.VMEM((width, block), F32),
                pltpu.VMEM((8, block), F32),
                pltpu.VMEM((8, block), F32),
                pltpu.VMEM((rows, width), BF16),
            ],
        ),
        out_shape=[jax.ShapeDtypeStruct((chunk, width), BF16)] * parts
        + [jax.ShapeDtypeStruct((heads, rows), F32)],
        compiler_params=pltpu.CompilerParams(vmem_limit_bytes=VMEM_BYTES),
        cost_estimate=cost(18),
        name="attend",
    )(info, queries, keys, values)
    return results[:parts], results[parts]


def attend_back_kernel(second, block, strip, group, parts, info_ref, q_ref, k_ref, v_ref, lse_ref, cos_ref, sin_ref, *refs):
    o_refs, refs = refs[:parts], refs[parts:]
    do_refs, refs = refs[:parts], refs[parts:]
    if not second:
        first_refs, refs = refs[:parts], refs[parts:]
    out_refs, refs = refs[:parts], refs[parts:]
    do_ref, all_ref, dq_ref, dk_ref, dv_ref, delta_ref = refs
    rows, width = q_ref.shape
    heads = width // HEAD_DIM
    per = group // HEAD_DIM
    chunk = rows // parts
    small = min(block, chunk)
    step = pl.program_id(0)
    steps = rows // block
    seg_len = info_ref[0]
    place = info_ref[1]

    @pl.when(step == 0)
    def _():
        dq_ref[...] = jnp.zeros_like(dq_ref)
        head = lax.broadcasted_iota(jnp.int32, (8, width), 0)
        lane = lax.broadcasted_iota(jnp.int32, (8, width), 1)
        pick = jnp.where(lane // HEAD_DIM == head, 1.0, 0.0).astype(F32)
        for part in range(parts):
            for at in range(0, chunk, small):
                grads = do_refs[part][at : at + small, :]
                prod = grads.astype(F32) * o_refs[part][at : at + small, :].astype(F32)
                delta = lax.dot_general(
                    pick, prod, NT, precision=lax.Precision.HIGHEST, preferred_element_type=F32
                )
                if parts == 1:
                    target = at
                else:
                    target = jnp.bitwise_xor(part, place) * chunk + at
                target = pl.ds(pl.multiple_of(target, small), small)
                do_ref[target, :] = grads
                delta_ref[:, target] = delta
            if not second:
                all_ref[part * chunk : (part + 1) * chunk, 2 * width :] = first_refs[part][...]

    dk_ref[...] = jnp.zeros_like(dk_ref)
    dv_ref[...] = jnp.zeros_like(dv_ref)
    base = step * block

    def one(key_off, key_size, query_start, query_size, masked):
        key_rows = pl.ds(pl.multiple_of(base + key_off, strip), key_size)
        query_rows = pl.ds(pl.multiple_of(query_start, strip), query_size)
        for pair in range(heads // per):
            at = pair * group
            keys = k_ref[key_rows, at : at + group]
            values = v_ref[key_rows, at : at + group]
            queries = q_ref[query_rows, at : at + group]
            grads = do_ref[query_rows, at : at + group]
            dq = dk = dv = None
            for sub in range(per):
                head = pair * per + sub
                q_one = head_lanes(queries, head, group)
                do_one = head_lanes(grads, head, group)
                scores = mm(keys, q_one, NT)
                if masked:
                    r = lax.broadcasted_iota(jnp.int32, scores.shape, 0)
                    c = lax.broadcasted_iota(jnp.int32, scores.shape, 1)
                    scores = jnp.where(r <= c, scores, -1e30)
                probs = jnp.exp(scores - lse_ref[head : head + 1, query_rows])
                g_probs = mm(values, do_one, NT)
                g_scores = (probs * (g_probs - delta_ref[head : head + 1, query_rows])).astype(BF16)
                dv_one = mm(probs.astype(BF16), do_one)
                dk_one = mm(g_scores, q_one)
                dq_one = mm(g_scores, head_lanes(keys, head, group), TN)
                dq = dq_one if dq is None else dq + dq_one
                dk = dk_one if dk is None else dk + dk_one
                dv = dv_one if dv is None else dv + dv_one
            dq_ref[query_rows, at : at + group] += dq
            dk_ref[key_off : key_off + key_size, at : at + group] += dk
            dv_ref[key_off : key_off + key_size, at : at + group] += dv

    for off in range(0, block, strip):
        one(off, strip, base + off, block - off, True)

    per_seg = seg_len // block

    @pl.loop(step + 1, (step // per_seg + 1) * per_seg)
    def _(row):
        one(0, block, row * block, block, False)

    def turn_back(value, at_rows):
        return value * cos_ref[at_rows, :] - swap_halves(value) * sin_ref[at_rows, :]

    for off in range(0, block, small):
        here = pl.ds(pl.multiple_of(base + off, small), small)
        if parts == 1:
            target = base + off
        else:
            target = jnp.bitwise_xor(step * (block // chunk) + off // chunk, place) * chunk + off % chunk
        target = pl.ds(pl.multiple_of(target, small), small)
        for at in range(0, width, group):
            g_query = turn_back(dq_ref[here, at : at + group] * SCALE, here)
            g_key = turn_back(dk_ref[off : off + small, at : at + group], here)
            all_ref[target, at : at + group] = g_query.astype(BF16)
            all_ref[target, width + at : width + at + group] = g_key.astype(BF16)
        g_value = dv_ref[off : off + small, :]
        if second:
            g_value = 0.5 * g_value
        else:
            g_value = g_value + all_ref[target, 2 * width :].astype(F32)
        all_ref[target, 2 * width :] = g_value.astype(BF16)

    @pl.when(step == steps - 1)
    def _():
        for part in range(parts):
            out_refs[part][...] = all_ref[part * chunk : (part + 1) * chunk, :]


def attend_back(queries, keys, values, lse, cosine, sine, attended, grads, g_first, info):
    rows, width = queries.shape
    parts = len(attended)
    group = min(width, 128)
    heads = width // HEAD_DIM
    block = rows // 2
    chunk = rows // parts
    second = g_first is None
    whole = pl.BlockSpec((rows, width), lambda i, n: (0, 0))
    table = pl.BlockSpec((rows, group), lambda i, n: (0, 0))
    piece = pl.BlockSpec((chunk, width), lambda i, n: (0, 0))
    in_specs = [whole] * 3 + [pl.BlockSpec((heads, rows), lambda i, n: (0, 0)), table, table] + [piece] * (2 * parts)
    args = [queries, keys, values, lse, cosine, sine, *attended, *grads]
    if not second:
        values_at = 2 if width % 128 == 0 else 0
        if values_at == 0:
            g_first = [part[:, 2 * width :] for part in g_first]
        in_specs += [pl.BlockSpec((chunk, width), lambda i, n: (0, values_at))] * parts
        args += list(g_first)
    return pl.pallas_call(
        functools.partial(attend_back_kernel, second, block, min(256, block), group, parts),
        grid_spec=pltpu.PrefetchScalarGridSpec(
            num_scalar_prefetch=1,
            grid=(rows // block,),
            in_specs=in_specs,
            out_specs=[pl.BlockSpec((chunk, 3 * width), lambda i, n: (0, 0))] * parts,
            scratch_shapes=[
                pltpu.VMEM((rows, width), BF16),
                pltpu.VMEM((rows, 3 * width), BF16),
                pltpu.VMEM((rows, width), F32),
                pltpu.VMEM((block, width), F32),
                pltpu.VMEM((block, width), F32),
                pltpu.VMEM((8, rows), F32),
            ],
        ),
        out_shape=[jax.ShapeDtypeStruct((chunk, 3 * width), BF16)] * parts,
        compiler_params=pltpu.CompilerParams(vmem_limit_bytes=VMEM_BYTES),
        cost_estimate=cost(36),
        name="attend_back",
    )(info, *args)


def out_kernel(info_ref, own_ref, other_ref, state_ref, gain_ref, *refs):
    att_refs = refs[:-3]
    middle_ref, normed_ref, full_ref = refs[-3:]
    mp, out_half, model = own_ref.shape
    low_core = info_ref[2] == 0
    square = mp == 4
    for at in range(mp):
        source = jnp.bitwise_xor(at, info_ref[1]) if square else at
        own, other = own_ref[source], other_ref[source]
        base = at * 2 * out_half
        full_ref[base : base + out_half, :] = jnp.where(low_core, own, other)
        full_ref[base + out_half : base + 2 * out_half, :] = jnp.where(low_core, other, own)
    total = state_ref[...].astype(F32)
    size = mp * 2 * out_half // len(att_refs)
    for part, att_ref in enumerate(att_refs):
        total = total + mm(att_ref[...], full_ref[part * size : (part + 1) * size, :])
    middle_ref[...] = total
    normed_ref[...] = normalize(total, gain_ref[...]).astype(BF16)


def out_project(attended, own, other, state, gain, info):
    rows, model = state.shape
    mp, out_half = own.shape[:2]
    whole = pl.BlockSpec((rows, model), lambda i, n: (0, 0))
    share = pl.BlockSpec(own.shape, lambda i, n: (0, 0, 0))
    full = (mp * 2 * out_half, model)
    return pl.pallas_call(
        out_kernel,
        grid_spec=pltpu.PrefetchScalarGridSpec(
            num_scalar_prefetch=1,
            grid=(1,),
            in_specs=[share, share, whole, pl.BlockSpec((1, model), lambda i, n: (0, 0))]
            + [pl.BlockSpec(part.shape, lambda i, n: (0, 0)) for part in attended],
            out_specs=[whole, whole, pl.BlockSpec(full, lambda i, n: (0, 0))],
        ),
        out_shape=[
            jax.ShapeDtypeStruct((rows, model), F32),
            jax.ShapeDtypeStruct((rows, model), BF16),
            jax.ShapeDtypeStruct(full, BF16),
        ],
        compiler_params=pltpu.CompilerParams(vmem_limit_bytes=VMEM_BYTES),
        cost_estimate=cost(5),
        name="out_project",
    )(info, own, other, state, gain.reshape(1, model), *attended)


def weight_copies(pieces_ref, wide_ref, sems):
    count, hidden, model = wide_ref.shape
    mp = pieces_ref.shape[0]
    size = hidden // mp
    groups = []
    for at in range(count):
        copies = []
        for part in range(mp):
            copies.append(
                pltpu.make_async_copy(
                    pieces_ref.at[part, pl.ds(at * size, size), :],
                    wide_ref.at[at, pl.ds(part * size, size), :],
                    sems.at[at, part],
                )
            )
        groups.append(copies)
    return groups


def ffn_kernel(x_ref, base_ref, pieces_ref, out_ref, silu_ref, slope_ref, act_ref, wide_ref, sems):
    groups = weight_copies(pieces_ref, wide_ref, sems)
    for copies in groups:
        for copy in copies:
            copy.start()
    for copy in groups[0]:
        copy.wait()
    gate = mm(x_ref[...], wide_ref[0], NT)
    for copy in groups[1]:
        copy.wait()
    up = mm(x_ref[...], wide_ref[1], NT)
    sig = 0.5 + 0.5 * jnp.tanh(0.5 * gate)
    silu = gate * sig
    act = (silu * up).astype(BF16)
    silu_ref[...] = silu.astype(BF16)
    slope_ref[...] = (up * (sig + silu * (1.0 - sig))).astype(BF16)
    act_ref[...] = act
    for copy in groups[2]:
        copy.wait()
    out_ref[...] = base_ref[...] + mm(act, wide_ref[2])


def ffn_forward(normed, base, pieces, hidden):
    rows, model = normed.shape
    mp = pieces.shape[0]
    whole = pl.BlockSpec((rows, model), lambda j: (0, 0))
    inner = pl.BlockSpec((rows, hidden), lambda j: (0, 0))
    shape = jax.ShapeDtypeStruct((rows, hidden), BF16)
    return pl.pallas_call(
        ffn_kernel,
        grid=(1,),
        in_specs=[whole, whole, pl.BlockSpec(memory_space=pl.ANY)],
        out_specs=[whole, inner, inner, inner],
        out_shape=[jax.ShapeDtypeStruct((rows, model), F32), shape, shape, shape],
        scratch_shapes=[pltpu.VMEM((3, hidden, model), BF16), pltpu.SemaphoreType.DMA((3, mp))],
        compiler_params=pltpu.CompilerParams(vmem_limit_bytes=VMEM_BYTES),
        cost_estimate=cost(9),
        name="ffn",
    )(normed, base, pieces)


def ffn_back_kernel(more, *refs):
    if more:
        base_ref, refs = refs[0], refs[1:]
    g_ref, silu_ref, slope_ref, pieces_ref, out_ref, g_gate_ref, g_up_ref, wide_ref, sems = refs
    groups = weight_copies(pieces_ref, wide_ref, sems)
    for at in (2, 0, 1):
        for copy in groups[at]:
            copy.start()
    for copy in groups[2]:
        copy.wait()
    g_act = mm(g_ref[...], wide_ref[2], NT)
    g_up = (g_act * silu_ref[...].astype(F32)).astype(BF16)
    g_gate = (g_act * slope_ref[...].astype(F32)).astype(BF16)
    g_gate_ref[...] = g_gate
    g_up_ref[...] = g_up
    for copy in groups[0]:
        copy.wait()
    total = mm(g_gate, wide_ref[0])
    for copy in groups[1]:
        copy.wait()
    total = total + mm(g_up, wide_ref[1])
    out_ref[...] = base_ref[...] + total if more else total


def ffn_backward(g_branch, base, silu, slope, pieces):
    rows, model = g_branch.shape
    hidden = silu.shape[1]
    mp = pieces.shape[0]
    whole = pl.BlockSpec((rows, model), lambda j: (0, 0))
    inner = pl.BlockSpec((rows, hidden), lambda j: (0, 0))
    shape = jax.ShapeDtypeStruct((rows, hidden), BF16)
    more = base is not None
    args = [g_branch, silu, slope, pieces]
    in_specs = [whole, inner, inner, pl.BlockSpec(memory_space=pl.ANY)]
    if more:
        args, in_specs = [base] + args, [whole] + in_specs
    return pl.pallas_call(
        functools.partial(ffn_back_kernel, more),
        grid=(1,),
        in_specs=in_specs,
        out_specs=[whole, inner, inner],
        out_shape=[jax.ShapeDtypeStruct((rows, model), F32), shape, shape],
        scratch_shapes=[pltpu.VMEM((3, hidden, model), BF16), pltpu.SemaphoreType.DMA((3, mp))],
        compiler_params=pltpu.CompilerParams(vmem_limit_bytes=VMEM_BYTES),
        cost_estimate=cost(9),
        name="ffn_back",
    )(*args)


def pack_grads_kernel(size, *refs):
    gate, got_gate, up, got_up, act, got_act, x_ref, got_x, g_ref, got_g, out_grad, pack_ref = refs
    count = pack_ref.shape[0]
    jobs = ((gate, x_ref, got_gate, got_x), (up, x_ref, got_up, got_x), (act, g_ref, got_act, got_g))
    for at, (left, right, left_two, right_two) in enumerate(jobs):
        acc = mm(left[...], right[...], TN) + mm(left_two[...], right_two[...], TN)
        for part in range(count):
            pack_ref[part, at * size : (at + 1) * size, :] = acc[part * size : (part + 1) * size].astype(BF16)
    for part in range(count):
        pack_ref[part, 3 * size :, :] = out_grad[part]


def pack_grads(inner, got_inner, normed, got_normed, g_branch, got_branch, out_grad):
    rows, model = normed.shape
    hidden = inner[0].shape[1]
    mp, out_half = out_grad.shape[:2]
    size = hidden // mp
    block = min(512, model)
    left = pl.BlockSpec((rows, hidden), lambda j: (0, 0))
    right = pl.BlockSpec((rows, block), lambda j: (0, j))
    pack_rows = 3 * size + out_half
    args = []
    for own, got in zip(inner, got_inner):
        args += [own, got]
    return pl.pallas_call(
        functools.partial(pack_grads_kernel, size),
        grid=(model // block,),
        in_specs=[left] * 6 + [right] * 4 + [pl.BlockSpec((mp, out_half, block), lambda j: (0, 0, j))],
        out_specs=pl.BlockSpec((mp, pack_rows, block), lambda j: (0, 0, j)),
        out_shape=jax.ShapeDtypeStruct((mp, pack_rows, model), BF16),
        compiler_params=pltpu.CompilerParams(vmem_limit_bytes=VMEM_BYTES),
        cost_estimate=cost(15),
        name="pack_grads",
    )(*args, normed, got_normed, g_branch, got_branch, out_grad)


def place_kernel(which_ref, first_ref, second_ref, out_ref):
    @pl.when(pl.program_id(0) == 0)
    def _():
        out_ref[...] = first_ref[...]

    @pl.when(pl.program_id(0) == 1)
    def _():
        out_ref[...] = second_ref[...]


def place_rows(first, second, which):
    rows, model = first.shape
    if rows % 16:
        ordered = jnp.where(which == 0, first, second), jnp.where(which == 0, second, first)
        return jnp.concatenate(ordered, axis=0)
    whole = pl.BlockSpec((rows, model), lambda i, w: (0, 0))
    return pl.pallas_call(
        place_kernel,
        grid_spec=pltpu.PrefetchScalarGridSpec(
            num_scalar_prefetch=1,
            grid=(2,),
            in_specs=[whole, whole],
            out_specs=pl.BlockSpec((rows, model), lambda i, w: (jnp.bitwise_xor(w[0], i), 0)),
        ),
        out_shape=jax.ShapeDtypeStruct((2 * rows, model), first.dtype),
        compiler_params=pltpu.CompilerParams(vmem_limit_bytes=VMEM_BYTES),
        cost_estimate=cost(2),
        name="place_rows",
    )(which.astype(jnp.int32).reshape(1), first, second)


def qkv_grad_kernel(count, *refs):
    out_ref = refs[-1]
    acc = None
    at = 0
    whole = count
    grads = refs[whole:-1]
    part = 0
    for i in range(count):
        size = refs[i].shape[0]
        chunk = grads[part].shape[0]
        product = mm(refs[i][...], grads[part][at : at + size, :], TN)
        acc = product if acc is None else acc + product
        at += size
        if at == chunk:
            at, part = 0, part + 1
    out_ref[...] = acc.astype(BF16)


def qkv_grad_sum(pieces, grads):
    model = pieces[0].shape[1]
    width = grads[0].shape[1]
    block = min(512, model)
    return pl.pallas_call(
        functools.partial(qkv_grad_kernel, len(pieces)),
        grid=(model // block,),
        in_specs=[pl.BlockSpec((piece.shape[0], block), lambda i: (0, i)) for piece in pieces]
        + [pl.BlockSpec(part.shape, lambda i: (0, 0)) for part in grads],
        out_specs=pl.BlockSpec((block, width), lambda i: (i, 0)),
        out_shape=jax.ShapeDtypeStruct((model, width), BF16),
        compiler_params=pltpu.CompilerParams(vmem_limit_bytes=VMEM_BYTES),
        cost_estimate=cost(7),
        name="qkv_grad",
    )(*pieces, *grads)


def normalize(rows_in, gain):
    scale = lax.rsqrt(jnp.mean(rows_in * rows_in, axis=-1, keepdims=True) + EPS)
    return rows_in * scale * gain


def normalize_back(rows_in, gain, grad):
    scale = lax.rsqrt(jnp.mean(rows_in * rows_in, axis=-1, keepdims=True) + EPS)
    gained = grad * gain
    inner = jnp.mean(gained * rows_in, axis=-1, keepdims=True)
    g_rows = scale * (gained - rows_in * (scale * scale * inner))
    return g_rows, jnp.sum(grad * (rows_in * scale), axis=0)


def rotary_tables(rows, seg_len, lanes):
    positions = (jnp.arange(rows, dtype=jnp.int32) % seg_len).astype(F32)
    inverse_freq = 10000.0 ** (-(jnp.arange(HALF, dtype=F32) * 2.0 / HEAD_DIM))
    angles = positions[:, None] * inverse_freq[None, :]
    cosine, sine = jnp.cos(angles), jnp.sin(angles)
    cosine = jnp.concatenate([cosine, cosine] * (lanes // HEAD_DIM), axis=1)
    sine = jnp.concatenate([-sine, sine] * (lanes // HEAD_DIM), axis=1)
    return cosine, sine


def swap_cores(value):
    return lax.ppermute(value, "section", [(0, 1), (1, 0)])


def across(value, axis, bits):
    return lax.ppermute(value, axis, [(i, i ^ bits) for i in range(lax.axis_size(axis))])


def is_square():
    return lax.axis_size("mp") == 4


def spread_rows(value):
    if not is_square():
        return [[lax.all_gather(value, "mp", axis=0, tiled=True)]]
    half = value.shape[0] // 2
    from_x, from_y = across(value, "mp", 1), across(value, "mp", 2)
    far_low, far_high = across(from_y[:half], "mp", 1), across(from_x[half:], "mp", 2)
    return [[value], [from_x], [from_y], [far_low, far_high]]


def sum_rows_to_owner(parts):
    if not is_square():
        total = lax.psum_scatter(jnp.concatenate(parts, axis=0), "mp", scatter_dimension=0, tiled=True)
        return total.astype(F32)
    half = parts[0].shape[0] // 2
    own, to_x, to_y, to_far = parts
    far_low = across(to_far[:half], "mp", 1)
    far_high = across(to_far[half:], "mp", 2)
    x_low = across(to_x[:half], "mp", 1)
    y_high = across(to_y[half:], "mp", 2)
    passed_x = (to_x[half:].astype(F32) + far_high.astype(F32)).astype(BF16)
    passed_y = (to_y[:half].astype(F32) + far_low.astype(F32)).astype(BF16)
    x_high = across(passed_x, "mp", 1)
    y_low = across(passed_y, "mp", 2)
    own = own.astype(F32)
    low = own[:half] + x_low.astype(F32) + y_low.astype(F32)
    high = own[half:] + x_high.astype(F32) + y_high.astype(F32)
    return jnp.concatenate([low, high], axis=0)


def group_steps():
    return 4 if lax.axis_size("dp") == 4 else 1


def sum_groups_step(step, state):
    if lax.axis_size("dp") != 4:
        return (lax.psum(state[0], "dp"), None)
    index = lax.axis_index("dp")
    low, high = index % 2, index // 2
    kept, got = state
    bits, which = ((1, low), (2, high), (2, high), (1, low))[step]
    if step < 2:
        whole = kept if got is None else (kept.astype(F32) + got.astype(F32)).astype(BF16)
        size = whole.shape[0] // 2
        kept = lax.dynamic_slice_in_dim(whole, which * size, size, 0)
        sent = lax.dynamic_slice_in_dim(whole, (1 - which) * size, size, 0)
        return kept, across(sent, "dp", bits)
    if step == 2:
        whole = (kept.astype(F32) + got.astype(F32)).astype(BF16)
    else:
        whole = place_rows(kept, got, high)
    return whole, across(whole, "dp", bits)


def sum_groups_end(state):
    if lax.axis_size("dp") != 4:
        return state[0]
    return place_rows(state[0], state[1], lax.axis_index("dp") % 2)


def sum_groups(value, state=None, start=0):
    if state is None:
        state = (value, None)
    for step in range(start, group_steps()):
        state = sum_groups_step(step, state)
    return sum_groups_end(state)


class Hook:
    def __init__(self, value):
        self.state = (value, None)
        self.step = 0

    def tie(self, value):
        value, self.state = lax.optimization_barrier((value, self.state))
        if self.step < group_steps():
            self.state = sum_groups_step(self.step, self.state)
            self.step += 1
        return value

    def end(self):
        return sum_groups(None, self.state, self.step)


def by_distance(blocks, place):
    if not is_square():
        return blocks
    blocks = jnp.where(place % 2 == 0, blocks, jnp.stack([blocks[i] for i in (1, 0, 3, 2)]))
    return jnp.where(place < 2, blocks, jnp.stack([blocks[i] for i in (2, 3, 0, 1)]))


def sum_all(value):
    if not is_square() or lax.axis_size("dp") != 4:
        return lax.psum(value, ("section", "dp", "mp"))
    value = value + across(value, "section", 1)
    for axis in ("mp", "dp"):
        for bits in (1, 2):
            value = value + across(value, axis, bits)
    return value


def pick_half(value, which, axis=0):
    size = value.shape[axis] // 2
    return lax.dynamic_slice_in_dim(value, which * size, size, axis)


def shards(
    tokens,
    layout,
    cotangent,
    attn_gain,
    query_weight,
    key_weight,
    value_weight,
    out_weight,
    ffn_gain,
    gate_weight,
    up_weight,
    down_weight,
):
    core = lax.axis_index("section")
    is_low = core == 0
    micro_count, tok_rows, model = tokens.shape
    mp = lax.axis_size("mp")
    place = lax.axis_index("mp").astype(jnp.int32)
    square = is_square()
    parts = mp if square else 1
    seq_rows = tok_rows * mp
    width = query_weight.shape[2]
    hidden = gate_weight.shape[2]
    hid_half = hidden // 2
    out_half = width // 2
    group = min(width, 128)

    def in_order(own, other):
        return jnp.where(is_low, own, other), jnp.where(is_low, other, own)

    inputs = lax.dynamic_index_in_dim(tokens, core, 0, keepdims=False)
    g_top = lax.dynamic_index_in_dim(cotangent, core, 0, keepdims=False)
    pack_layout = lax.dynamic_index_in_dim(layout[:, 0], core, 0, keepdims=False)
    seg_len = (seq_rows // pack_layout).astype(jnp.int32)
    info = jnp.stack([seg_len, place, core.astype(jnp.int32)])
    cosine, sine = rotary_tables(seq_rows, seg_len, group)

    own_qkv = jnp.concatenate([query_weight[0], key_weight[0], value_weight[0]], axis=1)
    qkv_weights = in_order(own_qkv, swap_cores(own_qkv))
    gains = jnp.concatenate([attn_gain, ffn_gain], axis=0)
    layer_gains = in_order(gains, swap_cores(gains))

    halves = jnp.concatenate(
        [
            gate_weight[0].T.reshape(2, hid_half, model),
            up_weight[0].T.reshape(2, hid_half, model),
            down_weight[0].reshape(2, hid_half, model),
            out_weight[0].reshape(2, out_half, model),
        ],
        axis=1,
    )
    kept = lax.dynamic_index_in_dim(halves, core, 0, keepdims=False)
    sent = lax.dynamic_index_in_dim(halves, 1 - core, 0, keepdims=False)
    packs = in_order(kept, swap_cores(sent))
    pack_rows = packs[0].shape[0]

    all_pieces = [lax.all_gather(pack, "mp", axis=0, tiled=False) for pack in packs]

    hid_all = mp * hid_half

    def whole_rows(pieces):
        if hid_half % 16 == 0:
            return pieces
        starts = [i * hid_half for i in range(3)]
        parts = [pieces[:, at : at + hid_half].reshape(hid_all, model) for at in starts]
        return jnp.concatenate(parts, axis=0)[None]

    def to_owners(attended):
        if not square:
            blocks = attended[0].reshape(mp, tok_rows, width)
            moved = lax.all_to_all(blocks, "mp", 0, 0)
            return [jnp.transpose(moved, (1, 0, 2)).reshape(tok_rows, mp * width)]
        moved = {i: across(attended[i], "mp", i) for i in (3, 1, 2)}
        return [attended[0], moved[1], moved[2], moved[3]]

    def to_heads(value):
        if not square:
            blocks = jnp.transpose(value.reshape(tok_rows, mp, width), (1, 0, 2))
            return [lax.all_to_all(blocks, "mp", 0, 0).reshape(seq_rows, width)]
        blocks = [value[:, i * width : (i + 1) * width] for i in range(mp)]
        moved = {i: across(blocks[i], "mp", i) for i in (3, 1, 2)}
        return [blocks[0], moved[1], moved[2], moved[3]]

    def forward(rows_low, first, weights):
        gain_a, gain_f, qkv_w, pieces_w = weights
        state = rows_low.astype(F32)
        normed = normalize(state, gain_a).astype(BF16)
        pieces = spread_rows(normed)
        held = None
        for index, piece in enumerate(pieces):
            spot = jnp.bitwise_xor(place, index) if square else jnp.int32(0)
            held = project_qkv(piece, spot.reshape(1), qkv_w, cosine, sine, first, held)
        queries, keys, values = held
        attended, lse = attend(queries, keys, values, info, parts)
        attended, pieces_w = lax.optimization_barrier((attended, pieces_w))
        out_own = pieces_w[:, 3 * hid_half :]
        out_other = swap_cores(out_own)
        own, other = whole_rows(pieces_w), whole_rows(swap_cores(pieces_w))
        att_rows = to_owners(attended)
        middle, normed_ffn, out_full = out_project(att_rows, out_own, out_other, rows_low, gain_f, info)
        result = middle
        inner = []
        for share in (own, other):
            result, silu, slope, activated = ffn_forward(normed_ffn, result, share, hid_all)
            inner.append((silu, slope, activated))
        flat = [part for piece in pieces for part in piece]
        kept_items = (state, flat, queries, keys, values, attended, lse, att_rows, middle, normed_ffn, inner)
        kept_items += (own, other, out_full)
        return result.astype(BF16), values, kept_items

    def backward(g_result, g_first, weights, kept_items, hook=None):
        tie = hook.tie if hook is not None else lambda value: value

        gain_a, gain_f, qkv_w, unused = weights
        state, pieces, queries, keys, values, attended, lse, att_rows, middle, normed_ffn, inner = kept_items[:11]
        own, other, out_full = kept_items[11:]
        g_branch = g_result.astype(BF16)
        got_normed, got_branch, got_act = swap_cores(normed_ffn), swap_cores(g_branch), swap_cores(inner[1][2])
        g_normed = None
        g_inner = []
        for (silu, slope, activated), share in zip(inner, (own, other)):
            g_normed, g_gate, g_up = ffn_backward(g_branch, g_normed, silu, slope, share)
            g_inner.append((g_gate, g_up, activated))
        got_gate, got_up = swap_cores(g_inner[1][0]), swap_cores(g_inner[1][1])
        g_normed = tie(g_normed)
        g_norm, g_gain_f = normalize_back(middle, gain_f, g_normed)
        g_middle = g_result + g_norm
        g_mid_low = g_middle.astype(BF16)
        g_att = to_heads(mm(g_mid_low, out_full, NT).astype(BF16))
        g_att = tie(g_att)
        g_qkv = attend_back(queries, keys, values, lse, cosine, sine, attended, g_att, g_first, info)
        g_qkv = tie(g_qkv)
        g_parts = [mm(part, qkv_w, NT).astype(BF16) for part in g_qkv]
        if not square:
            g_parts = [g_parts[0][i * tok_rows : (i + 1) * tok_rows] for i in range(mp)]
        g_norm, g_gain_a = normalize_back(state, gain_a, tie(sum_rows_to_owner(g_parts)))
        g_inputs = g_middle + g_norm

        att_whole = jnp.concatenate(att_rows, axis=1)
        out_grad = mm(att_whole, g_mid_low, TN).astype(BF16).reshape(mp, 2, out_half, model)
        out_kept = lax.dynamic_index_in_dim(out_grad, core, 1, keepdims=False)
        out_sent = lax.dynamic_index_in_dim(out_grad, 1 - core, 1, keepdims=False)
        out_grad = (out_kept.astype(F32) + swap_cores(out_sent).astype(F32)).astype(BF16)
        pack = pack_grads(
            g_inner[0],
            (got_gate, got_up, got_act),
            normed_ffn,
            got_normed,
            g_branch,
            got_branch,
            by_distance(out_grad, place),
        )
        ffn_grads = lax.psum_scatter(pack.reshape(mp * pack_rows, model), "mp", scatter_dimension=0, tiled=True)
        qkv_grad = qkv_grad_sum(pieces, g_qkv)
        qkv_grad = pick_half(qkv_grad, core).astype(F32) + swap_cores(pick_half(qkv_grad, 1 - core)).astype(F32)
        return g_inputs, g_qkv, (ffn_grads, qkv_grad, g_gain_a, g_gain_f)

    layers = [
        (layer_gains[i][0], layer_gains[i][1], qkv_weights[i], all_pieces[i]) for i in range(2)
    ]
    h_first, first_values, kept_first = forward(inputs, None, layers[0])
    h_second, unused, kept_second = forward(h_first, first_values, layers[1])
    g_second, g_qkv_second, grads_second = backward(g_top, None, layers[1], kept_second)
    hook = Hook(grads_second[0])
    g_tokens, unused, grads_first = backward(
        g_second.astype(BF16).astype(F32), g_qkv_second, layers[0], kept_first, hook
    )

    def flat_rows(value):
        return value.reshape(-1, model).astype(BF16)

    totals_second = [hook.end(), sum_groups(flat_rows(grads_second[1]))]
    cut = pack_rows // 64 * 32
    totals_first = [
        jnp.concatenate([sum_groups(grads_first[0][:cut]), sum_groups(grads_first[0][cut:])], axis=0),
        sum_groups(flat_rows(grads_first[1])),
    ]

    def by_layer(low, high, wire):
        mine = jnp.where(is_low, low, high)
        theirs = swap_cores(jnp.where(is_low, high, low).astype(wire)).astype(mine.dtype)
        return in_order(mine, theirs)

    layer_out = jnp.stack(by_layer(h_first, h_second, BF16))
    input_grads = jnp.stack(by_layer(g_tokens, g_second, BF16))
    all_first = jnp.stack(in_order(first_values, swap_cores(first_values)))

    low, high = by_layer(totals_first[0], totals_second[0], BF16)
    qkv_low, qkv_high = by_layer(totals_first[1], totals_second[1], BF16)

    def joined(start, size):
        return jnp.concatenate([low[start : start + size], high[start : start + size]], axis=0).astype(F32)

    gate_grad = joined(0, hid_half)
    up_grad = joined(hid_half, hid_half)
    down_grad = joined(2 * hid_half, hid_half)
    out_grad = joined(3 * hid_half, out_half)
    qkv_grad = jnp.concatenate([qkv_low, qkv_high], axis=0).astype(F32).reshape(model, 3 * width)

    heads_here = width // HEAD_DIM
    first_f32 = first_values.astype(F32).reshape(seq_rows, heads_here, HEAD_DIM)
    squares = jnp.sum(first_f32 * first_f32, axis=(0, 2))
    placed = lax.dynamic_update_slice(
        jnp.zeros((micro_count, heads_here * mp), F32), squares[None], (core, place * heads_here)
    )
    sums = [grads_first[2], grads_second[2], grads_first[3], grads_second[3], placed.reshape(-1)]
    sums = sum_all(jnp.concatenate(sums))
    gain_grads = sums[: 4 * model].reshape(4, model)
    value_norms = sums[4 * model :].reshape(placed.shape)
    attn_gain_grad = lax.dynamic_slice_in_dim(gain_grads, core, 1, 0)
    ffn_gain_grad = lax.dynamic_slice_in_dim(gain_grads, 2 + core, 1, 0)
    return (
        layer_out[None],
        input_grads[None],
        all_first,
        value_norms,
        attn_gain_grad,
        qkv_grad[:, :width][None],
        qkv_grad[:, width : 2 * width][None],
        qkv_grad[:, 2 * width :][None],
        out_grad[None],
        ffn_gain_grad,
        gate_grad.T[None],
        up_grad.T[None],
        down_grad[None],
    )


def solution(mesh):
    in_specs = (
        P(None, ("dp", "mp"), None),
        P(None, "dp"),
        P(None, ("dp", "mp"), None),
        P("section", None),
        P("section", None, "mp"),
        P("section", None, "mp"),
        P("section", None, "mp"),
        P("section", "mp", None),
        P("section", None),
        P("section", None, "mp"),
        P("section", None, "mp"),
        P("section", "mp", None),
    )
    out_specs = (
        P("section", None, ("dp", "mp"), None),
        P("section", None, ("dp", "mp"), None),
        P(None, "dp", "mp"),
        P(),
        P("section", None),
        P("section", None, "mp"),
        P("section", None, "mp"),
        P("section", None, "mp"),
        P("section", "mp", None),
        P("section", None),
        P("section", None, "mp"),
        P("section", None, "mp"),
        P("section", "mp", None),
    )
    return jax.shard_map(shards, mesh=mesh, in_specs=in_specs, out_specs=out_specs, check_vma=False)
```

```python
import functools

import jax
import jax.numpy as jnp
from jax import lax
from jax.experimental import pallas as pl
from jax.experimental.pallas import tpu as pltpu
from jax.sharding import PartitionSpec as P

HEAD_DIM = 64
HALF = HEAD_DIM // 2
EPS = 1e-05
SCALE = HEAD_DIM**-0.5
F32 = jnp.float32
BF16 = jnp.bfloat16
VMEM_BYTES = 56 * 1024 * 1024

NT = (((1,), (1,)), ((), ()))
NN = (((1,), (0,)), ((), ()))
TN = (((0,), (0,)), ((), ()))


def cost(micros):
    return pl.CostEstimate(flops=int(micros * 1.15e9), transcendentals=0, bytes_accessed=1 << 20)


def mm(left, right, dims=NN):
    return lax.dot_general(left, right, dims, preferred_element_type=F32)


def swap_halves(tensor):
    width = tensor.shape[1]
    if width % 128 == 0:
        lane = lax.broadcasted_iota(jnp.int32, tensor.shape, 1)
        ahead = pltpu.roll(tensor, width - HALF, 1)
        behind = pltpu.roll(tensor, HALF, 1)
        return jnp.where(lane % HEAD_DIM < HALF, ahead, behind)
    return jnp.concatenate([tensor[:, HALF:], tensor[:, :HALF]], axis=1)


def qkv_kernel(second, group, parts, fresh, place_ref, *refs):
    piece_refs, refs = refs[:parts], refs[parts:]
    w_ref, cos_ref, sin_ref = refs[:3]
    refs = refs[3:]
    if second:
        first_ref, refs = refs[0], refs[1:]
    if not fresh:
        refs = refs[3:]
    q_ref, k_ref, v_ref = refs
    width = q_ref.shape[1]
    rows = piece_refs[0][...]
    if parts == 2:
        rows = jnp.where(pl.program_id(0) == 0, rows, piece_refs[1][...])
    acc = mm(rows, w_ref[...])
    cosine, sine = cos_ref[...], sin_ref[...]
    for at in range(0, width, group):
        part = acc[:, at : at + group]
        turned = part * cosine + swap_halves(part) * sine
        q_ref[:, at : at + group] = (turned * SCALE).astype(BF16)
        part = acc[:, width + at : width + at + group]
        turned = part * cosine + swap_halves(part) * sine
        k_ref[:, at : at + group] = turned.astype(BF16)
    value = acc[:, 2 * width :]
    if second:
        value = 0.5 * value + 0.5 * first_ref[...].astype(F32)
    v_ref[...] = value.astype(BF16)


def project_qkv(pieces, place, weight, cosine, sine, first, held):
    rows, model = cosine.shape[0], weight.shape[0]
    width = weight.shape[1] // 3
    group = min(width, 128)
    chunk = sum(piece.shape[0] for piece in pieces)
    parts = len(pieces)
    block = pieces[0].shape[0] if parts == 2 else min(512, chunk)
    steps = chunk // block
    second = first is not None
    fresh = held is None

    def at_place(i, place_ref):
        return (place_ref[0] * steps + i, 0)

    row_spec = pl.BlockSpec((block, width), at_place)
    if parts == 2:
        piece_specs = [pl.BlockSpec((block, model), lambda i, p: (0, 0))] * 2
    else:
        piece_specs = [pl.BlockSpec((block, model), lambda i, p: (i, 0))]
    in_specs = piece_specs + [
        pl.BlockSpec((model, 3 * width), lambda i, p: (0, 0)),
        pl.BlockSpec((block, group), at_place),
        pl.BlockSpec((block, group), at_place),
    ]
    args = [*pieces, weight, cosine, sine]
    if second:
        in_specs.append(row_spec)
        args.append(first)
    aliases = {}
    if not fresh:
        aliases = {1 + len(args) + i: i for i in range(3)}
        in_specs += [pl.BlockSpec(memory_space=pl.ANY)] * 3
        args += list(held)
    shape = jax.ShapeDtypeStruct((rows, width), BF16)
    return pl.pallas_call(
        functools.partial(qkv_kernel, second, group, parts, fresh),
        grid_spec=pltpu.PrefetchScalarGridSpec(
            num_scalar_prefetch=1,
            grid=(steps,),
            in_specs=in_specs,
            out_specs=[row_spec] * 3,
        ),
        out_shape=[shape] * 3,
        input_output_aliases=aliases,
        compiler_params=pltpu.CompilerParams(vmem_limit_bytes=VMEM_BYTES),
        cost_estimate=cost(4),
        name="qkv_rope",
    )(place, *args)


def head_lanes(value, head, group):
    per = group // HEAD_DIM
    if per == 1:
        return value
    lane = lax.broadcasted_iota(jnp.int32, value.shape, 1)
    return jnp.where(lane // HEAD_DIM == head % per, value, jnp.zeros_like(value))


def attend_kernel(block, group, parts, info_ref, q_ref, k_ref, v_ref, *refs):
    o_refs, refs = refs[:parts], refs[parts:]
    lse_ref, vt_ref, acc_ref, top_ref, sum_ref, all_ref = refs
    rows, width = k_ref.shape
    heads = width // HEAD_DIM
    per = group // HEAD_DIM
    chunk = rows // parts
    small = min(block, chunk)
    step = pl.program_id(0)
    seg_len = info_ref[0]
    place = info_ref[1]

    @pl.when(step == 0)
    def _():
        for at in range(0, rows, small):
            vt_ref[:, at : at + small] = v_ref[at : at + small, :].astype(F32).T.astype(BF16)

    q_heads = []
    for head in range(heads):
        at = head // per * group
        q_heads.append(head_lanes(q_ref[:, at : at + group], head, group))

    def one(col, masked):
        key_rows = pl.ds(pl.multiple_of(col * block, block), block)
        for head in range(heads):
            at = head // per * group
            own = slice(head * HEAD_DIM, (head + 1) * HEAD_DIM)
            scores = mm(k_ref[key_rows, at : at + group], q_heads[head], NT)
            if masked:
                r = lax.broadcasted_iota(jnp.int32, scores.shape, 0)
                c = lax.broadcasted_iota(jnp.int32, scores.shape, 1)
                scores = jnp.where(r <= c, scores, -1e30)
            top = jnp.max(scores, axis=0, keepdims=True)
            if not masked:
                old = top_ref[head : head + 1, :]
                top = jnp.maximum(top, old)
            probs = jnp.exp(scores - top)
            count = jnp.sum(probs, axis=0, keepdims=True)
            total = mm(vt_ref[own, key_rows], probs.astype(BF16))
            if not masked:
                shrink = jnp.exp(old - top)
                count = count + sum_ref[head : head + 1, :] * shrink
                total = total + acc_ref[own, :] * shrink
            acc_ref[own, :] = total
            top_ref[head : head + 1, :] = top
            sum_ref[head : head + 1, :] = count

    one(step, True)

    @pl.loop(step * block // seg_len * (seg_len // block), step)
    def _(col):
        one(col, False)

    lse_ref[...] = top_ref[:heads, :] + jnp.log(sum_ref[:heads, :])
    for head in range(heads):
        own = slice(head * HEAD_DIM, (head + 1) * HEAD_DIM)
        acc_ref[own, :] = acc_ref[own, :] * (1.0 / sum_ref[head : head + 1, :])
    for at in range(0, block, small):
        turned = acc_ref[:, at : at + small].T.astype(BF16)
        if parts == 1:
            target = step * block + at
        else:
            target = jnp.bitwise_xor(step * (block // chunk) + at // chunk, place) * chunk + at % chunk
        all_ref[pl.ds(pl.multiple_of(target, small), small), :] = turned

    @pl.when(step == pl.num_programs(0) - 1)
    def _():
        for part in range(parts):
            o_refs[part][...] = all_ref[part * chunk : (part + 1) * chunk, :]


def attend(queries, keys, values, info, parts):
    rows, width = queries.shape
    group = min(width, 128)
    heads = width // HEAD_DIM
    block = rows // 2
    chunk = rows // parts
    whole = pl.BlockSpec((rows, width), lambda i, n: (0, 0))
    results = pl.pallas_call(
        functools.partial(attend_kernel, block, group, parts),
        grid_spec=pltpu.PrefetchScalarGridSpec(
            num_scalar_prefetch=1,
            grid=(rows // block,),
            in_specs=[pl.BlockSpec((block, width), lambda i, n: (i, 0)), whole, whole],
            out_specs=[pl.BlockSpec((chunk, width), lambda i, n: (0, 0))] * parts
            + [pl.BlockSpec((heads, block), lambda i, n: (0, i))],
            scratch_shapes=[
                pltpu.VMEM((width, rows), BF16),
                pltpu.VMEM((width, block), F32),
                pltpu.VMEM((8, block), F32),
                pltpu.VMEM((8, block), F32),
                pltpu.VMEM((rows, width), BF16),
            ],
        ),
        out_shape=[jax.ShapeDtypeStruct((chunk, width), BF16)] * parts
        + [jax.ShapeDtypeStruct((heads, rows), F32)],
        compiler_params=pltpu.CompilerParams(vmem_limit_bytes=VMEM_BYTES),
        cost_estimate=cost(18),
        name="attend",
    )(info, queries, keys, values)
    return results[:parts], results[parts]


def attend_back_kernel(second, block, strip, group, parts, info_ref, q_ref, k_ref, v_ref, lse_ref, cos_ref, sin_ref, *refs):
    o_refs, refs = refs[:parts], refs[parts:]
    do_refs, refs = refs[:parts], refs[parts:]
    if not second:
        first_refs, refs = refs[:parts], refs[parts:]
    out_refs, refs = refs[:parts], refs[parts:]
    do_ref, all_ref, dq_ref, dk_ref, dv_ref, delta_ref = refs
    rows, width = q_ref.shape
    heads = width // HEAD_DIM
    per = group // HEAD_DIM
    chunk = rows // parts
    small = min(block, chunk)
    step = pl.program_id(0)
    steps = rows // block
    seg_len = info_ref[0]
    place = info_ref[1]

    @pl.when(step == 0)
    def _():
        dq_ref[...] = jnp.zeros_like(dq_ref)
        head = lax.broadcasted_iota(jnp.int32, (8, width), 0)
        lane = lax.broadcasted_iota(jnp.int32, (8, width), 1)
        pick = jnp.where(lane // HEAD_DIM == head, 1.0, 0.0).astype(F32)
        for part in range(parts):
            for at in range(0, chunk, small):
                grads = do_refs[part][at : at + small, :]
                prod = grads.astype(F32) * o_refs[part][at : at + small, :].astype(F32)
                delta = lax.dot_general(
                    pick, prod, NT, precision=lax.Precision.HIGHEST, preferred_element_type=F32
                )
                if parts == 1:
                    target = at
                else:
                    target = jnp.bitwise_xor(part, place) * chunk + at
                target = pl.ds(pl.multiple_of(target, small), small)
                do_ref[target, :] = grads
                delta_ref[:, target] = delta
            if not second:
                all_ref[part * chunk : (part + 1) * chunk, 2 * width :] = first_refs[part][...]

    dk_ref[...] = jnp.zeros_like(dk_ref)
    dv_ref[...] = jnp.zeros_like(dv_ref)
    base = step * block

    def one(key_off, key_size, query_start, query_size, masked):
        key_rows = pl.ds(pl.multiple_of(base + key_off, strip), key_size)
        query_rows = pl.ds(pl.multiple_of(query_start, strip), query_size)
        for pair in range(heads // per):
            at = pair * group
            keys = k_ref[key_rows, at : at + group]
            values = v_ref[key_rows, at : at + group]
            queries = q_ref[query_rows, at : at + group]
            grads = do_ref[query_rows, at : at + group]
            dq = dk = dv = None
            for sub in range(per):
                head = pair * per + sub
                q_one = head_lanes(queries, head, group)
                do_one = head_lanes(grads, head, group)
                scores = mm(keys, q_one, NT)
                if masked:
                    r = lax.broadcasted_iota(jnp.int32, scores.shape, 0)
                    c = lax.broadcasted_iota(jnp.int32, scores.shape, 1)
                    scores = jnp.where(r <= c, scores, -1e30)
                probs = jnp.exp(scores - lse_ref[head : head + 1, query_rows])
                g_probs = mm(values, do_one, NT)
                g_scores = (probs * (g_probs - delta_ref[head : head + 1, query_rows])).astype(BF16)
                dv_one = mm(probs.astype(BF16), do_one)
                dk_one = mm(g_scores, q_one)
                dq_one = mm(g_scores, head_lanes(keys, head, group), TN)
                dq = dq_one if dq is None else dq + dq_one
                dk = dk_one if dk is None else dk + dk_one
                dv = dv_one if dv is None else dv + dv_one
            dq_ref[query_rows, at : at + group] += dq
            dk_ref[key_off : key_off + key_size, at : at + group] += dk
            dv_ref[key_off : key_off + key_size, at : at + group] += dv

    for off in range(0, block, strip):
        one(off, strip, base + off, block - off, True)

    per_seg = seg_len // block

    @pl.loop(step + 1, (step // per_seg + 1) * per_seg)
    def _(row):
        one(0, block, row * block, block, False)

    def turn_back(value, at_rows):
        return value * cos_ref[at_rows, :] - swap_halves(value) * sin_ref[at_rows, :]

    for off in range(0, block, small):
        here = pl.ds(pl.multiple_of(base + off, small), small)
        if parts == 1:
            target = base + off
        else:
            target = jnp.bitwise_xor(step * (block // chunk) + off // chunk, place) * chunk + off % chunk
        target = pl.ds(pl.multiple_of(target, small), small)
        for at in range(0, width, group):
            g_query = turn_back(dq_ref[here, at : at + group] * SCALE, here)
            g_key = turn_back(dk_ref[off : off + small, at : at + group], here)
            all_ref[target, at : at + group] = g_query.astype(BF16)
            all_ref[target, width + at : width + at + group] = g_key.astype(BF16)
        g_value = dv_ref[off : off + small, :]
        if second:
            g_value = 0.5 * g_value
        else:
            g_value = g_value + all_ref[target, 2 * width :].astype(F32)
        all_ref[target, 2 * width :] = g_value.astype(BF16)

    @pl.when(step == steps - 1)
    def _():
        for part in range(parts):
            out_refs[part][...] = all_ref[part * chunk : (part + 1) * chunk, :]


def attend_back(queries, keys, values, lse, cosine, sine, attended, grads, g_first, info):
    rows, width = queries.shape
    parts = len(attended)
    group = min(width, 128)
    heads = width // HEAD_DIM
    block = rows // 2
    chunk = rows // parts
    second = g_first is None
    whole = pl.BlockSpec((rows, width), lambda i, n: (0, 0))
    table = pl.BlockSpec((rows, group), lambda i, n: (0, 0))
    piece = pl.BlockSpec((chunk, width), lambda i, n: (0, 0))
    in_specs = [whole] * 3 + [pl.BlockSpec((heads, rows), lambda i, n: (0, 0)), table, table] + [piece] * (2 * parts)
    args = [queries, keys, values, lse, cosine, sine, *attended, *grads]
    if not second:
        values_at = 2 if width % 128 == 0 else 0
        if values_at == 0:
            g_first = [part[:, 2 * width :] for part in g_first]
        in_specs += [pl.BlockSpec((chunk, width), lambda i, n: (0, values_at))] * parts
        args += list(g_first)
    return pl.pallas_call(
        functools.partial(attend_back_kernel, second, block, min(256, block), group, parts),
        grid_spec=pltpu.PrefetchScalarGridSpec(
            num_scalar_prefetch=1,
            grid=(rows // block,),
            in_specs=in_specs,
            out_specs=[pl.BlockSpec((chunk, 3 * width), lambda i, n: (0, 0))] * parts,
            scratch_shapes=[
                pltpu.VMEM((rows, width), BF16),
                pltpu.VMEM((rows, 3 * width), BF16),
                pltpu.VMEM((rows, width), F32),
                pltpu.VMEM((block, width), F32),
                pltpu.VMEM((block, width), F32),
                pltpu.VMEM((8, rows), F32),
            ],
        ),
        out_shape=[jax.ShapeDtypeStruct((chunk, 3 * width), BF16)] * parts,
        compiler_params=pltpu.CompilerParams(vmem_limit_bytes=VMEM_BYTES),
        cost_estimate=cost(36),
        name="attend_back",
    )(info, *args)


def out_kernel(info_ref, own_ref, other_ref, state_ref, gain_ref, *refs):
    att_refs = refs[:-3]
    middle_ref, normed_ref, full_ref = refs[-3:]
    mp, out_half, model = own_ref.shape
    low_core = info_ref[2] == 0
    square = mp == 4
    for at in range(mp):
        source = jnp.bitwise_xor(at, info_ref[1]) if square else at
        own, other = own_ref[source], other_ref[source]
        base = at * 2 * out_half
        full_ref[base : base + out_half, :] = jnp.where(low_core, own, other)
        full_ref[base + out_half : base + 2 * out_half, :] = jnp.where(low_core, other, own)
    total = state_ref[...].astype(F32)
    size = mp * 2 * out_half // len(att_refs)
    for part, att_ref in enumerate(att_refs):
        total = total + mm(att_ref[...], full_ref[part * size : (part + 1) * size, :])
    middle_ref[...] = total
    normed_ref[...] = normalize(total, gain_ref[...]).astype(BF16)


def out_project(attended, own, other, state, gain, info):
    rows, model = state.shape
    mp, out_half = own.shape[:2]
    whole = pl.BlockSpec((rows, model), lambda i, n: (0, 0))
    share = pl.BlockSpec(own.shape, lambda i, n: (0, 0, 0))
    full = (mp * 2 * out_half, model)
    return pl.pallas_call(
        out_kernel,
        grid_spec=pltpu.PrefetchScalarGridSpec(
            num_scalar_prefetch=1,
            grid=(1,),
            in_specs=[share, share, whole, pl.BlockSpec((1, model), lambda i, n: (0, 0))]
            + [pl.BlockSpec(part.shape, lambda i, n: (0, 0)) for part in attended],
            out_specs=[whole, whole, pl.BlockSpec(full, lambda i, n: (0, 0))],
        ),
        out_shape=[
            jax.ShapeDtypeStruct((rows, model), F32),
            jax.ShapeDtypeStruct((rows, model), BF16),
            jax.ShapeDtypeStruct(full, BF16),
        ],
        compiler_params=pltpu.CompilerParams(vmem_limit_bytes=VMEM_BYTES),
        cost_estimate=cost(5),
        name="out_project",
    )(info, own, other, state, gain.reshape(1, model), *attended)


def weight_copies(pieces_ref, wide_ref, sems):
    count, hidden, model = wide_ref.shape
    mp = pieces_ref.shape[0]
    size = hidden // mp
    groups = []
    for at in range(count):
        copies = []
        for part in range(mp):
            copies.append(
                pltpu.make_async_copy(
                    pieces_ref.at[part, pl.ds(at * size, size), :],
                    wide_ref.at[at, pl.ds(part * size, size), :],
                    sems.at[at, part],
                )
            )
        groups.append(copies)
    return groups


def ffn_kernel(x_ref, base_ref, pieces_ref, out_ref, silu_ref, slope_ref, act_ref, wide_ref, sems):
    groups = weight_copies(pieces_ref, wide_ref, sems)
    for copies in groups:
        for copy in copies:
            copy.start()
    for copy in groups[0]:
        copy.wait()
    gate = mm(x_ref[...], wide_ref[0], NT)
    for copy in groups[1]:
        copy.wait()
    up = mm(x_ref[...], wide_ref[1], NT)
    sig = 0.5 + 0.5 * jnp.tanh(0.5 * gate)
    silu = gate * sig
    act = (silu * up).astype(BF16)
    silu_ref[...] = silu.astype(BF16)
    slope_ref[...] = (up * (sig + silu * (1.0 - sig))).astype(BF16)
    act_ref[...] = act
    for copy in groups[2]:
        copy.wait()
    out_ref[...] = base_ref[...] + mm(act, wide_ref[2])


def ffn_forward(normed, base, pieces, hidden):
    rows, model = normed.shape
    mp = pieces.shape[0]
    whole = pl.BlockSpec((rows, model), lambda j: (0, 0))
    inner = pl.BlockSpec((rows, hidden), lambda j: (0, 0))
    shape = jax.ShapeDtypeStruct((rows, hidden), BF16)
    return pl.pallas_call(
        ffn_kernel,
        grid=(1,),
        in_specs=[whole, whole, pl.BlockSpec(memory_space=pl.ANY)],
        out_specs=[whole, inner, inner, inner],
        out_shape=[jax.ShapeDtypeStruct((rows, model), F32), shape, shape, shape],
        scratch_shapes=[pltpu.VMEM((3, hidden, model), BF16), pltpu.SemaphoreType.DMA((3, mp))],
        compiler_params=pltpu.CompilerParams(vmem_limit_bytes=VMEM_BYTES),
        cost_estimate=cost(9),
        name="ffn",
    )(normed, base, pieces)


def ffn_back_kernel(more, *refs):
    if more:
        base_ref, refs = refs[0], refs[1:]
    g_ref, silu_ref, slope_ref, pieces_ref, out_ref, g_gate_ref, g_up_ref, wide_ref, sems = refs
    groups = weight_copies(pieces_ref, wide_ref, sems)
    for at in (2, 0, 1):
        for copy in groups[at]:
            copy.start()
    for copy in groups[2]:
        copy.wait()
    g_act = mm(g_ref[...], wide_ref[2], NT)
    g_up = (g_act * silu_ref[...].astype(F32)).astype(BF16)
    g_gate = (g_act * slope_ref[...].astype(F32)).astype(BF16)
    g_gate_ref[...] = g_gate
    g_up_ref[...] = g_up
    for copy in groups[0]:
        copy.wait()
    total = mm(g_gate, wide_ref[0])
    for copy in groups[1]:
        copy.wait()
    total = total + mm(g_up, wide_ref[1])
    out_ref[...] = base_ref[...] + total if more else total


def ffn_backward(g_branch, base, silu, slope, pieces):
    rows, model = g_branch.shape
    hidden = silu.shape[1]
    mp = pieces.shape[0]
    whole = pl.BlockSpec((rows, model), lambda j: (0, 0))
    inner = pl.BlockSpec((rows, hidden), lambda j: (0, 0))
    shape = jax.ShapeDtypeStruct((rows, hidden), BF16)
    more = base is not None
    args = [g_branch, silu, slope, pieces]
    in_specs = [whole, inner, inner, pl.BlockSpec(memory_space=pl.ANY)]
    if more:
        args, in_specs = [base] + args, [whole] + in_specs
    return pl.pallas_call(
        functools.partial(ffn_back_kernel, more),
        grid=(1,),
        in_specs=in_specs,
        out_specs=[whole, inner, inner],
        out_shape=[jax.ShapeDtypeStruct((rows, model), F32), shape, shape],
        scratch_shapes=[pltpu.VMEM((3, hidden, model), BF16), pltpu.SemaphoreType.DMA((3, mp))],
        compiler_params=pltpu.CompilerParams(vmem_limit_bytes=VMEM_BYTES),
        cost_estimate=cost(1),
        name="ffn_back",
    )(*args)


def pack_grads_kernel(size, plain, halves, info_ref, *refs):
    gate, got_gate, up, got_up, act, got_act, x_ref, got_x, g_ref, got_g, out_grad = refs[:11]
    out_refs = refs[11:]
    pack_ref = out_refs[-1]
    count = pack_ref.shape[0]
    jobs = ((gate, x_ref, got_gate, got_x), (up, x_ref, got_up, got_x), (act, g_ref, got_act, got_g))
    for at, (left, right, left_two, right_two) in enumerate(jobs):
        acc = mm(left[...], right[...], TN) + mm(left_two[...], right_two[...], TN)
        for part in range(count):
            pack_ref[part, at * size : (at + 1) * size, :] = acc[part * size : (part + 1) * size].astype(BF16)
    for part in range(count):
        pack_ref[part, 3 * size :, :] = out_grad[part]
    if plain:
        out_refs[0][...] = pack_ref[:, :plain, :]
        out_refs = out_refs[1:]
    if halves:
        cut = plain + halves

        @pl.when(info_ref[0] == 0)
        def _():
            out_refs[0][...] = pack_ref[:, plain:cut, :]
            out_refs[1][...] = pack_ref[:, cut:, :]

        @pl.when(info_ref[0] == 1)
        def _():
            out_refs[0][...] = pack_ref[:, cut:, :]
            out_refs[1][...] = pack_ref[:, plain:cut, :]


def pack_grads(inner, got_inner, normed, got_normed, g_branch, got_branch, out_grad, plain, first):
    rows, model = normed.shape
    hidden = inner[0].shape[1]
    mp, out_half = out_grad.shape[:2]
    size = hidden // mp
    block = min(512, model)
    left = pl.BlockSpec((rows, hidden), lambda j, n: (0, 0))
    right = pl.BlockSpec((rows, block), lambda j, n: (0, j))
    pack_rows = 3 * size + out_half
    args = []
    for own, got in zip(inner, got_inner):
        args += [own, got]
    halves = (pack_rows - plain) // 2
    if halves == 0:
        plain, sizes, scratch = 0, [pack_rows], []
    else:
        sizes = ([plain] if plain else []) + [halves, halves]
        scratch = [pltpu.VMEM((mp, pack_rows, block), BF16)]
    return pl.pallas_call(
        functools.partial(pack_grads_kernel, size, plain, halves),
        grid_spec=pltpu.PrefetchScalarGridSpec(
            num_scalar_prefetch=1,
            grid=(model // block,),
            in_specs=[left] * 6
            + [right] * 4
            + [pl.BlockSpec((mp, out_half, block), lambda j, n: (0, 0, j))],
            out_specs=[pl.BlockSpec((mp, part, block), lambda j, n: (0, 0, j)) for part in sizes],
            scratch_shapes=scratch,
        ),
        out_shape=[jax.ShapeDtypeStruct((mp, part, model), BF16) for part in sizes],
        compiler_params=pltpu.CompilerParams(vmem_limit_bytes=VMEM_BYTES),
        cost_estimate=cost(15),
        name="pack_grads",
    )(first.astype(jnp.int32).reshape(1), *args, normed, got_normed, g_branch, got_branch, out_grad)


def place_kernel(which_ref, first_ref, second_ref, out_ref):
    @pl.when(pl.program_id(0) == 0)
    def _():
        out_ref[...] = first_ref[...]

    @pl.when(pl.program_id(0) == 1)
    def _():
        out_ref[...] = second_ref[...]


def place_two(first, second, which, axis):
    rows, model = first.shape
    if (rows, model)[axis] % (16, 128)[axis]:
        ordered = jnp.where(which == 0, first, second), jnp.where(which == 0, second, first)
        return jnp.concatenate(ordered, axis=axis)
    whole = pl.BlockSpec((rows, model), lambda i, w: (0, 0))

    def target(i, w):
        spot = jnp.bitwise_xor(w[0], i)
        return (spot, 0) if axis == 0 else (0, spot)

    shape = (2 * rows, model) if axis == 0 else (rows, 2 * model)
    return pl.pallas_call(
        place_kernel,
        grid_spec=pltpu.PrefetchScalarGridSpec(
            num_scalar_prefetch=1,
            grid=(2,),
            in_specs=[whole, whole],
            out_specs=pl.BlockSpec((rows, model), target),
        ),
        out_shape=jax.ShapeDtypeStruct(shape, first.dtype),
        compiler_params=pltpu.CompilerParams(vmem_limit_bytes=VMEM_BYTES),
        cost_estimate=cost(2),
        name="place_two",
    )(which.astype(jnp.int32).reshape(1), first, second)


def qkv_grad_kernel(count, *refs):
    out_ref = refs[-1]
    acc = None
    at = 0
    whole = count
    grads = refs[whole:-1]
    part = 0
    for i in range(count):
        size = refs[i].shape[0]
        chunk = grads[part].shape[0]
        product = mm(refs[i][...], grads[part][at : at + size, :], TN)
        acc = product if acc is None else acc + product
        at += size
        if at == chunk:
            at, part = 0, part + 1
    out_ref[...] = acc.astype(BF16)


def qkv_grad_sum(pieces, grads):
    model = pieces[0].shape[1]
    width = grads[0].shape[1]
    block = min(512, model)
    return pl.pallas_call(
        functools.partial(qkv_grad_kernel, len(pieces)),
        grid=(model // block,),
        in_specs=[pl.BlockSpec((piece.shape[0], block), lambda i: (0, i)) for piece in pieces]
        + [pl.BlockSpec(part.shape, lambda i: (0, 0)) for part in grads],
        out_specs=pl.BlockSpec((block, width), lambda i: (i, 0)),
        out_shape=jax.ShapeDtypeStruct((model, width), BF16),
        compiler_params=pltpu.CompilerParams(vmem_limit_bytes=VMEM_BYTES),
        cost_estimate=cost(7),
        name="qkv_grad",
    )(*pieces, *grads)


def normalize(rows_in, gain):
    scale = lax.rsqrt(jnp.mean(rows_in * rows_in, axis=-1, keepdims=True) + EPS)
    return rows_in * scale * gain


def normalize_back(rows_in, gain, grad):
    scale = lax.rsqrt(jnp.mean(rows_in * rows_in, axis=-1, keepdims=True) + EPS)
    gained = grad * gain
    inner = jnp.mean(gained * rows_in, axis=-1, keepdims=True)
    g_rows = scale * (gained - rows_in * (scale * scale * inner))
    return g_rows, jnp.sum(grad * (rows_in * scale), axis=0)


def rotary_tables(rows, seg_len, lanes):
    positions = (jnp.arange(rows, dtype=jnp.int32) % seg_len).astype(F32)
    inverse_freq = 10000.0 ** (-(jnp.arange(HALF, dtype=F32) * 2.0 / HEAD_DIM))
    angles = positions[:, None] * inverse_freq[None, :]
    cosine, sine = jnp.cos(angles), jnp.sin(angles)
    cosine = jnp.concatenate([cosine, cosine] * (lanes // HEAD_DIM), axis=1)
    sine = jnp.concatenate([-sine, sine] * (lanes // HEAD_DIM), axis=1)
    return cosine, sine


def swap_cores(value):
    return lax.ppermute(value, "section", [(0, 1), (1, 0)])


def across(value, axis, bits):
    return lax.ppermute(value, axis, [(i, i ^ bits) for i in range(lax.axis_size(axis))])


def is_square():
    return lax.axis_size("mp") == 4


def spread_rows(value):
    if not is_square():
        return [[lax.all_gather(value, "mp", axis=0, tiled=True)]]
    half = value.shape[0] // 2
    from_x, from_y = across(value, "mp", 1), across(value, "mp", 2)
    far_low, far_high = across(from_y[:half], "mp", 1), across(from_x[half:], "mp", 2)
    return [[value], [from_x], [from_y], [far_low, far_high]]


def sum_rows_to_owner(parts):
    if not is_square():
        total = lax.psum_scatter(jnp.concatenate(parts, axis=0), "mp", scatter_dimension=0, tiled=True)
        return total.astype(F32)
    half = parts[0].shape[0] // 2
    own, to_x, to_y, to_far = parts
    far_low = across(to_far[:half], "mp", 1)
    far_high = across(to_far[half:], "mp", 2)
    x_low = across(to_x[:half], "mp", 1)
    y_high = across(to_y[half:], "mp", 2)
    passed_x = (to_x[half:].astype(F32) + far_high.astype(F32)).astype(BF16)
    passed_y = (to_y[:half].astype(F32) + far_low.astype(F32)).astype(BF16)
    x_high = across(passed_x, "mp", 1)
    y_low = across(passed_y, "mp", 2)
    own = own.astype(F32)
    low = own[:half] + x_low.astype(F32) + y_low.astype(F32)
    high = own[half:] + x_high.astype(F32) + y_high.astype(F32)
    return jnp.concatenate([low, high], axis=0)


def group_steps():
    return 4 if lax.axis_size("dp") == 4 else 1


def sum_groups_step(step, state):
    if lax.axis_size("dp") != 4:
        return (lax.psum(state[0], "dp"), None)
    index = lax.axis_index("dp")
    low, high = index % 2, index // 2
    kept, got = state
    bits, which = ((1, low), (2, high), (2, high), (1, low))[step]
    if step < 2:
        whole = kept if got is None else (kept.astype(F32) + got.astype(F32)).astype(BF16)
        size = whole.shape[1] // 2
        kept = lax.dynamic_slice_in_dim(whole, which * size, size, 1)
        sent = lax.dynamic_slice_in_dim(whole, (1 - which) * size, size, 1)
        return kept, across(sent, "dp", bits)
    if step == 2:
        whole = (kept.astype(F32) + got.astype(F32)).astype(BF16)
    else:
        whole = place_two(kept, got, high, 1)
    return whole, across(whole, "dp", bits)


def sum_groups_end(state):
    if lax.axis_size("dp") != 4:
        return state[0]
    return place_two(state[0], state[1], lax.axis_index("dp") % 2, 1)


def sum_groups(value, state=None, start=0):
    if state is None:
        state = (value, None)
    for step in range(start, group_steps()):
        state = sum_groups_step(step, state)
    return sum_groups_end(state)


def add_low(left, right):
    return (left.astype(F32) + right.astype(F32)).astype(BF16)


def scatter_parts(parts):
    rows = parts.reshape(-1, parts.shape[2])
    return lax.psum_scatter(rows, "mp", scatter_dimension=0, tiled=True)


class Chain:
    def __init__(self, state, steps, last):
        self.state, self.steps, self.last = state, list(steps), last

    def tie(self, value):
        if self.steps:
            value, self.state = lax.optimization_barrier((value, self.state))
            self.state = self.steps.pop(0)(self.state)
        return value

    def end(self):
        while self.steps:
            self.state = self.steps.pop(0)(self.state)
        return self.last(self.state)


def groups_chain(parts):
    steps = [lambda state: sum_groups_step(0, (state, None))]
    steps += [functools.partial(sum_groups_step, step) for step in range(1, group_steps())]
    return Chain(scatter_parts(parts), steps, sum_groups_end)


def plain_chain(value):
    steps = [functools.partial(sum_groups_step, step) for step in range(1, group_steps())]
    return Chain(sum_groups_step(0, (value, None)), steps, sum_groups_end)


def halves_chain(kept, sent):
    steps = [
        lambda state: scatter_parts(add_low(*state)),
        lambda state: (state, across(state, "dp", 2)),
        lambda state: (lambda total: (total, across(total, "dp", 1)))(add_low(*state)),
    ]
    return Chain(
        (kept, across(sent, "dp", 1)),
        steps,
        lambda state: place_two(state[0], state[1], lax.axis_index("dp") % 2, 0),
    )


def by_distance(blocks, place):
    if not is_square():
        return blocks
    blocks = jnp.where(place % 2 == 0, blocks, jnp.stack([blocks[i] for i in (1, 0, 3, 2)]))
    return jnp.where(place < 2, blocks, jnp.stack([blocks[i] for i in (2, 3, 0, 1)]))


def sum_all(value):
    if not is_square() or lax.axis_size("dp") != 4:
        return lax.psum(value, ("section", "dp", "mp"))
    value = value + across(value, "section", 1)
    for axis in ("mp", "dp"):
        for bits in (1, 2):
            value = value + across(value, axis, bits)
    return value


def pick_half(value, which, axis=0):
    size = value.shape[axis] // 2
    return lax.dynamic_slice_in_dim(value, which * size, size, axis)


def shards(
    tokens,
    layout,
    cotangent,
    attn_gain,
    query_weight,
    key_weight,
    value_weight,
    out_weight,
    ffn_gain,
    gate_weight,
    up_weight,
    down_weight,
):
    core = lax.axis_index("section")
    is_low = core == 0
    micro_count, tok_rows, model = tokens.shape
    mp = lax.axis_size("mp")
    place = lax.axis_index("mp").astype(jnp.int32)
    square = is_square()
    parts = mp if square else 1
    seq_rows = tok_rows * mp
    width = query_weight.shape[2]
    hidden = gate_weight.shape[2]
    hid_half = hidden // 2
    out_half = width // 2
    group = min(width, 128)

    def in_order(own, other):
        return jnp.where(is_low, own, other), jnp.where(is_low, other, own)

    inputs = lax.dynamic_index_in_dim(tokens, core, 0, keepdims=False)
    g_top = lax.dynamic_index_in_dim(cotangent, core, 0, keepdims=False)
    pack_layout = lax.dynamic_index_in_dim(layout[:, 0], core, 0, keepdims=False)
    seg_len = (seq_rows // pack_layout).astype(jnp.int32)
    info = jnp.stack([seg_len, place, core.astype(jnp.int32)])
    cosine, sine = rotary_tables(seq_rows, seg_len, group)

    own_qkv = jnp.concatenate([query_weight[0], key_weight[0], value_weight[0]], axis=1)
    qkv_weights = in_order(own_qkv, swap_cores(own_qkv))
    gains = jnp.concatenate([attn_gain, ffn_gain], axis=0)
    layer_gains = in_order(gains, swap_cores(gains))

    first_normed = normalize(inputs.astype(F32), layer_gains[0][0]).astype(BF16)
    first_normed, gate_weight, up_weight, down_weight, out_weight = lax.optimization_barrier(
        (first_normed, gate_weight, up_weight, down_weight, out_weight)
    )
    halves = jnp.concatenate(
        [
            gate_weight[0].T.reshape(2, hid_half, model),
            up_weight[0].T.reshape(2, hid_half, model),
            down_weight[0].reshape(2, hid_half, model),
            out_weight[0].reshape(2, out_half, model),
        ],
        axis=1,
    )
    kept = lax.dynamic_index_in_dim(halves, core, 0, keepdims=False)
    sent = lax.dynamic_index_in_dim(halves, 1 - core, 0, keepdims=False)
    packs = in_order(kept, swap_cores(sent))
    pack_rows = packs[0].shape[0]

    all_pieces = [lax.all_gather(pack, "mp", axis=0, tiled=False) for pack in packs]

    hid_all = mp * hid_half

    def whole_rows(pieces):
        if hid_half % 16 == 0:
            return pieces
        starts = [i * hid_half for i in range(3)]
        parts = [pieces[:, at : at + hid_half].reshape(hid_all, model) for at in starts]
        return jnp.concatenate(parts, axis=0)[None]

    def to_owners(attended):
        if not square:
            blocks = attended[0].reshape(mp, tok_rows, width)
            moved = lax.all_to_all(blocks, "mp", 0, 0)
            return [jnp.transpose(moved, (1, 0, 2)).reshape(tok_rows, mp * width)]
        moved = {i: across(attended[i], "mp", i) for i in (3, 1, 2)}
        return [attended[0], moved[1], moved[2], moved[3]]

    def to_heads(value):
        if not square:
            blocks = jnp.transpose(value.reshape(tok_rows, mp, width), (1, 0, 2))
            return [lax.all_to_all(blocks, "mp", 0, 0).reshape(seq_rows, width)]
        blocks = [value[:, i * width : (i + 1) * width] for i in range(mp)]
        moved = {i: across(blocks[i], "mp", i) for i in (3, 1, 2)}
        return [blocks[0], moved[1], moved[2], moved[3]]

    def forward(rows_low, first, weights, normed=None):
        gain_a, gain_f, qkv_w, pieces_w = weights
        state = rows_low.astype(F32)
        if normed is None:
            normed = normalize(state, gain_a).astype(BF16)
        pieces = spread_rows(normed)
        held = None
        for index, piece in enumerate(pieces):
            spot = jnp.bitwise_xor(place, index) if square else jnp.int32(0)
            held = project_qkv(piece, spot.reshape(1), qkv_w, cosine, sine, first, held)
        queries, keys, values = held
        attended, lse = attend(queries, keys, values, info, parts)
        attended, pieces_w = lax.optimization_barrier((attended, pieces_w))
        out_own = pieces_w[:, 3 * hid_half :]
        out_other = swap_cores(out_own)
        own, other = whole_rows(pieces_w), whole_rows(swap_cores(pieces_w))
        att_rows = to_owners(attended)
        middle, normed_ffn, out_full = out_project(att_rows, out_own, out_other, rows_low, gain_f, info)
        result = middle
        inner = []
        for share in (own, other):
            result, silu, slope, activated = ffn_forward(normed_ffn, result, share, hid_all)
            inner.append((silu, slope, activated))
        flat = [part for piece in pieces for part in piece]
        kept_items = (state, flat, queries, keys, values, attended, lse, att_rows, middle, normed_ffn, inner)
        kept_items += (own, other, out_full)
        return result.astype(BF16), values, kept_items

    split = square and lax.axis_size("dp") == 4
    plain_rows = {False: pack_rows, True: pack_rows}
    if split:
        plain_rows = {False: 0, True: pack_rows // 64 * 32 + 32}

    def tied(chains, value):
        for chain in chains:
            value = chain.tie(value)
        return value

    def backward(g_result, g_first, weights, kept_items, earlier=()):
        late = len(earlier) > 0

        gain_a, gain_f, qkv_w, unused = weights
        state, pieces, queries, keys, values, attended, lse, att_rows, middle, normed_ffn, inner = kept_items[:11]
        own, other, out_full = kept_items[11:]
        g_branch = g_result.astype(BF16)
        got_normed, got_branch, got_act = swap_cores(normed_ffn), swap_cores(g_branch), swap_cores(inner[1][2])
        g_normed = None
        g_inner = []
        for (silu, slope, activated), share in zip(inner, (own, other)):
            g_normed, g_gate, g_up = ffn_backward(g_branch, g_normed, silu, slope, share)
            g_inner.append((g_gate, g_up, activated))
        got_gate, got_up = swap_cores(g_inner[1][0]), swap_cores(g_inner[1][1])
        if late:
            g_normed = tied(earlier[0], g_normed)
        g_norm, g_gain_f = normalize_back(middle, gain_f, g_normed)
        g_middle = g_result + g_norm
        g_mid_low = g_middle.astype(BF16)
        g_att_rows = mm(g_mid_low, out_full, NT).astype(BF16)
        g_att_rows, got_gate, got_up = lax.optimization_barrier((g_att_rows, got_gate, got_up))
        g_att = to_heads(g_att_rows)

        def make_packs():
            att_whole = jnp.concatenate(att_rows, axis=1)
            out_grad = mm(att_whole, g_mid_low, TN).astype(BF16).reshape(mp, 2, out_half, model)
            out_kept = lax.dynamic_index_in_dim(out_grad, core, 1, keepdims=False)
            out_sent = lax.dynamic_index_in_dim(out_grad, 1 - core, 1, keepdims=False)
            out_grad = (out_kept.astype(F32) + swap_cores(out_sent).astype(F32)).astype(BF16)
            return pack_grads(
                g_inner[0],
                (got_gate, got_up, got_act),
                normed_ffn,
                got_normed,
                g_branch,
                got_branch,
                by_distance(out_grad, place),
                plain_rows[late],
                lax.axis_index("dp") % 2,
            )

        if not late:
            hidden_packs = make_packs()
            g_att, hidden_packs = lax.optimization_barrier((g_att, hidden_packs))
        if late:
            g_att = tied(earlier[1], g_att)
        g_qkv = attend_back(queries, keys, values, lse, cosine, sine, attended, g_att, g_first, info)
        packs = hidden_packs if not late else make_packs()
        own_chains = [groups_chain(packs[0])] if len(packs) != 2 else []
        if split:
            own_chains.append(halves_chain(packs[-2], packs[-1]))
        if late:
            g_qkv = tied(earlier[2] + own_chains[:1], g_qkv)
        g_parts = [mm(part, qkv_w, NT).astype(BF16) for part in g_qkv]
        if not square:
            g_parts = [g_parts[0][i * tok_rows : (i + 1) * tok_rows] for i in range(mp)]
        g_rows = tied(earlier[3] if late else (), sum_rows_to_owner(g_parts))
        g_norm, g_gain_a = normalize_back(state, gain_a, g_rows)
        g_inputs = g_middle + g_norm
        qkv_grad = qkv_grad_sum(pieces, tied(own_chains[1:], g_qkv) if late else g_qkv)
        qkv_grad = pick_half(qkv_grad, core).astype(F32) + swap_cores(pick_half(qkv_grad, 1 - core)).astype(F32)
        qkv_grad = qkv_grad.reshape(-1, model).astype(BF16)
        if late:
            qkv_grad = plain_chain(qkv_grad)
        else:
            qkv_grad = Chain(qkv_grad, [lambda state: lax.psum(state, "dp")], lambda state: state)
        return g_inputs, g_qkv, (own_chains, qkv_grad, g_gain_a, g_gain_f)

    layers = [
        (layer_gains[i][0], layer_gains[i][1], qkv_weights[i], all_pieces[i]) for i in range(2)
    ]
    h_first, first_values, kept_first = forward(inputs, None, layers[0], first_normed)
    h_second, unused, kept_second = forward(h_first, first_values, layers[1])
    g_second, g_qkv_second, grads_second = backward(g_top, None, layers[1], kept_second)
    chains = grads_second[0]
    g_tokens, unused, grads_first = backward(
        g_second.astype(BF16).astype(F32),
        g_qkv_second,
        layers[0],
        kept_first,
        (chains, chains, [grads_second[1]], chains),
    )

    def ended(chains):
        return jnp.concatenate([chain.end() for chain in chains], axis=0)

    totals_first = (ended(grads_first[0]), grads_first[1].end())
    totals_second = (ended(grads_second[0]), grads_second[1].end())

    def by_layer(low, high, wire):
        mine = jnp.where(is_low, low, high)
        theirs = swap_cores(jnp.where(is_low, high, low).astype(wire)).astype(mine.dtype)
        return in_order(mine, theirs)

    layer_out = jnp.stack(by_layer(h_first, h_second, BF16))
    input_grads = jnp.stack(by_layer(g_tokens, g_second, BF16))
    all_first = jnp.stack(in_order(first_values, swap_cores(first_values)))

    low, high = by_layer(totals_first[0], totals_second[0], BF16)
    qkv_low, qkv_high = by_layer(totals_first[1], totals_second[1], BF16)

    def joined(start, size):
        return jnp.concatenate([low[start : start + size], high[start : start + size]], axis=0).astype(F32)

    gate_grad = joined(0, hid_half)
    up_grad = joined(hid_half, hid_half)
    down_grad = joined(2 * hid_half, hid_half)
    out_grad = joined(3 * hid_half, out_half)
    qkv_grad = jnp.concatenate([qkv_low, qkv_high], axis=0).astype(F32).reshape(model, 3 * width)

    heads_here = width // HEAD_DIM
    first_f32 = first_values.astype(F32).reshape(seq_rows, heads_here, HEAD_DIM)
    squares = jnp.sum(first_f32 * first_f32, axis=(0, 2))
    placed = lax.dynamic_update_slice(
        jnp.zeros((micro_count, heads_here * mp), F32), squares[None], (core, place * heads_here)
    )
    sums = [grads_first[2], grads_second[2], grads_first[3], grads_second[3], placed.reshape(-1)]
    sums = sum_all(jnp.concatenate(sums))
    gain_grads = sums[: 4 * model].reshape(4, model)
    value_norms = sums[4 * model :].reshape(placed.shape)
    attn_gain_grad = lax.dynamic_slice_in_dim(gain_grads, core, 1, 0)
    ffn_gain_grad = lax.dynamic_slice_in_dim(gain_grads, 2 + core, 1, 0)
    return (
        layer_out[None],
        input_grads[None],
        all_first,
        value_norms,
        attn_gain_grad,
        qkv_grad[:, :width][None],
        qkv_grad[:, width : 2 * width][None],
        qkv_grad[:, 2 * width :][None],
        out_grad[None],
        ffn_gain_grad,
        gate_grad.T[None],
        up_grad.T[None],
        down_grad[None],
    )


def solution(mesh):
    in_specs = (
        P(None, ("dp", "mp"), None),
        P(None, "dp"),
        P(None, ("dp", "mp"), None),
        P("section", None),
        P("section", None, "mp"),
        P("section", None, "mp"),
        P("section", None, "mp"),
        P("section", "mp", None),
        P("section", None),
        P("section", None, "mp"),
        P("section", None, "mp"),
        P("section", "mp", None),
    )
    out_specs = (
        P("section", None, ("dp", "mp"), None),
        P("section", None, ("dp", "mp"), None),
        P(None, "dp", "mp"),
        P(),
        P("section", None),
        P("section", None, "mp"),
        P("section", None, "mp"),
        P("section", None, "mp"),
        P("section", "mp", None),
        P("section", None),
        P("section", None, "mp"),
        P("section", None, "mp"),
        P("section", "mp", None),
    )
    return jax.shard_map(shards, mesh=mesh, in_specs=in_specs, out_specs=out_specs, check_vma=False)
```

```python
import functools

import jax
import jax.numpy as jnp
from jax import lax
from jax.experimental import pallas as pl
from jax.experimental.pallas import tpu as pltpu
from jax.sharding import PartitionSpec as P

HEAD_DIM = 64
HALF = HEAD_DIM // 2
EPS = 1e-05
SCALE = HEAD_DIM**-0.5
F32 = jnp.float32
BF16 = jnp.bfloat16
VMEM_BYTES = 56 * 1024 * 1024

NT = (((1,), (1,)), ((), ()))
NN = (((1,), (0,)), ((), ()))
TN = (((0,), (0,)), ((), ()))


def cost(micros):
    return pl.CostEstimate(flops=int(micros * 1.15e9), transcendentals=0, bytes_accessed=1 << 20)


def mm(left, right, dims=NN):
    return lax.dot_general(left, right, dims, preferred_element_type=F32)


def swap_halves(tensor):
    width = tensor.shape[1]
    if width % 128 == 0:
        lane = lax.broadcasted_iota(jnp.int32, tensor.shape, 1)
        ahead = pltpu.roll(tensor, width - HALF, 1)
        behind = pltpu.roll(tensor, HALF, 1)
        return jnp.where(lane % HEAD_DIM < HALF, ahead, behind)
    return jnp.concatenate([tensor[:, HALF:], tensor[:, :HALF]], axis=1)


def qkv_kernel(second, group, parts, fresh, place_ref, *refs):
    piece_refs, refs = refs[:parts], refs[parts:]
    w_ref, cos_ref, sin_ref = refs[:3]
    refs = refs[3:]
    if second:
        first_ref, refs = refs[0], refs[1:]
    if not fresh:
        refs = refs[3:]
    q_ref, k_ref, v_ref = refs
    width = q_ref.shape[1]
    rows = piece_refs[0][...]
    if parts == 2:
        rows = jnp.where(pl.program_id(0) == 0, rows, piece_refs[1][...])
    acc = mm(rows, w_ref[...])
    cosine, sine = cos_ref[...], sin_ref[...]
    for at in range(0, width, group):
        part = acc[:, at : at + group]
        turned = part * cosine + swap_halves(part) * sine
        q_ref[:, at : at + group] = (turned * SCALE).astype(BF16)
        part = acc[:, width + at : width + at + group]
        turned = part * cosine + swap_halves(part) * sine
        k_ref[:, at : at + group] = turned.astype(BF16)
    value = acc[:, 2 * width :]
    if second:
        value = 0.5 * value + 0.5 * first_ref[...].astype(F32)
    v_ref[...] = value.astype(BF16)


def project_qkv(pieces, place, weight, cosine, sine, first, held):
    rows, model = cosine.shape[0], weight.shape[0]
    width = weight.shape[1] // 3
    group = min(width, 128)
    chunk = sum(piece.shape[0] for piece in pieces)
    parts = len(pieces)
    block = pieces[0].shape[0] if parts == 2 else min(512, chunk)
    steps = chunk // block
    second = first is not None
    fresh = held is None

    def at_place(i, place_ref):
        return (place_ref[0] * steps + i, 0)

    row_spec = pl.BlockSpec((block, width), at_place)
    if parts == 2:
        piece_specs = [pl.BlockSpec((block, model), lambda i, p: (0, 0))] * 2
    else:
        piece_specs = [pl.BlockSpec((block, model), lambda i, p: (i, 0))]
    in_specs = piece_specs + [
        pl.BlockSpec((model, 3 * width), lambda i, p: (0, 0)),
        pl.BlockSpec((block, group), at_place),
        pl.BlockSpec((block, group), at_place),
    ]
    args = [*pieces, weight, cosine, sine]
    if second:
        in_specs.append(row_spec)
        args.append(first)
    aliases = {}
    if not fresh:
        aliases = {1 + len(args) + i: i for i in range(3)}
        in_specs += [pl.BlockSpec(memory_space=pl.ANY)] * 3
        args += list(held)
    shape = jax.ShapeDtypeStruct((rows, width), BF16)
    return pl.pallas_call(
        functools.partial(qkv_kernel, second, group, parts, fresh),
        grid_spec=pltpu.PrefetchScalarGridSpec(
            num_scalar_prefetch=1,
            grid=(steps,),
            in_specs=in_specs,
            out_specs=[row_spec] * 3,
        ),
        out_shape=[shape] * 3,
        input_output_aliases=aliases,
        compiler_params=pltpu.CompilerParams(vmem_limit_bytes=VMEM_BYTES),
        cost_estimate=cost(4),
        name="qkv_rope",
    )(place, *args)


def head_lanes(value, head, group):
    per = group // HEAD_DIM
    if per == 1:
        return value
    lane = lax.broadcasted_iota(jnp.int32, value.shape, 1)
    return jnp.where(lane // HEAD_DIM == head % per, value, jnp.zeros_like(value))


def attend_kernel(block, group, parts, info_ref, q_ref, k_ref, v_ref, *refs):
    o_refs, refs = refs[:parts], refs[parts:]
    lse_ref, vt_ref, acc_ref, top_ref, sum_ref, all_ref = refs
    rows, width = k_ref.shape
    heads = width // HEAD_DIM
    per = group // HEAD_DIM
    chunk = rows // parts
    small = min(block, chunk)
    step = pl.program_id(0)
    seg_len = info_ref[0]
    place = info_ref[1]

    @pl.when(step == 0)
    def _():
        for at in range(0, rows, small):
            vt_ref[:, at : at + small] = v_ref[at : at + small, :].astype(F32).T.astype(BF16)

    q_heads = []
    for head in range(heads):
        at = head // per * group
        q_heads.append(head_lanes(q_ref[:, at : at + group], head, group))

    def one(col, masked):
        key_rows = pl.ds(pl.multiple_of(col * block, block), block)
        for head in range(heads):
            at = head // per * group
            own = slice(head * HEAD_DIM, (head + 1) * HEAD_DIM)
            scores = mm(k_ref[key_rows, at : at + group], q_heads[head], NT)
            if masked:
                r = lax.broadcasted_iota(jnp.int32, scores.shape, 0)
                c = lax.broadcasted_iota(jnp.int32, scores.shape, 1)
                scores = jnp.where(r <= c, scores, -1e30)
            top = jnp.max(scores, axis=0, keepdims=True)
            if not masked:
                old = top_ref[head : head + 1, :]
                top = jnp.maximum(top, old)
            probs = jnp.exp(scores - top)
            count = jnp.sum(probs, axis=0, keepdims=True)
            total = mm(vt_ref[own, key_rows], probs.astype(BF16))
            if not masked:
                shrink = jnp.exp(old - top)
                count = count + sum_ref[head : head + 1, :] * shrink
                total = total + acc_ref[own, :] * shrink
            acc_ref[own, :] = total
            top_ref[head : head + 1, :] = top
            sum_ref[head : head + 1, :] = count

    one(step, True)

    @pl.loop(step * block // seg_len * (seg_len // block), step)
    def _(col):
        one(col, False)

    lse_ref[...] = top_ref[:heads, :] + jnp.log(sum_ref[:heads, :])
    for head in range(heads):
        own = slice(head * HEAD_DIM, (head + 1) * HEAD_DIM)
        acc_ref[own, :] = acc_ref[own, :] * (1.0 / sum_ref[head : head + 1, :])
    for at in range(0, block, small):
        turned = acc_ref[:, at : at + small].T.astype(BF16)
        if parts == 1:
            target = step * block + at
        else:
            target = jnp.bitwise_xor(step * (block // chunk) + at // chunk, place) * chunk + at % chunk
        all_ref[pl.ds(pl.multiple_of(target, small), small), :] = turned

    @pl.when(step == pl.num_programs(0) - 1)
    def _():
        for part in range(parts):
            o_refs[part][...] = all_ref[part * chunk : (part + 1) * chunk, :]


def attend(queries, keys, values, info, parts):
    rows, width = queries.shape
    group = min(width, 128)
    heads = width // HEAD_DIM
    block = rows // 2
    chunk = rows // parts
    whole = pl.BlockSpec((rows, width), lambda i, n: (0, 0))
    results = pl.pallas_call(
        functools.partial(attend_kernel, block, group, parts),
        grid_spec=pltpu.PrefetchScalarGridSpec(
            num_scalar_prefetch=1,
            grid=(rows // block,),
            in_specs=[pl.BlockSpec((block, width), lambda i, n: (i, 0)), whole, whole],
            out_specs=[pl.BlockSpec((chunk, width), lambda i, n: (0, 0))] * parts
            + [pl.BlockSpec((heads, block), lambda i, n: (0, i))],
            scratch_shapes=[
                pltpu.VMEM((width, rows), BF16),
                pltpu.VMEM((width, block), F32),
                pltpu.VMEM((8, block), F32),
                pltpu.VMEM((8, block), F32),
                pltpu.VMEM((rows, width), BF16),
            ],
        ),
        out_shape=[jax.ShapeDtypeStruct((chunk, width), BF16)] * parts
        + [jax.ShapeDtypeStruct((heads, rows), F32)],
        compiler_params=pltpu.CompilerParams(vmem_limit_bytes=VMEM_BYTES),
        cost_estimate=cost(18),
        name="attend",
    )(info, queries, keys, values)
    return results[:parts], results[parts]


def attend_back_kernel(second, block, strip, group, parts, info_ref, q_ref, k_ref, v_ref, lse_ref, cos_ref, sin_ref, *refs):
    o_refs, refs = refs[:parts], refs[parts:]
    do_refs, refs = refs[:parts], refs[parts:]
    if not second:
        first_refs, refs = refs[:parts], refs[parts:]
    out_refs, refs = refs[:parts], refs[parts:]
    do_ref, all_ref, dq_ref, dk_ref, dv_ref, delta_ref = refs
    rows, width = q_ref.shape
    heads = width // HEAD_DIM
    per = group // HEAD_DIM
    chunk = rows // parts
    small = min(block, chunk)
    step = pl.program_id(0)
    steps = rows // block
    seg_len = info_ref[0]
    place = info_ref[1]

    @pl.when(step == 0)
    def _():
        dq_ref[...] = jnp.zeros_like(dq_ref)
        head = lax.broadcasted_iota(jnp.int32, (8, width), 0)
        lane = lax.broadcasted_iota(jnp.int32, (8, width), 1)
        pick = jnp.where(lane // HEAD_DIM == head, 1.0, 0.0).astype(F32)
        for part in range(parts):
            for at in range(0, chunk, small):
                grads = do_refs[part][at : at + small, :]
                prod = grads.astype(F32) * o_refs[part][at : at + small, :].astype(F32)
                delta = lax.dot_general(
                    pick, prod, NT, precision=lax.Precision.HIGHEST, preferred_element_type=F32
                )
                if parts == 1:
                    target = at
                else:
                    target = jnp.bitwise_xor(part, place) * chunk + at
                target = pl.ds(pl.multiple_of(target, small), small)
                do_ref[target, :] = grads
                delta_ref[:, target] = delta
            if not second:
                all_ref[part * chunk : (part + 1) * chunk, 2 * width :] = first_refs[part][...]

    dk_ref[...] = jnp.zeros_like(dk_ref)
    dv_ref[...] = jnp.zeros_like(dv_ref)
    base = step * block

    def one(key_off, key_size, query_start, query_size, masked):
        key_rows = pl.ds(pl.multiple_of(base + key_off, strip), key_size)
        query_rows = pl.ds(pl.multiple_of(query_start, strip), query_size)
        for pair in range(heads // per):
            at = pair * group
            keys = k_ref[key_rows, at : at + group]
            values = v_ref[key_rows, at : at + group]
            queries = q_ref[query_rows, at : at + group]
            grads = do_ref[query_rows, at : at + group]
            dq = dk = dv = None
            for sub in range(per):
                head = pair * per + sub
                q_one = head_lanes(queries, head, group)
                do_one = head_lanes(grads, head, group)
                scores = mm(keys, q_one, NT)
                if masked:
                    r = lax.broadcasted_iota(jnp.int32, scores.shape, 0)
                    c = lax.broadcasted_iota(jnp.int32, scores.shape, 1)
                    scores = jnp.where(r <= c, scores, -1e30)
                probs = jnp.exp(scores - lse_ref[head : head + 1, query_rows])
                g_probs = mm(values, do_one, NT)
                g_scores = (probs * (g_probs - delta_ref[head : head + 1, query_rows])).astype(BF16)
                dv_one = mm(probs.astype(BF16), do_one)
                dk_one = mm(g_scores, q_one)
                dq_one = mm(g_scores, head_lanes(keys, head, group), TN)
                dq = dq_one if dq is None else dq + dq_one
                dk = dk_one if dk is None else dk + dk_one
                dv = dv_one if dv is None else dv + dv_one
            dq_ref[query_rows, at : at + group] += dq
            dk_ref[key_off : key_off + key_size, at : at + group] += dk
            dv_ref[key_off : key_off + key_size, at : at + group] += dv

    for off in range(0, block, strip):
        one(off, strip, base + off, block - off, True)

    per_seg = seg_len // block

    @pl.loop(step + 1, (step // per_seg + 1) * per_seg)
    def _(row):
        one(0, block, row * block, block, False)

    def turn_back(value, at_rows):
        return value * cos_ref[at_rows, :] - swap_halves(value) * sin_ref[at_rows, :]

    for off in range(0, block, small):
        here = pl.ds(pl.multiple_of(base + off, small), small)
        if parts == 1:
            target = base + off
        else:
            target = jnp.bitwise_xor(step * (block // chunk) + off // chunk, place) * chunk + off % chunk
        target = pl.ds(pl.multiple_of(target, small), small)
        for at in range(0, width, group):
            g_query = turn_back(dq_ref[here, at : at + group] * SCALE, here)
            g_key = turn_back(dk_ref[off : off + small, at : at + group], here)
            all_ref[target, at : at + group] = g_query.astype(BF16)
            all_ref[target, width + at : width + at + group] = g_key.astype(BF16)
        g_value = dv_ref[off : off + small, :]
        if second:
            g_value = 0.5 * g_value
        else:
            g_value = g_value + all_ref[target, 2 * width :].astype(F32)
        all_ref[target, 2 * width :] = g_value.astype(BF16)

    @pl.when(step == steps - 1)
    def _():
        for part in range(parts):
            out_refs[part][...] = all_ref[part * chunk : (part + 1) * chunk, :]


def attend_back(queries, keys, values, lse, cosine, sine, attended, grads, g_first, info):
    rows, width = queries.shape
    parts = len(attended)
    group = min(width, 128)
    heads = width // HEAD_DIM
    block = rows // 2
    chunk = rows // parts
    second = g_first is None
    whole = pl.BlockSpec((rows, width), lambda i, n: (0, 0))
    table = pl.BlockSpec((rows, group), lambda i, n: (0, 0))
    piece = pl.BlockSpec((chunk, width), lambda i, n: (0, 0))
    in_specs = [whole] * 3 + [pl.BlockSpec((heads, rows), lambda i, n: (0, 0)), table, table] + [piece] * (2 * parts)
    args = [queries, keys, values, lse, cosine, sine, *attended, *grads]
    if not second:
        values_at = 2 if width % 128 == 0 else 0
        if values_at == 0:
            g_first = [part[:, 2 * width :] for part in g_first]
        in_specs += [pl.BlockSpec((chunk, width), lambda i, n: (0, values_at))] * parts
        args += list(g_first)
    return pl.pallas_call(
        functools.partial(attend_back_kernel, second, block, min(256, block), group, parts),
        grid_spec=pltpu.PrefetchScalarGridSpec(
            num_scalar_prefetch=1,
            grid=(rows // block,),
            in_specs=in_specs,
            out_specs=[pl.BlockSpec((chunk, 3 * width), lambda i, n: (0, 0))] * parts,
            scratch_shapes=[
                pltpu.VMEM((rows, width), BF16),
                pltpu.VMEM((rows, 3 * width), BF16),
                pltpu.VMEM((rows, width), F32),
                pltpu.VMEM((block, width), F32),
                pltpu.VMEM((block, width), F32),
                pltpu.VMEM((8, rows), F32),
            ],
        ),
        out_shape=[jax.ShapeDtypeStruct((chunk, 3 * width), BF16)] * parts,
        compiler_params=pltpu.CompilerParams(vmem_limit_bytes=VMEM_BYTES),
        cost_estimate=cost(36),
        name="attend_back",
    )(info, *args)


def out_kernel(info_ref, own_ref, other_ref, state_ref, gain_ref, *refs):
    att_refs = refs[:-3]
    middle_ref, normed_ref, full_ref = refs[-3:]
    mp, out_half, model = own_ref.shape
    low_core = info_ref[2] == 0
    square = mp == 4
    for at in range(mp):
        source = jnp.bitwise_xor(at, info_ref[1]) if square else at
        own, other = own_ref[source], other_ref[source]
        base = at * 2 * out_half
        full_ref[base : base + out_half, :] = jnp.where(low_core, own, other)
        full_ref[base + out_half : base + 2 * out_half, :] = jnp.where(low_core, other, own)
    total = state_ref[...].astype(F32)
    size = mp * 2 * out_half // len(att_refs)
    for part, att_ref in enumerate(att_refs):
        total = total + mm(att_ref[...], full_ref[part * size : (part + 1) * size, :])
    middle_ref[...] = total
    normed_ref[...] = normalize(total, gain_ref[...]).astype(BF16)


def out_project(attended, own, other, state, gain, info):
    rows, model = state.shape
    mp, out_half = own.shape[:2]
    whole = pl.BlockSpec((rows, model), lambda i, n: (0, 0))
    share = pl.BlockSpec(own.shape, lambda i, n: (0, 0, 0))
    full = (mp * 2 * out_half, model)
    return pl.pallas_call(
        out_kernel,
        grid_spec=pltpu.PrefetchScalarGridSpec(
            num_scalar_prefetch=1,
            grid=(1,),
            in_specs=[share, share, whole, pl.BlockSpec((1, model), lambda i, n: (0, 0))]
            + [pl.BlockSpec(part.shape, lambda i, n: (0, 0)) for part in attended],
            out_specs=[whole, whole, pl.BlockSpec(full, lambda i, n: (0, 0))],
        ),
        out_shape=[
            jax.ShapeDtypeStruct((rows, model), F32),
            jax.ShapeDtypeStruct((rows, model), BF16),
            jax.ShapeDtypeStruct(full, BF16),
        ],
        compiler_params=pltpu.CompilerParams(vmem_limit_bytes=VMEM_BYTES),
        cost_estimate=cost(5),
        name="out_project",
    )(info, own, other, state, gain.reshape(1, model), *attended)


def weight_copies(pieces_ref, wide_ref, sems):
    count, hidden, model = wide_ref.shape
    mp = pieces_ref.shape[0]
    size = hidden // mp
    groups = []
    for at in range(count):
        copies = []
        for part in range(mp):
            copies.append(
                pltpu.make_async_copy(
                    pieces_ref.at[part, pl.ds(at * size, size), :],
                    wide_ref.at[at, pl.ds(part * size, size), :],
                    sems.at[at, part],
                )
            )
        groups.append(copies)
    return groups


def ffn_kernel(x_ref, base_ref, pieces_ref, out_ref, silu_ref, slope_ref, act_ref, wide_ref, sems):
    groups = weight_copies(pieces_ref, wide_ref, sems)
    for copies in groups:
        for copy in copies:
            copy.start()
    for copy in groups[0]:
        copy.wait()
    gate = mm(x_ref[...], wide_ref[0], NT)
    for copy in groups[1]:
        copy.wait()
    up = mm(x_ref[...], wide_ref[1], NT)
    sig = 0.5 + 0.5 * jnp.tanh(0.5 * gate)
    silu = gate * sig
    act = (silu * up).astype(BF16)
    silu_ref[...] = silu.astype(BF16)
    slope_ref[...] = (up * (sig + silu * (1.0 - sig))).astype(BF16)
    act_ref[...] = act
    for copy in groups[2]:
        copy.wait()
    out_ref[...] = base_ref[...] + mm(act, wide_ref[2])


def ffn_forward(normed, base, pieces, hidden):
    rows, model = normed.shape
    mp = pieces.shape[0]
    whole = pl.BlockSpec((rows, model), lambda j: (0, 0))
    inner = pl.BlockSpec((rows, hidden), lambda j: (0, 0))
    shape = jax.ShapeDtypeStruct((rows, hidden), BF16)
    return pl.pallas_call(
        ffn_kernel,
        grid=(1,),
        in_specs=[whole, whole, pl.BlockSpec(memory_space=pl.ANY)],
        out_specs=[whole, inner, inner, inner],
        out_shape=[jax.ShapeDtypeStruct((rows, model), F32), shape, shape, shape],
        scratch_shapes=[pltpu.VMEM((3, hidden, model), BF16), pltpu.SemaphoreType.DMA((3, mp))],
        compiler_params=pltpu.CompilerParams(vmem_limit_bytes=VMEM_BYTES),
        cost_estimate=cost(9),
        name="ffn",
    )(normed, base, pieces)


def ffn_back_kernel(more, *refs):
    if more:
        base_ref, refs = refs[0], refs[1:]
    g_ref, silu_ref, slope_ref, pieces_ref, out_ref, g_gate_ref, g_up_ref, wide_ref, sems = refs
    groups = weight_copies(pieces_ref, wide_ref, sems)
    for at in (2, 0, 1):
        for copy in groups[at]:
            copy.start()
    for copy in groups[2]:
        copy.wait()
    g_act = mm(g_ref[...], wide_ref[2], NT)
    g_up = (g_act * silu_ref[...].astype(F32)).astype(BF16)
    g_gate = (g_act * slope_ref[...].astype(F32)).astype(BF16)
    g_gate_ref[...] = g_gate
    g_up_ref[...] = g_up
    for copy in groups[0]:
        copy.wait()
    total = mm(g_gate, wide_ref[0])
    for copy in groups[1]:
        copy.wait()
    total = total + mm(g_up, wide_ref[1])
    out_ref[...] = base_ref[...] + total if more else total


def ffn_backward(g_branch, base, silu, slope, pieces):
    rows, model = g_branch.shape
    hidden = silu.shape[1]
    mp = pieces.shape[0]
    whole = pl.BlockSpec((rows, model), lambda j: (0, 0))
    inner = pl.BlockSpec((rows, hidden), lambda j: (0, 0))
    shape = jax.ShapeDtypeStruct((rows, hidden), BF16)
    more = base is not None
    args = [g_branch, silu, slope, pieces]
    in_specs = [whole, inner, inner, pl.BlockSpec(memory_space=pl.ANY)]
    if more:
        args, in_specs = [base] + args, [whole] + in_specs
    return pl.pallas_call(
        functools.partial(ffn_back_kernel, more),
        grid=(1,),
        in_specs=in_specs,
        out_specs=[whole, inner, inner],
        out_shape=[jax.ShapeDtypeStruct((rows, model), F32), shape, shape],
        scratch_shapes=[pltpu.VMEM((3, hidden, model), BF16), pltpu.SemaphoreType.DMA((3, mp))],
        compiler_params=pltpu.CompilerParams(vmem_limit_bytes=VMEM_BYTES),
        cost_estimate=cost(1),
        name="ffn_back",
    )(*args)


def pack_grads_kernel(size, plain, halves, info_ref, *refs):
    gate, got_gate, up, got_up, act, got_act, x_ref, got_x, g_ref, got_g, out_grad = refs[:11]
    out_refs = refs[11:]
    pack_ref = out_refs[-1]
    count = pack_ref.shape[0]
    jobs = ((gate, x_ref, got_gate, got_x), (up, x_ref, got_up, got_x), (act, g_ref, got_act, got_g))
    for at, (left, right, left_two, right_two) in enumerate(jobs):
        acc = mm(left[...], right[...], TN) + mm(left_two[...], right_two[...], TN)
        for part in range(count):
            pack_ref[part, at * size : (at + 1) * size, :] = acc[part * size : (part + 1) * size].astype(BF16)
    for part in range(count):
        pack_ref[part, 3 * size :, :] = out_grad[part]
    if plain:
        out_refs[0][...] = pack_ref[:, :plain, :]
        out_refs = out_refs[1:]
    if halves:
        cut = plain + halves

        @pl.when(info_ref[0] == 0)
        def _():
            out_refs[0][...] = pack_ref[:, plain:cut, :]
            out_refs[1][...] = pack_ref[:, cut:, :]

        @pl.when(info_ref[0] == 1)
        def _():
            out_refs[0][...] = pack_ref[:, cut:, :]
            out_refs[1][...] = pack_ref[:, plain:cut, :]


def pack_grads(inner, got_inner, normed, got_normed, g_branch, got_branch, out_grad, plain, first):
    rows, model = normed.shape
    hidden = inner[0].shape[1]
    mp, out_half = out_grad.shape[:2]
    size = hidden // mp
    block = min(512, model)
    left = pl.BlockSpec((rows, hidden), lambda j, n: (0, 0))
    right = pl.BlockSpec((rows, block), lambda j, n: (0, j))
    pack_rows = 3 * size + out_half
    args = []
    for own, got in zip(inner, got_inner):
        args += [own, got]
    halves = (pack_rows - plain) // 2
    if halves == 0:
        plain, sizes, scratch = 0, [pack_rows], []
    else:
        sizes = ([plain] if plain else []) + [halves, halves]
        scratch = [pltpu.VMEM((mp, pack_rows, block), BF16)]
    return pl.pallas_call(
        functools.partial(pack_grads_kernel, size, plain, halves),
        grid_spec=pltpu.PrefetchScalarGridSpec(
            num_scalar_prefetch=1,
            grid=(model // block,),
            in_specs=[left] * 6
            + [right] * 4
            + [pl.BlockSpec((mp, out_half, block), lambda j, n: (0, 0, j))],
            out_specs=[pl.BlockSpec((mp, part, block), lambda j, n: (0, 0, j)) for part in sizes],
            scratch_shapes=scratch,
        ),
        out_shape=[jax.ShapeDtypeStruct((mp, part, model), BF16) for part in sizes],
        compiler_params=pltpu.CompilerParams(vmem_limit_bytes=VMEM_BYTES),
        cost_estimate=cost(15),
        name="pack_grads",
    )(first.astype(jnp.int32).reshape(1), *args, normed, got_normed, g_branch, got_branch, out_grad)


def place_kernel(which_ref, first_ref, second_ref, out_ref):
    @pl.when(pl.program_id(0) == 0)
    def _():
        out_ref[...] = first_ref[...]

    @pl.when(pl.program_id(0) == 1)
    def _():
        out_ref[...] = second_ref[...]


def place_two(first, second, which, axis):
    rows, model = first.shape
    if (rows, model)[axis] % (16, 128)[axis]:
        ordered = jnp.where(which == 0, first, second), jnp.where(which == 0, second, first)
        return jnp.concatenate(ordered, axis=axis)
    whole = pl.BlockSpec((rows, model), lambda i, w: (0, 0))

    def target(i, w):
        spot = jnp.bitwise_xor(w[0], i)
        return (spot, 0) if axis == 0 else (0, spot)

    shape = (2 * rows, model) if axis == 0 else (rows, 2 * model)
    return pl.pallas_call(
        place_kernel,
        grid_spec=pltpu.PrefetchScalarGridSpec(
            num_scalar_prefetch=1,
            grid=(2,),
            in_specs=[whole, whole],
            out_specs=pl.BlockSpec((rows, model), target),
        ),
        out_shape=jax.ShapeDtypeStruct(shape, first.dtype),
        compiler_params=pltpu.CompilerParams(vmem_limit_bytes=VMEM_BYTES),
        cost_estimate=cost(2),
        name="place_two",
    )(which.astype(jnp.int32).reshape(1), first, second)


def qkv_grad_kernel(count, *refs):
    out_ref = refs[-1]
    acc = None
    at = 0
    whole = count
    grads = refs[whole:-1]
    part = 0
    for i in range(count):
        size = refs[i].shape[0]
        chunk = grads[part].shape[0]
        product = mm(refs[i][...], grads[part][at : at + size, :], TN)
        acc = product if acc is None else acc + product
        at += size
        if at == chunk:
            at, part = 0, part + 1
    out_ref[...] = acc.astype(BF16)


def qkv_grad_sum(pieces, grads):
    model = pieces[0].shape[1]
    width = grads[0].shape[1]
    block = min(512, model)
    return pl.pallas_call(
        functools.partial(qkv_grad_kernel, len(pieces)),
        grid=(model // block,),
        in_specs=[pl.BlockSpec((piece.shape[0], block), lambda i: (0, i)) for piece in pieces]
        + [pl.BlockSpec(part.shape, lambda i: (0, 0)) for part in grads],
        out_specs=pl.BlockSpec((block, width), lambda i: (i, 0)),
        out_shape=jax.ShapeDtypeStruct((model, width), BF16),
        compiler_params=pltpu.CompilerParams(vmem_limit_bytes=VMEM_BYTES),
        cost_estimate=cost(7),
        name="qkv_grad",
    )(*pieces, *grads)


def normalize(rows_in, gain):
    scale = lax.rsqrt(jnp.mean(rows_in * rows_in, axis=-1, keepdims=True) + EPS)
    return rows_in * scale * gain


def normalize_back(rows_in, gain, grad):
    scale = lax.rsqrt(jnp.mean(rows_in * rows_in, axis=-1, keepdims=True) + EPS)
    gained = grad * gain
    inner = jnp.mean(gained * rows_in, axis=-1, keepdims=True)
    g_rows = scale * (gained - rows_in * (scale * scale * inner))
    return g_rows, jnp.sum(grad * (rows_in * scale), axis=0)


def rotary_tables(rows, seg_len, lanes):
    positions = (jnp.arange(rows, dtype=jnp.int32) % seg_len).astype(F32)
    inverse_freq = 10000.0 ** (-(jnp.arange(HALF, dtype=F32) * 2.0 / HEAD_DIM))
    angles = positions[:, None] * inverse_freq[None, :]
    cosine, sine = jnp.cos(angles), jnp.sin(angles)
    cosine = jnp.concatenate([cosine, cosine] * (lanes // HEAD_DIM), axis=1)
    sine = jnp.concatenate([-sine, sine] * (lanes // HEAD_DIM), axis=1)
    return cosine, sine


def swap_cores(value):
    return lax.ppermute(value, "section", [(0, 1), (1, 0)])


def across(value, axis, bits):
    return lax.ppermute(value, axis, [(i, i ^ bits) for i in range(lax.axis_size(axis))])


def is_square():
    return lax.axis_size("mp") == 4


def spread_rows(value):
    if not is_square():
        return [[lax.all_gather(value, "mp", axis=0, tiled=True)]]
    half = value.shape[0] // 2
    from_x, from_y = across(value, "mp", 1), across(value, "mp", 2)
    far_low, far_high = across(from_y[:half], "mp", 1), across(from_x[half:], "mp", 2)
    return [[value], [from_x], [from_y], [far_low, far_high]]


def sum_rows_to_owner(parts):
    if not is_square():
        total = lax.psum_scatter(jnp.concatenate(parts, axis=0), "mp", scatter_dimension=0, tiled=True)
        return total.astype(F32)
    half = parts[0].shape[0] // 2
    own, to_x, to_y, to_far = parts
    far_low = across(to_far[:half], "mp", 1)
    far_high = across(to_far[half:], "mp", 2)
    x_low = across(to_x[:half], "mp", 1)
    y_high = across(to_y[half:], "mp", 2)
    passed_x = (to_x[half:].astype(F32) + far_high.astype(F32)).astype(BF16)
    passed_y = (to_y[:half].astype(F32) + far_low.astype(F32)).astype(BF16)
    x_high = across(passed_x, "mp", 1)
    y_low = across(passed_y, "mp", 2)
    own = own.astype(F32)
    low = own[:half] + x_low.astype(F32) + y_low.astype(F32)
    high = own[half:] + x_high.astype(F32) + y_high.astype(F32)
    return jnp.concatenate([low, high], axis=0)


def group_steps():
    return 4 if lax.axis_size("dp") == 4 else 1


def sum_groups_step(step, state):
    if lax.axis_size("dp") != 4:
        return (lax.psum(state[0], "dp"), None)
    index = lax.axis_index("dp")
    low, high = index % 2, index // 2
    kept, got = state
    bits, which = ((1, low), (2, high), (2, high), (1, low))[step]
    if step < 2:
        whole = kept if got is None else (kept.astype(F32) + got.astype(F32)).astype(BF16)
        size = whole.shape[1] // 2
        kept = lax.dynamic_slice_in_dim(whole, which * size, size, 1)
        sent = lax.dynamic_slice_in_dim(whole, (1 - which) * size, size, 1)
        return kept, across(sent, "dp", bits)
    if step == 2:
        whole = (kept.astype(F32) + got.astype(F32)).astype(BF16)
    else:
        whole = place_two(kept, got, high, 1)
    return whole, across(whole, "dp", bits)


def sum_groups_end(state):
    if lax.axis_size("dp") != 4:
        return state[0]
    return place_two(state[0], state[1], lax.axis_index("dp") % 2, 1)


def sum_groups(value, state=None, start=0):
    if state is None:
        state = (value, None)
    for step in range(start, group_steps()):
        state = sum_groups_step(step, state)
    return sum_groups_end(state)


def add_low(left, right):
    return (left.astype(F32) + right.astype(F32)).astype(BF16)


def scatter_parts(parts):
    rows = parts.reshape(-1, parts.shape[2])
    return lax.psum_scatter(rows, "mp", scatter_dimension=0, tiled=True)


class Chain:
    def __init__(self, state, steps, last):
        self.state, self.steps, self.last = state, list(steps), last

    def tie(self, value):
        if self.steps:
            value, self.state = lax.optimization_barrier((value, self.state))
            self.state = self.steps.pop(0)(self.state)
        return value

    def end(self):
        while self.steps:
            self.state = self.steps.pop(0)(self.state)
        return self.last(self.state)


def groups_chain(parts):
    steps = [lambda state: sum_groups_step(0, (state, None))]
    steps += [functools.partial(sum_groups_step, step) for step in range(1, group_steps())]
    return Chain(scatter_parts(parts), steps, sum_groups_end)


def waiting_chain(value):
    steps = [lambda state: sum_groups_step(0, (state, None))]
    steps += [functools.partial(sum_groups_step, step) for step in range(1, group_steps())]
    return Chain(value, steps, sum_groups_end)


def plain_chain(value):
    steps = [functools.partial(sum_groups_step, step) for step in range(1, group_steps())]
    return Chain(sum_groups_step(0, (value, None)), steps, sum_groups_end)


def halves_chain(kept, sent):
    steps = [
        lambda state: scatter_parts(add_low(*state)),
        lambda state: (state, across(state, "dp", 2)),
        lambda state: (lambda total: (total, across(total, "dp", 1)))(add_low(*state)),
    ]
    return Chain(
        (kept, across(sent, "dp", 1)),
        steps,
        lambda state: place_two(state[0], state[1], lax.axis_index("dp") % 2, 0),
    )


def by_distance(blocks, place):
    if not is_square():
        return blocks
    blocks = jnp.where(place % 2 == 0, blocks, jnp.stack([blocks[i] for i in (1, 0, 3, 2)]))
    return jnp.where(place < 2, blocks, jnp.stack([blocks[i] for i in (2, 3, 0, 1)]))


def sum_all(value):
    if not is_square() or lax.axis_size("dp") != 4:
        return lax.psum(value, ("section", "dp", "mp"))
    value = value + across(value, "section", 1)
    for axis in ("mp", "dp"):
        for bits in (1, 2):
            value = value + across(value, axis, bits)
    return value


def pick_half(value, which, axis=0):
    size = value.shape[axis] // 2
    return lax.dynamic_slice_in_dim(value, which * size, size, axis)


def shards(
    tokens,
    layout,
    cotangent,
    attn_gain,
    query_weight,
    key_weight,
    value_weight,
    out_weight,
    ffn_gain,
    gate_weight,
    up_weight,
    down_weight,
):
    core = lax.axis_index("section")
    is_low = core == 0
    micro_count, tok_rows, model = tokens.shape
    mp = lax.axis_size("mp")
    place = lax.axis_index("mp").astype(jnp.int32)
    square = is_square()
    parts = mp if square else 1
    seq_rows = tok_rows * mp
    width = query_weight.shape[2]
    hidden = gate_weight.shape[2]
    hid_half = hidden // 2
    out_half = width // 2
    group = min(width, 128)

    def in_order(own, other):
        return jnp.where(is_low, own, other), jnp.where(is_low, other, own)

    inputs = lax.dynamic_index_in_dim(tokens, core, 0, keepdims=False)
    g_top = lax.dynamic_index_in_dim(cotangent, core, 0, keepdims=False)
    pack_layout = lax.dynamic_index_in_dim(layout[:, 0], core, 0, keepdims=False)
    seg_len = (seq_rows // pack_layout).astype(jnp.int32)
    info = jnp.stack([seg_len, place, core.astype(jnp.int32)])
    cosine, sine = rotary_tables(seq_rows, seg_len, group)

    own_qkv = jnp.concatenate([query_weight[0], key_weight[0], value_weight[0]], axis=1)
    qkv_weights = in_order(own_qkv, swap_cores(own_qkv))
    gains = jnp.concatenate([attn_gain, ffn_gain], axis=0)
    layer_gains = in_order(gains, swap_cores(gains))

    first_normed = normalize(inputs.astype(F32), layer_gains[0][0]).astype(BF16)
    first_normed, gate_weight, up_weight, down_weight, out_weight = lax.optimization_barrier(
        (first_normed, gate_weight, up_weight, down_weight, out_weight)
    )
    halves = jnp.concatenate(
        [
            gate_weight[0].T.reshape(2, hid_half, model),
            up_weight[0].T.reshape(2, hid_half, model),
            down_weight[0].reshape(2, hid_half, model),
            out_weight[0].reshape(2, out_half, model),
        ],
        axis=1,
    )
    kept = lax.dynamic_index_in_dim(halves, core, 0, keepdims=False)
    sent = lax.dynamic_index_in_dim(halves, 1 - core, 0, keepdims=False)
    packs = in_order(kept, swap_cores(sent))
    pack_rows = packs[0].shape[0]

    all_pieces = [lax.all_gather(pack, "mp", axis=0, tiled=False) for pack in packs]

    hid_all = mp * hid_half

    def whole_rows(pieces):
        if hid_half % 16 == 0:
            return pieces
        starts = [i * hid_half for i in range(3)]
        parts = [pieces[:, at : at + hid_half].reshape(hid_all, model) for at in starts]
        return jnp.concatenate(parts, axis=0)[None]

    def to_owners(attended):
        if not square:
            blocks = attended[0].reshape(mp, tok_rows, width)
            moved = lax.all_to_all(blocks, "mp", 0, 0)
            return [jnp.transpose(moved, (1, 0, 2)).reshape(tok_rows, mp * width)]
        moved = {i: across(attended[i], "mp", i) for i in (3, 1, 2)}
        return [attended[0], moved[1], moved[2], moved[3]]

    def to_heads(value):
        if not square:
            blocks = jnp.transpose(value.reshape(tok_rows, mp, width), (1, 0, 2))
            return [lax.all_to_all(blocks, "mp", 0, 0).reshape(seq_rows, width)]
        blocks = [value[:, i * width : (i + 1) * width] for i in range(mp)]
        moved = {i: across(blocks[i], "mp", i) for i in (3, 1, 2)}
        return [blocks[0], moved[1], moved[2], moved[3]]

    def forward(rows_low, first, weights, normed=None):
        gain_a, gain_f, qkv_w, pieces_w = weights
        state = rows_low.astype(F32)
        if normed is None:
            normed = normalize(state, gain_a).astype(BF16)
        pieces = spread_rows(normed)
        held = None
        for index, piece in enumerate(pieces):
            spot = jnp.bitwise_xor(place, index) if square else jnp.int32(0)
            held = project_qkv(piece, spot.reshape(1), qkv_w, cosine, sine, first, held)
        queries, keys, values = held
        attended, lse = attend(queries, keys, values, info, parts)
        attended, pieces_w = lax.optimization_barrier((attended, pieces_w))
        out_own = pieces_w[:, 3 * hid_half :]
        out_other = swap_cores(out_own)
        own, other = whole_rows(pieces_w), whole_rows(swap_cores(pieces_w))
        att_rows = to_owners(attended)
        middle, normed_ffn, out_full = out_project(att_rows, out_own, out_other, rows_low, gain_f, info)
        result = middle
        inner = []
        for share in (own, other):
            result, silu, slope, activated = ffn_forward(normed_ffn, result, share, hid_all)
            inner.append((silu, slope, activated))
        flat = [part for piece in pieces for part in piece]
        kept_items = (state, flat, queries, keys, values, attended, lse, att_rows, middle, normed_ffn, inner)
        kept_items += (own, other, out_full)
        return result.astype(BF16), values, kept_items

    split = square and lax.axis_size("dp") == 4
    plain_rows = {False: pack_rows, True: pack_rows}
    if split:
        plain_rows = {False: 0, True: pack_rows // 64 * 32 + 32}

    def tied(chains, value):
        for chain in chains:
            value = chain.tie(value)
        return value

    def backward(g_result, g_first, weights, kept_items, earlier=()):
        late = len(earlier) > 0

        gain_a, gain_f, qkv_w, unused = weights
        state, pieces, queries, keys, values, attended, lse, att_rows, middle, normed_ffn, inner = kept_items[:11]
        own, other, out_full = kept_items[11:]
        g_branch = g_result.astype(BF16)
        got_normed, got_branch, got_act = swap_cores(normed_ffn), swap_cores(g_branch), swap_cores(inner[1][2])
        g_normed = None
        g_inner = []
        for (silu, slope, activated), share in zip(inner, (own, other)):
            g_normed, g_gate, g_up = ffn_backward(g_branch, g_normed, silu, slope, share)
            g_inner.append((g_gate, g_up, activated))
        got_gate, got_up = swap_cores(g_inner[1][0]), swap_cores(g_inner[1][1])
        if late:
            g_normed = tied(earlier[0], g_normed)
        g_norm, g_gain_f = normalize_back(middle, gain_f, g_normed)
        g_middle = g_result + g_norm
        g_mid_low = g_middle.astype(BF16)
        g_att_rows = mm(g_mid_low, out_full, NT).astype(BF16)
        g_att_rows, got_gate, got_up = lax.optimization_barrier((g_att_rows, got_gate, got_up))
        g_att = to_heads(g_att_rows)

        def make_packs():
            att_whole = jnp.concatenate(att_rows, axis=1)
            out_grad = mm(att_whole, g_mid_low, TN).astype(BF16).reshape(mp, 2, out_half, model)
            out_kept = lax.dynamic_index_in_dim(out_grad, core, 1, keepdims=False)
            out_sent = lax.dynamic_index_in_dim(out_grad, 1 - core, 1, keepdims=False)
            out_grad = (out_kept.astype(F32) + swap_cores(out_sent).astype(F32)).astype(BF16)
            return pack_grads(
                g_inner[0],
                (got_gate, got_up, got_act),
                normed_ffn,
                got_normed,
                g_branch,
                got_branch,
                by_distance(out_grad, place),
                plain_rows[late],
                lax.axis_index("dp") % 2,
            )

        if not late:
            hidden_packs = make_packs()
            g_att, hidden_packs = lax.optimization_barrier((g_att, hidden_packs))
        if late:
            g_att = tied(earlier[1], g_att)
        g_qkv = attend_back(queries, keys, values, lse, cosine, sine, attended, g_att, g_first, info)
        packs = hidden_packs if not late else make_packs()
        own_chains = [groups_chain(packs[0])] if len(packs) != 2 else []
        if split:
            own_chains.append(halves_chain(packs[-2], packs[-1]))
        if late:
            g_qkv = tied(earlier[2] + own_chains[:1], g_qkv)
        g_parts = [mm(part, qkv_w, NT).astype(BF16) for part in g_qkv]
        if not square:
            g_parts = [g_parts[0][i * tok_rows : (i + 1) * tok_rows] for i in range(mp)]
        g_rows = tied(earlier[3] if late else (), sum_rows_to_owner(g_parts))
        g_norm, g_gain_a = normalize_back(state, gain_a, g_rows)
        g_inputs = g_middle + g_norm
        qkv_grad = qkv_grad_sum(pieces, tied(own_chains[1:], g_qkv) if late else g_qkv)
        qkv_grad = pick_half(qkv_grad, core).astype(F32) + swap_cores(pick_half(qkv_grad, 1 - core)).astype(F32)
        qkv_grad = qkv_grad.reshape(-1, model).astype(BF16)
        if late:
            qkv_grad = plain_chain(qkv_grad)
        else:
            qkv_grad = waiting_chain(qkv_grad)
        return g_inputs, g_qkv, (own_chains, qkv_grad, g_gain_a, g_gain_f)

    layers = [
        (layer_gains[i][0], layer_gains[i][1], qkv_weights[i], all_pieces[i]) for i in range(2)
    ]
    h_first, first_values, kept_first = forward(inputs, None, layers[0], first_normed)
    h_second, unused, kept_second = forward(h_first, first_values, layers[1])
    g_second, g_qkv_second, grads_second = backward(g_top, None, layers[1], kept_second)
    chains = grads_second[0]
    g_tokens, unused, grads_first = backward(
        g_second.astype(BF16).astype(F32),
        g_qkv_second,
        layers[0],
        kept_first,
        (chains, chains + [grads_second[1]], [], chains + [grads_second[1]]),
    )

    large, small = grads_first[0][0], grads_first[1]
    while len(large.steps) > 1:
        large.state = large.steps.pop(0)(large.state)
    if large.steps:
        large.state = large.steps.pop(0)(large.state)
        small.state = small.steps.pop(0)(small.state)
        large.state, small.state = lax.optimization_barrier((large.state, small.state))

    def ended(chains):
        return jnp.concatenate([chain.end() for chain in chains], axis=0)

    totals_first = (ended(grads_first[0]), grads_first[1].end())
    totals_second = (ended(grads_second[0]), grads_second[1].end())

    def by_layer(low, high, wire):
        mine = jnp.where(is_low, low, high)
        theirs = swap_cores(jnp.where(is_low, high, low).astype(wire)).astype(mine.dtype)
        return in_order(mine, theirs)

    layer_out = jnp.stack(by_layer(h_first, h_second, BF16))
    input_grads = jnp.stack(by_layer(g_tokens, g_second, BF16))
    all_first = jnp.stack(in_order(first_values, swap_cores(first_values)))

    low, high = by_layer(totals_first[0], totals_second[0], BF16)
    qkv_low, qkv_high = by_layer(totals_first[1], totals_second[1], BF16)

    def joined(start, size):
        return jnp.concatenate([low[start : start + size], high[start : start + size]], axis=0).astype(F32)

    gate_grad = joined(0, hid_half)
    up_grad = joined(hid_half, hid_half)
    down_grad = joined(2 * hid_half, hid_half)
    out_grad = joined(3 * hid_half, out_half)
    qkv_grad = jnp.concatenate([qkv_low, qkv_high], axis=0).astype(F32).reshape(model, 3 * width)

    heads_here = width // HEAD_DIM
    first_f32 = first_values.astype(F32).reshape(seq_rows, heads_here, HEAD_DIM)
    squares = jnp.sum(first_f32 * first_f32, axis=(0, 2))
    placed = lax.dynamic_update_slice(
        jnp.zeros((micro_count, heads_here * mp), F32), squares[None], (core, place * heads_here)
    )
    sums = [grads_first[2], grads_second[2], grads_first[3], grads_second[3], placed.reshape(-1)]
    sums = sum_all(jnp.concatenate(sums))
    gain_grads = sums[: 4 * model].reshape(4, model)
    value_norms = sums[4 * model :].reshape(placed.shape)
    attn_gain_grad = lax.dynamic_slice_in_dim(gain_grads, core, 1, 0)
    ffn_gain_grad = lax.dynamic_slice_in_dim(gain_grads, 2 + core, 1, 0)
    return (
        layer_out[None],
        input_grads[None],
        all_first,
        value_norms,
        attn_gain_grad,
        qkv_grad[:, :width][None],
        qkv_grad[:, width : 2 * width][None],
        qkv_grad[:, 2 * width :][None],
        out_grad[None],
        ffn_gain_grad,
        gate_grad.T[None],
        up_grad.T[None],
        down_grad[None],
    )


def solution(mesh):
    in_specs = (
        P(None, ("dp", "mp"), None),
        P(None, "dp"),
        P(None, ("dp", "mp"), None),
        P("section", None),
        P("section", None, "mp"),
        P("section", None, "mp"),
        P("section", None, "mp"),
        P("section", "mp", None),
        P("section", None),
        P("section", None, "mp"),
        P("section", None, "mp"),
        P("section", "mp", None),
    )
    out_specs = (
        P("section", None, ("dp", "mp"), None),
        P("section", None, ("dp", "mp"), None),
        P(None, "dp", "mp"),
        P(),
        P("section", None),
        P("section", None, "mp"),
        P("section", None, "mp"),
        P("section", None, "mp"),
        P("section", "mp", None),
        P("section", None),
        P("section", None, "mp"),
        P("section", None, "mp"),
        P("section", "mp", None),
    )
    return jax.shard_map(shards, mesh=mesh, in_specs=in_specs, out_specs=out_specs, check_vma=False)
```

```python
import functools

import jax
import jax.numpy as jnp
from jax import lax
from jax.experimental import pallas as pl
from jax.experimental.pallas import tpu as pltpu
from jax.sharding import PartitionSpec as P

HEAD_DIM = 64
HALF = HEAD_DIM // 2
EPS = 1e-05
SCALE = HEAD_DIM**-0.5
F32 = jnp.float32
BF16 = jnp.bfloat16
VMEM_BYTES = 56 * 1024 * 1024

NT = (((1,), (1,)), ((), ()))
NN = (((1,), (0,)), ((), ()))
TN = (((0,), (0,)), ((), ()))


def cost(micros):
    return pl.CostEstimate(flops=int(micros * 1.15e9), transcendentals=0, bytes_accessed=1 << 20)


def mm(left, right, dims=NN):
    return lax.dot_general(left, right, dims, preferred_element_type=F32)


def swap_halves(tensor):
    width = tensor.shape[1]
    if width % 128 == 0:
        lane = lax.broadcasted_iota(jnp.int32, tensor.shape, 1)
        ahead = pltpu.roll(tensor, width - HALF, 1)
        behind = pltpu.roll(tensor, HALF, 1)
        return jnp.where(lane % HEAD_DIM < HALF, ahead, behind)
    return jnp.concatenate([tensor[:, HALF:], tensor[:, :HALF]], axis=1)


def qkv_kernel(second, group, parts, fresh, place_ref, *refs):
    piece_refs, refs = refs[:parts], refs[parts:]
    w_ref, cos_ref, sin_ref = refs[:3]
    refs = refs[3:]
    if second:
        first_ref, refs = refs[0], refs[1:]
    if not fresh:
        refs = refs[3:]
    q_ref, k_ref, v_ref = refs
    width = q_ref.shape[1]
    rows = piece_refs[0][...]
    if parts == 2:
        rows = jnp.where(pl.program_id(0) == 0, rows, piece_refs[1][...])
    acc = mm(rows, w_ref[...])
    cosine, sine = cos_ref[...], sin_ref[...]
    for at in range(0, width, group):
        part = acc[:, at : at + group]
        turned = part * cosine + swap_halves(part) * sine
        q_ref[:, at : at + group] = (turned * SCALE).astype(BF16)
        part = acc[:, width + at : width + at + group]
        turned = part * cosine + swap_halves(part) * sine
        k_ref[:, at : at + group] = turned.astype(BF16)
    value = acc[:, 2 * width :]
    if second:
        value = 0.5 * value + 0.5 * first_ref[...].astype(F32)
    v_ref[...] = value.astype(BF16)


def project_qkv(pieces, place, weight, cosine, sine, first, held):
    rows, model = cosine.shape[0], weight.shape[0]
    width = weight.shape[1] // 3
    group = min(width, 128)
    chunk = sum(piece.shape[0] for piece in pieces)
    parts = len(pieces)
    block = pieces[0].shape[0] if parts == 2 else min(512, chunk)
    steps = chunk // block
    second = first is not None
    fresh = held is None

    def at_place(i, place_ref):
        return (place_ref[0] * steps + i, 0)

    row_spec = pl.BlockSpec((block, width), at_place)
    if parts == 2:
        piece_specs = [pl.BlockSpec((block, model), lambda i, p: (0, 0))] * 2
    else:
        piece_specs = [pl.BlockSpec((block, model), lambda i, p: (i, 0))]
    in_specs = piece_specs + [
        pl.BlockSpec((model, 3 * width), lambda i, p: (0, 0)),
        pl.BlockSpec((block, group), at_place),
        pl.BlockSpec((block, group), at_place),
    ]
    args = [*pieces, weight, cosine, sine]
    if second:
        in_specs.append(row_spec)
        args.append(first)
    aliases = {}
    if not fresh:
        aliases = {1 + len(args) + i: i for i in range(3)}
        in_specs += [pl.BlockSpec(memory_space=pl.ANY)] * 3
        args += list(held)
    shape = jax.ShapeDtypeStruct((rows, width), BF16)
    return pl.pallas_call(
        functools.partial(qkv_kernel, second, group, parts, fresh),
        grid_spec=pltpu.PrefetchScalarGridSpec(
            num_scalar_prefetch=1,
            grid=(steps,),
            in_specs=in_specs,
            out_specs=[row_spec] * 3,
        ),
        out_shape=[shape] * 3,
        input_output_aliases=aliases,
        compiler_params=pltpu.CompilerParams(vmem_limit_bytes=VMEM_BYTES),
        cost_estimate=cost(4),
        name="qkv_rope",
    )(place, *args)


def head_lanes(value, head, group):
    per = group // HEAD_DIM
    if per == 1:
        return value
    lane = lax.broadcasted_iota(jnp.int32, value.shape, 1)
    return jnp.where(lane // HEAD_DIM == head % per, value, jnp.zeros_like(value))


def attend_kernel(block, group, parts, info_ref, q_ref, k_ref, v_ref, *refs):
    o_refs, refs = refs[:parts], refs[parts:]
    lse_ref, vt_ref, acc_ref, top_ref, sum_ref, all_ref = refs
    rows, width = k_ref.shape
    heads = width // HEAD_DIM
    per = group // HEAD_DIM
    chunk = rows // parts
    small = min(block, chunk)
    step = pl.program_id(0)
    seg_len = info_ref[0]
    place = info_ref[1]

    @pl.when(step == 0)
    def _():
        for at in range(0, rows, small):
            vt_ref[:, at : at + small] = v_ref[at : at + small, :].astype(F32).T.astype(BF16)

    q_heads = []
    for head in range(heads):
        at = head // per * group
        q_heads.append(head_lanes(q_ref[:, at : at + group], head, group))

    def one(col, masked):
        key_rows = pl.ds(pl.multiple_of(col * block, block), block)
        for head in range(heads):
            at = head // per * group
            own = slice(head * HEAD_DIM, (head + 1) * HEAD_DIM)
            scores = mm(k_ref[key_rows, at : at + group], q_heads[head], NT)
            if masked:
                r = lax.broadcasted_iota(jnp.int32, scores.shape, 0)
                c = lax.broadcasted_iota(jnp.int32, scores.shape, 1)
                scores = jnp.where(r <= c, scores, -1e30)
            top = jnp.max(scores, axis=0, keepdims=True)
            if not masked:
                old = top_ref[head : head + 1, :]
                top = jnp.maximum(top, old)
            probs = jnp.exp(scores - top)
            count = jnp.sum(probs, axis=0, keepdims=True)
            total = mm(vt_ref[own, key_rows], probs.astype(BF16))
            if not masked:
                shrink = jnp.exp(old - top)
                count = count + sum_ref[head : head + 1, :] * shrink
                total = total + acc_ref[own, :] * shrink
            acc_ref[own, :] = total
            top_ref[head : head + 1, :] = top
            sum_ref[head : head + 1, :] = count

    one(step, True)

    @pl.loop(step * block // seg_len * (seg_len // block), step)
    def _(col):
        one(col, False)

    lse_ref[...] = top_ref[:heads, :] + jnp.log(sum_ref[:heads, :])
    for head in range(heads):
        own = slice(head * HEAD_DIM, (head + 1) * HEAD_DIM)
        acc_ref[own, :] = acc_ref[own, :] * (1.0 / sum_ref[head : head + 1, :])
    for at in range(0, block, small):
        turned = acc_ref[:, at : at + small].T.astype(BF16)
        if parts == 1:
            target = step * block + at
        else:
            target = jnp.bitwise_xor(step * (block // chunk) + at // chunk, place) * chunk + at % chunk
        all_ref[pl.ds(pl.multiple_of(target, small), small), :] = turned

    @pl.when(step == pl.num_programs(0) - 1)
    def _():
        for part in range(parts):
            o_refs[part][...] = all_ref[part * chunk : (part + 1) * chunk, :]


def attend(queries, keys, values, info, parts):
    rows, width = queries.shape
    group = min(width, 128)
    heads = width // HEAD_DIM
    block = rows // 2
    chunk = rows // parts
    whole = pl.BlockSpec((rows, width), lambda i, n: (0, 0))
    results = pl.pallas_call(
        functools.partial(attend_kernel, block, group, parts),
        grid_spec=pltpu.PrefetchScalarGridSpec(
            num_scalar_prefetch=1,
            grid=(rows // block,),
            in_specs=[pl.BlockSpec((block, width), lambda i, n: (i, 0)), whole, whole],
            out_specs=[pl.BlockSpec((chunk, width), lambda i, n: (0, 0))] * parts
            + [pl.BlockSpec((heads, block), lambda i, n: (0, i))],
            scratch_shapes=[
                pltpu.VMEM((width, rows), BF16),
                pltpu.VMEM((width, block), F32),
                pltpu.VMEM((8, block), F32),
                pltpu.VMEM((8, block), F32),
                pltpu.VMEM((rows, width), BF16),
            ],
        ),
        out_shape=[jax.ShapeDtypeStruct((chunk, width), BF16)] * parts
        + [jax.ShapeDtypeStruct((heads, rows), F32)],
        compiler_params=pltpu.CompilerParams(vmem_limit_bytes=VMEM_BYTES),
        cost_estimate=cost(18),
        name="attend",
    )(info, queries, keys, values)
    return results[:parts], results[parts]


def attend_back_kernel(second, block, strip, group, parts, info_ref, q_ref, k_ref, v_ref, lse_ref, cos_ref, sin_ref, *refs):
    o_refs, refs = refs[:parts], refs[parts:]
    do_refs, refs = refs[:parts], refs[parts:]
    if not second:
        first_refs, refs = refs[:parts], refs[parts:]
    out_refs, refs = refs[:parts], refs[parts:]
    do_ref, all_ref, dq_ref, dk_ref, dv_ref, delta_ref = refs
    rows, width = q_ref.shape
    heads = width // HEAD_DIM
    per = group // HEAD_DIM
    chunk = rows // parts
    small = min(block, chunk)
    step = pl.program_id(0)
    steps = rows // block
    seg_len = info_ref[0]
    place = info_ref[1]

    @pl.when(step == 0)
    def _():
        dq_ref[...] = jnp.zeros_like(dq_ref)
        head = lax.broadcasted_iota(jnp.int32, (8, width), 0)
        lane = lax.broadcasted_iota(jnp.int32, (8, width), 1)
        pick = jnp.where(lane // HEAD_DIM == head, 1.0, 0.0).astype(F32)
        for part in range(parts):
            for at in range(0, chunk, small):
                grads = do_refs[part][at : at + small, :]
                prod = grads.astype(F32) * o_refs[part][at : at + small, :].astype(F32)
                delta = lax.dot_general(
                    pick, prod, NT, precision=lax.Precision.HIGHEST, preferred_element_type=F32
                )
                if parts == 1:
                    target = at
                else:
                    target = jnp.bitwise_xor(part, place) * chunk + at
                target = pl.ds(pl.multiple_of(target, small), small)
                do_ref[target, :] = grads
                delta_ref[:, target] = delta
            if not second:
                all_ref[part * chunk : (part + 1) * chunk, 2 * width :] = first_refs[part][...]

    dk_ref[...] = jnp.zeros_like(dk_ref)
    dv_ref[...] = jnp.zeros_like(dv_ref)
    base = step * block

    def one(key_off, key_size, query_start, query_size, masked):
        key_rows = pl.ds(pl.multiple_of(base + key_off, strip), key_size)
        query_rows = pl.ds(pl.multiple_of(query_start, strip), query_size)
        for pair in range(heads // per):
            at = pair * group
            keys = k_ref[key_rows, at : at + group]
            values = v_ref[key_rows, at : at + group]
            queries = q_ref[query_rows, at : at + group]
            grads = do_ref[query_rows, at : at + group]
            dq = dk = dv = None
            for sub in range(per):
                head = pair * per + sub
                q_one = head_lanes(queries, head, group)
                do_one = head_lanes(grads, head, group)
                scores = mm(keys, q_one, NT)
                if masked:
                    r = lax.broadcasted_iota(jnp.int32, scores.shape, 0)
                    c = lax.broadcasted_iota(jnp.int32, scores.shape, 1)
                    scores = jnp.where(r <= c, scores, -1e30)
                probs = jnp.exp(scores - lse_ref[head : head + 1, query_rows])
                g_probs = mm(values, do_one, NT)
                g_scores = (probs * (g_probs - delta_ref[head : head + 1, query_rows])).astype(BF16)
                dv_one = mm(probs.astype(BF16), do_one)
                dk_one = mm(g_scores, q_one)
                dq_one = mm(g_scores, head_lanes(keys, head, group), TN)
                dq = dq_one if dq is None else dq + dq_one
                dk = dk_one if dk is None else dk + dk_one
                dv = dv_one if dv is None else dv + dv_one
            dq_ref[query_rows, at : at + group] += dq
            dk_ref[key_off : key_off + key_size, at : at + group] += dk
            dv_ref[key_off : key_off + key_size, at : at + group] += dv

    for off in range(0, block, strip):
        one(off, strip, base + off, block - off, True)

    per_seg = seg_len // block

    @pl.loop(step + 1, (step // per_seg + 1) * per_seg)
    def _(row):
        one(0, block, row * block, block, False)

    def turn_back(value, at_rows):
        return value * cos_ref[at_rows, :] - swap_halves(value) * sin_ref[at_rows, :]

    for off in range(0, block, small):
        here = pl.ds(pl.multiple_of(base + off, small), small)
        if parts == 1:
            target = base + off
        else:
            target = jnp.bitwise_xor(step * (block // chunk) + off // chunk, place) * chunk + off % chunk
        target = pl.ds(pl.multiple_of(target, small), small)
        for at in range(0, width, group):
            g_query = turn_back(dq_ref[here, at : at + group] * SCALE, here)
            g_key = turn_back(dk_ref[off : off + small, at : at + group], here)
            all_ref[target, at : at + group] = g_query.astype(BF16)
            all_ref[target, width + at : width + at + group] = g_key.astype(BF16)
        g_value = dv_ref[off : off + small, :]
        if second:
            g_value = 0.5 * g_value
        else:
            g_value = g_value + all_ref[target, 2 * width :].astype(F32)
        all_ref[target, 2 * width :] = g_value.astype(BF16)

    @pl.when(step == steps - 1)
    def _():
        for part in range(parts):
            out_refs[part][...] = all_ref[part * chunk : (part + 1) * chunk, :]


def attend_back(queries, keys, values, lse, cosine, sine, attended, grads, g_first, info):
    rows, width = queries.shape
    parts = len(attended)
    group = min(width, 128)
    heads = width // HEAD_DIM
    block = rows // 2
    chunk = rows // parts
    second = g_first is None
    whole = pl.BlockSpec((rows, width), lambda i, n: (0, 0))
    table = pl.BlockSpec((rows, group), lambda i, n: (0, 0))
    piece = pl.BlockSpec((chunk, width), lambda i, n: (0, 0))
    in_specs = [whole] * 3 + [pl.BlockSpec((heads, rows), lambda i, n: (0, 0)), table, table] + [piece] * (2 * parts)
    args = [queries, keys, values, lse, cosine, sine, *attended, *grads]
    if not second:
        values_at = 2 if width % 128 == 0 else 0
        if values_at == 0:
            g_first = [part[:, 2 * width :] for part in g_first]
        in_specs += [pl.BlockSpec((chunk, width), lambda i, n: (0, values_at))] * parts
        args += list(g_first)
    return pl.pallas_call(
        functools.partial(attend_back_kernel, second, block, min(256, block), group, parts),
        grid_spec=pltpu.PrefetchScalarGridSpec(
            num_scalar_prefetch=1,
            grid=(rows // block,),
            in_specs=in_specs,
            out_specs=[pl.BlockSpec((chunk, 3 * width), lambda i, n: (0, 0))] * parts,
            scratch_shapes=[
                pltpu.VMEM((rows, width), BF16),
                pltpu.VMEM((rows, 3 * width), BF16),
                pltpu.VMEM((rows, width), F32),
                pltpu.VMEM((block, width), F32),
                pltpu.VMEM((block, width), F32),
                pltpu.VMEM((8, rows), F32),
            ],
        ),
        out_shape=[jax.ShapeDtypeStruct((chunk, 3 * width), BF16)] * parts,
        compiler_params=pltpu.CompilerParams(vmem_limit_bytes=VMEM_BYTES),
        cost_estimate=cost(36),
        name="attend_back",
    )(info, *args)


def out_kernel(info_ref, own_ref, other_ref, state_ref, gain_ref, *refs):
    att_refs = refs[:-3]
    middle_ref, normed_ref, full_ref = refs[-3:]
    mp, out_half, model = own_ref.shape
    low_core = info_ref[2] == 0
    square = mp == 4
    for at in range(mp):
        source = jnp.bitwise_xor(at, info_ref[1]) if square else at
        own, other = own_ref[source], other_ref[source]
        base = at * 2 * out_half
        full_ref[base : base + out_half, :] = jnp.where(low_core, own, other)
        full_ref[base + out_half : base + 2 * out_half, :] = jnp.where(low_core, other, own)
    total = state_ref[...].astype(F32)
    size = mp * 2 * out_half // len(att_refs)
    for part, att_ref in enumerate(att_refs):
        total = total + mm(att_ref[...], full_ref[part * size : (part + 1) * size, :])
    middle_ref[...] = total
    normed_ref[...] = normalize(total, gain_ref[...]).astype(BF16)


def out_project(attended, own, other, state, gain, info):
    rows, model = state.shape
    mp, out_half = own.shape[:2]
    whole = pl.BlockSpec((rows, model), lambda i, n: (0, 0))
    share = pl.BlockSpec(own.shape, lambda i, n: (0, 0, 0))
    full = (mp * 2 * out_half, model)
    return pl.pallas_call(
        out_kernel,
        grid_spec=pltpu.PrefetchScalarGridSpec(
            num_scalar_prefetch=1,
            grid=(1,),
            in_specs=[share, share, whole, pl.BlockSpec((1, model), lambda i, n: (0, 0))]
            + [pl.BlockSpec(part.shape, lambda i, n: (0, 0)) for part in attended],
            out_specs=[whole, whole, pl.BlockSpec(full, lambda i, n: (0, 0))],
        ),
        out_shape=[
            jax.ShapeDtypeStruct((rows, model), F32),
            jax.ShapeDtypeStruct((rows, model), BF16),
            jax.ShapeDtypeStruct(full, BF16),
        ],
        compiler_params=pltpu.CompilerParams(vmem_limit_bytes=VMEM_BYTES),
        cost_estimate=cost(5),
        name="out_project",
    )(info, own, other, state, gain.reshape(1, model), *attended)


def weight_copies(pieces_ref, wide_ref, sems):
    count, hidden, model = wide_ref.shape
    mp = pieces_ref.shape[0]
    size = hidden // mp
    groups = []
    for at in range(count):
        copies = []
        for part in range(mp):
            copies.append(
                pltpu.make_async_copy(
                    pieces_ref.at[part, pl.ds(at * size, size), :],
                    wide_ref.at[at, pl.ds(part * size, size), :],
                    sems.at[at, part],
                )
            )
        groups.append(copies)
    return groups


def ffn_kernel(x_ref, base_ref, pieces_ref, out_ref, silu_ref, slope_ref, act_ref, wide_ref, sems):
    groups = weight_copies(pieces_ref, wide_ref, sems)
    for copies in groups:
        for copy in copies:
            copy.start()
    for copy in groups[0]:
        copy.wait()
    gate = mm(x_ref[...], wide_ref[0], NT)
    for copy in groups[1]:
        copy.wait()
    up = mm(x_ref[...], wide_ref[1], NT)
    sig = 0.5 + 0.5 * jnp.tanh(0.5 * gate)
    silu = gate * sig
    act = (silu * up).astype(BF16)
    silu_ref[...] = silu.astype(BF16)
    slope_ref[...] = (up * (sig + silu * (1.0 - sig))).astype(BF16)
    act_ref[...] = act
    for copy in groups[2]:
        copy.wait()
    out_ref[...] = base_ref[...] + mm(act, wide_ref[2])


def ffn_forward(normed, base, pieces, hidden):
    rows, model = normed.shape
    mp = pieces.shape[0]
    whole = pl.BlockSpec((rows, model), lambda j: (0, 0))
    inner = pl.BlockSpec((rows, hidden), lambda j: (0, 0))
    shape = jax.ShapeDtypeStruct((rows, hidden), BF16)
    return pl.pallas_call(
        ffn_kernel,
        grid=(1,),
        in_specs=[whole, whole, pl.BlockSpec(memory_space=pl.ANY)],
        out_specs=[whole, inner, inner, inner],
        out_shape=[jax.ShapeDtypeStruct((rows, model), F32), shape, shape, shape],
        scratch_shapes=[pltpu.VMEM((3, hidden, model), BF16), pltpu.SemaphoreType.DMA((3, mp))],
        compiler_params=pltpu.CompilerParams(vmem_limit_bytes=VMEM_BYTES),
        cost_estimate=cost(9),
        name="ffn",
    )(normed, base, pieces)


def ffn_back_kernel(more, *refs):
    if more:
        base_ref, refs = refs[0], refs[1:]
    g_ref, silu_ref, slope_ref, pieces_ref, out_ref, g_gate_ref, g_up_ref, wide_ref, sems = refs
    groups = weight_copies(pieces_ref, wide_ref, sems)
    for at in (2, 0, 1):
        for copy in groups[at]:
            copy.start()
    for copy in groups[2]:
        copy.wait()
    g_act = mm(g_ref[...], wide_ref[2], NT)
    g_up = (g_act * silu_ref[...].astype(F32)).astype(BF16)
    g_gate = (g_act * slope_ref[...].astype(F32)).astype(BF16)
    g_gate_ref[...] = g_gate
    g_up_ref[...] = g_up
    for copy in groups[0]:
        copy.wait()
    total = mm(g_gate, wide_ref[0])
    for copy in groups[1]:
        copy.wait()
    total = total + mm(g_up, wide_ref[1])
    out_ref[...] = base_ref[...] + total if more else total


def ffn_backward(g_branch, base, silu, slope, pieces):
    rows, model = g_branch.shape
    hidden = silu.shape[1]
    mp = pieces.shape[0]
    whole = pl.BlockSpec((rows, model), lambda j: (0, 0))
    inner = pl.BlockSpec((rows, hidden), lambda j: (0, 0))
    shape = jax.ShapeDtypeStruct((rows, hidden), BF16)
    more = base is not None
    args = [g_branch, silu, slope, pieces]
    in_specs = [whole, inner, inner, pl.BlockSpec(memory_space=pl.ANY)]
    if more:
        args, in_specs = [base] + args, [whole] + in_specs
    return pl.pallas_call(
        functools.partial(ffn_back_kernel, more),
        grid=(1,),
        in_specs=in_specs,
        out_specs=[whole, inner, inner],
        out_shape=[jax.ShapeDtypeStruct((rows, model), F32), shape, shape],
        scratch_shapes=[pltpu.VMEM((3, hidden, model), BF16), pltpu.SemaphoreType.DMA((3, mp))],
        compiler_params=pltpu.CompilerParams(vmem_limit_bytes=VMEM_BYTES),
        cost_estimate=cost(1),
        name="ffn_back",
    )(*args)


def pack_grads_kernel(size, plain, halves, info_ref, *refs):
    gate, got_gate, up, got_up, act, got_act, x_ref, got_x, g_ref, got_g, out_grad = refs[:11]
    out_refs = refs[11:]
    pack_ref = out_refs[-1]
    count = pack_ref.shape[0]
    jobs = ((gate, x_ref, got_gate, got_x), (up, x_ref, got_up, got_x), (act, g_ref, got_act, got_g))
    for at, (left, right, left_two, right_two) in enumerate(jobs):
        acc = mm(left[...], right[...], TN) + mm(left_two[...], right_two[...], TN)
        for part in range(count):
            pack_ref[part, at * size : (at + 1) * size, :] = acc[part * size : (part + 1) * size].astype(BF16)
    for part in range(count):
        pack_ref[part, 3 * size :, :] = out_grad[part]
    if plain:
        out_refs[0][...] = pack_ref[:, :plain, :]
        out_refs = out_refs[1:]
    if halves:
        cut = plain + halves

        @pl.when(info_ref[0] == 0)
        def _():
            out_refs[0][...] = pack_ref[:, plain:cut, :]
            out_refs[1][...] = pack_ref[:, cut:, :]

        @pl.when(info_ref[0] == 1)
        def _():
            out_refs[0][...] = pack_ref[:, cut:, :]
            out_refs[1][...] = pack_ref[:, plain:cut, :]


def pack_grads(inner, got_inner, normed, got_normed, g_branch, got_branch, out_grad, plain, first):
    rows, model = normed.shape
    hidden = inner[0].shape[1]
    mp, out_half = out_grad.shape[:2]
    size = hidden // mp
    block = min(512, model)
    left = pl.BlockSpec((rows, hidden), lambda j, n: (0, 0))
    right = pl.BlockSpec((rows, block), lambda j, n: (0, j))
    pack_rows = 3 * size + out_half
    args = []
    for own, got in zip(inner, got_inner):
        args += [own, got]
    halves = (pack_rows - plain) // 2
    if halves == 0:
        plain, sizes, scratch = 0, [pack_rows], []
    else:
        sizes = ([plain] if plain else []) + [halves, halves]
        scratch = [pltpu.VMEM((mp, pack_rows, block), BF16)]
    return pl.pallas_call(
        functools.partial(pack_grads_kernel, size, plain, halves),
        grid_spec=pltpu.PrefetchScalarGridSpec(
            num_scalar_prefetch=1,
            grid=(model // block,),
            in_specs=[left] * 6
            + [right] * 4
            + [pl.BlockSpec((mp, out_half, block), lambda j, n: (0, 0, j))],
            out_specs=[pl.BlockSpec((mp, part, block), lambda j, n: (0, 0, j)) for part in sizes],
            scratch_shapes=scratch,
        ),
        out_shape=[jax.ShapeDtypeStruct((mp, part, model), BF16) for part in sizes],
        compiler_params=pltpu.CompilerParams(vmem_limit_bytes=VMEM_BYTES),
        cost_estimate=cost(15),
        name="pack_grads",
    )(first.astype(jnp.int32).reshape(1), *args, normed, got_normed, g_branch, got_branch, out_grad)


def place_kernel(which_ref, first_ref, second_ref, out_ref):
    @pl.when(pl.program_id(0) == 0)
    def _():
        out_ref[...] = first_ref[...]

    @pl.when(pl.program_id(0) == 1)
    def _():
        out_ref[...] = second_ref[...]


def place_two(first, second, which, axis):
    rows, model = first.shape
    if (rows, model)[axis] % (16, 128)[axis]:
        ordered = jnp.where(which == 0, first, second), jnp.where(which == 0, second, first)
        return jnp.concatenate(ordered, axis=axis)
    whole = pl.BlockSpec((rows, model), lambda i, w: (0, 0))

    def target(i, w):
        spot = jnp.bitwise_xor(w[0], i)
        return (spot, 0) if axis == 0 else (0, spot)

    shape = (2 * rows, model) if axis == 0 else (rows, 2 * model)
    return pl.pallas_call(
        place_kernel,
        grid_spec=pltpu.PrefetchScalarGridSpec(
            num_scalar_prefetch=1,
            grid=(2,),
            in_specs=[whole, whole],
            out_specs=pl.BlockSpec((rows, model), target),
        ),
        out_shape=jax.ShapeDtypeStruct(shape, first.dtype),
        compiler_params=pltpu.CompilerParams(vmem_limit_bytes=VMEM_BYTES),
        cost_estimate=cost(2),
        name="place_two",
    )(which.astype(jnp.int32).reshape(1), first, second)


def qkv_grad_kernel(count, *refs):
    out_ref = refs[-1]
    acc = None
    at = 0
    whole = count
    grads = refs[whole:-1]
    part = 0
    for i in range(count):
        size = refs[i].shape[0]
        chunk = grads[part].shape[0]
        product = mm(refs[i][...], grads[part][at : at + size, :], TN)
        acc = product if acc is None else acc + product
        at += size
        if at == chunk:
            at, part = 0, part + 1
    out_ref[...] = acc.astype(BF16)


def qkv_grad_sum(pieces, grads):
    model = pieces[0].shape[1]
    width = grads[0].shape[1]
    block = min(512, model)
    return pl.pallas_call(
        functools.partial(qkv_grad_kernel, len(pieces)),
        grid=(model // block,),
        in_specs=[pl.BlockSpec((piece.shape[0], block), lambda i: (0, i)) for piece in pieces]
        + [pl.BlockSpec(part.shape, lambda i: (0, 0)) for part in grads],
        out_specs=pl.BlockSpec((block, width), lambda i: (i, 0)),
        out_shape=jax.ShapeDtypeStruct((model, width), BF16),
        compiler_params=pltpu.CompilerParams(vmem_limit_bytes=VMEM_BYTES),
        cost_estimate=cost(7),
        name="qkv_grad",
    )(*pieces, *grads)


def normalize(rows_in, gain):
    scale = lax.rsqrt(jnp.mean(rows_in * rows_in, axis=-1, keepdims=True) + EPS)
    return rows_in * scale * gain


def normalize_back(rows_in, gain, grad):
    scale = lax.rsqrt(jnp.mean(rows_in * rows_in, axis=-1, keepdims=True) + EPS)
    gained = grad * gain
    inner = jnp.mean(gained * rows_in, axis=-1, keepdims=True)
    g_rows = scale * (gained - rows_in * (scale * scale * inner))
    return g_rows, jnp.sum(grad * (rows_in * scale), axis=0)


def rotary_tables(rows, seg_len, lanes):
    positions = (jnp.arange(rows, dtype=jnp.int32) % seg_len).astype(F32)
    inverse_freq = 10000.0 ** (-(jnp.arange(HALF, dtype=F32) * 2.0 / HEAD_DIM))
    angles = positions[:, None] * inverse_freq[None, :]
    cosine, sine = jnp.cos(angles), jnp.sin(angles)
    cosine = jnp.concatenate([cosine, cosine] * (lanes // HEAD_DIM), axis=1)
    sine = jnp.concatenate([-sine, sine] * (lanes // HEAD_DIM), axis=1)
    return cosine, sine


def swap_cores(value):
    return lax.ppermute(value, "section", [(0, 1), (1, 0)])


def across(value, axis, bits):
    return lax.ppermute(value, axis, [(i, i ^ bits) for i in range(lax.axis_size(axis))])


def is_square():
    return lax.axis_size("mp") == 4


def spread_rows(value):
    if not is_square():
        return [[lax.all_gather(value, "mp", axis=0, tiled=True)]]
    half = value.shape[0] // 2
    from_x, from_y = across(value, "mp", 1), across(value, "mp", 2)
    far_low, far_high = across(from_y[:half], "mp", 1), across(from_x[half:], "mp", 2)
    return [[value], [from_x], [from_y], [far_low, far_high]]


def sum_rows_to_owner(parts):
    if not is_square():
        total = lax.psum_scatter(jnp.concatenate(parts, axis=0), "mp", scatter_dimension=0, tiled=True)
        return total.astype(F32)
    half = parts[0].shape[0] // 2
    own, to_x, to_y, to_far = parts
    far_low = across(to_far[:half], "mp", 1)
    far_high = across(to_far[half:], "mp", 2)
    x_low = across(to_x[:half], "mp", 1)
    y_high = across(to_y[half:], "mp", 2)
    passed_x = (to_x[half:].astype(F32) + far_high.astype(F32)).astype(BF16)
    passed_y = (to_y[:half].astype(F32) + far_low.astype(F32)).astype(BF16)
    x_high = across(passed_x, "mp", 1)
    y_low = across(passed_y, "mp", 2)
    own = own.astype(F32)
    low = own[:half] + x_low.astype(F32) + y_low.astype(F32)
    high = own[half:] + x_high.astype(F32) + y_high.astype(F32)
    return jnp.concatenate([low, high], axis=0)


def group_steps():
    return 4 if lax.axis_size("dp") == 4 else 1


def sum_groups_step(step, state):
    if lax.axis_size("dp") != 4:
        return (lax.psum(state[0], "dp"), None)
    index = lax.axis_index("dp")
    low, high = index % 2, index // 2
    kept, got = state
    bits, which = ((1, low), (2, high), (2, high), (1, low))[step]
    if step < 2:
        whole = kept if got is None else (kept.astype(F32) + got.astype(F32)).astype(BF16)
        size = whole.shape[1] // 2
        kept = lax.dynamic_slice_in_dim(whole, which * size, size, 1)
        sent = lax.dynamic_slice_in_dim(whole, (1 - which) * size, size, 1)
        return kept, across(sent, "dp", bits)
    if step == 2:
        whole = (kept.astype(F32) + got.astype(F32)).astype(BF16)
    else:
        whole = place_two(kept, got, high, 1)
    return whole, across(whole, "dp", bits)


def sum_groups_end(state):
    if lax.axis_size("dp") != 4:
        return state[0]
    return place_two(state[0], state[1], lax.axis_index("dp") % 2, 1)


def sum_groups(value, state=None, start=0):
    if state is None:
        state = (value, None)
    for step in range(start, group_steps()):
        state = sum_groups_step(step, state)
    return sum_groups_end(state)


def add_low(left, right):
    return (left.astype(F32) + right.astype(F32)).astype(BF16)


def scatter_parts(parts):
    rows = parts.reshape(-1, parts.shape[2])
    return lax.psum_scatter(rows, "mp", scatter_dimension=0, tiled=True)


class Chain:
    def __init__(self, state, steps, last):
        self.state, self.steps, self.last = state, list(steps), last

    def tie(self, value):
        if self.steps:
            value, self.state = lax.optimization_barrier((value, self.state))
            self.state = self.steps.pop(0)(self.state)
        return value

    def end(self):
        while self.steps:
            self.state = self.steps.pop(0)(self.state)
        return self.last(self.state)


def groups_chain(parts):
    steps = [lambda state: sum_groups_step(0, (state, None))]
    steps += [functools.partial(sum_groups_step, step) for step in range(1, group_steps())]
    return Chain(scatter_parts(parts), steps, sum_groups_end)


def waiting_chain(value):
    steps = [lambda state: sum_groups_step(0, (state, None))]
    steps += [functools.partial(sum_groups_step, step) for step in range(1, group_steps())]
    return Chain(value, steps, sum_groups_end)


def plain_chain(value):
    steps = [functools.partial(sum_groups_step, step) for step in range(1, group_steps())]
    return Chain(sum_groups_step(0, (value, None)), steps, sum_groups_end)


def halves_chain(kept, sent):
    steps = [
        lambda state: scatter_parts(add_low(*state)),
        lambda state: (state, across(state, "dp", 2)),
        lambda state: (lambda total: (total, across(total, "dp", 1)))(add_low(*state)),
    ]
    return Chain(
        (kept, across(sent, "dp", 1)),
        steps,
        lambda state: place_two(state[0], state[1], lax.axis_index("dp") % 2, 0),
    )


def by_distance(blocks, place):
    if not is_square():
        return blocks
    blocks = jnp.where(place % 2 == 0, blocks, jnp.stack([blocks[i] for i in (1, 0, 3, 2)]))
    return jnp.where(place < 2, blocks, jnp.stack([blocks[i] for i in (2, 3, 0, 1)]))


def sum_all(value):
    if not is_square() or lax.axis_size("dp") != 4:
        return lax.psum(value, ("section", "dp", "mp"))
    value = value + across(value, "section", 1)
    for axis in ("mp", "dp"):
        for bits in (1, 2):
            value = value + across(value, axis, bits)
    return value


def pick_half(value, which, axis=0):
    size = value.shape[axis] // 2
    return lax.dynamic_slice_in_dim(value, which * size, size, axis)


def shards(
    tokens,
    layout,
    cotangent,
    attn_gain,
    query_weight,
    key_weight,
    value_weight,
    out_weight,
    ffn_gain,
    gate_weight,
    up_weight,
    down_weight,
):
    core = lax.axis_index("section")
    is_low = core == 0
    micro_count, tok_rows, model = tokens.shape
    mp = lax.axis_size("mp")
    place = lax.axis_index("mp").astype(jnp.int32)
    square = is_square()
    parts = mp if square else 1
    seq_rows = tok_rows * mp
    width = query_weight.shape[2]
    hidden = gate_weight.shape[2]
    hid_half = hidden // 2
    out_half = width // 2
    group = min(width, 128)

    def in_order(own, other):
        return jnp.where(is_low, own, other), jnp.where(is_low, other, own)

    inputs = lax.dynamic_index_in_dim(tokens, core, 0, keepdims=False)
    g_top = lax.dynamic_index_in_dim(cotangent, core, 0, keepdims=False)
    pack_layout = lax.dynamic_index_in_dim(layout[:, 0], core, 0, keepdims=False)
    seg_len = (seq_rows // pack_layout).astype(jnp.int32)
    info = jnp.stack([seg_len, place, core.astype(jnp.int32)])
    cosine, sine = rotary_tables(seq_rows, seg_len, group)

    own_qkv = jnp.concatenate([query_weight[0], key_weight[0], value_weight[0]], axis=1)
    qkv_weights = in_order(own_qkv, swap_cores(own_qkv))
    gains = jnp.concatenate([attn_gain, ffn_gain], axis=0)
    layer_gains = in_order(gains, swap_cores(gains))

    first_normed = normalize(inputs.astype(F32), layer_gains[0][0]).astype(BF16)
    first_normed, gate_weight, up_weight, down_weight, out_weight = lax.optimization_barrier(
        (first_normed, gate_weight, up_weight, down_weight, out_weight)
    )
    halves = jnp.concatenate(
        [
            gate_weight[0].T.reshape(2, hid_half, model),
            up_weight[0].T.reshape(2, hid_half, model),
            down_weight[0].reshape(2, hid_half, model),
            out_weight[0].reshape(2, out_half, model),
        ],
        axis=1,
    )
    kept = lax.dynamic_index_in_dim(halves, core, 0, keepdims=False)
    sent = lax.dynamic_index_in_dim(halves, 1 - core, 0, keepdims=False)
    packs = in_order(kept, swap_cores(sent))
    pack_rows = packs[0].shape[0]

    all_pieces = [lax.all_gather(pack, "mp", axis=0, tiled=False) for pack in packs]

    hid_all = mp * hid_half

    def whole_rows(pieces):
        if hid_half % 16 == 0:
            return pieces
        starts = [i * hid_half for i in range(3)]
        parts = [pieces[:, at : at + hid_half].reshape(hid_all, model) for at in starts]
        return jnp.concatenate(parts, axis=0)[None]

    def to_owners(attended):
        if not square:
            blocks = attended[0].reshape(mp, tok_rows, width)
            moved = lax.all_to_all(blocks, "mp", 0, 0)
            return [jnp.transpose(moved, (1, 0, 2)).reshape(tok_rows, mp * width)]
        moved = {i: across(attended[i], "mp", i) for i in (3, 1, 2)}
        return [attended[0], moved[1], moved[2], moved[3]]

    def to_heads(value):
        if not square:
            blocks = jnp.transpose(value.reshape(tok_rows, mp, width), (1, 0, 2))
            return [lax.all_to_all(blocks, "mp", 0, 0).reshape(seq_rows, width)]
        blocks = [value[:, i * width : (i + 1) * width] for i in range(mp)]
        moved = {i: across(blocks[i], "mp", i) for i in (3, 1, 2)}
        return [blocks[0], moved[1], moved[2], moved[3]]

    def forward(rows_low, first, weights, normed=None):
        gain_a, gain_f, qkv_w, pieces_w = weights
        state = rows_low.astype(F32)
        if normed is None:
            normed = normalize(state, gain_a).astype(BF16)
        pieces = spread_rows(normed)
        held = None
        for index, piece in enumerate(pieces):
            spot = jnp.bitwise_xor(place, index) if square else jnp.int32(0)
            held = project_qkv(piece, spot.reshape(1), qkv_w, cosine, sine, first, held)
        queries, keys, values = held
        attended, lse = attend(queries, keys, values, info, parts)
        attended, pieces_w = lax.optimization_barrier((attended, pieces_w))
        out_own = pieces_w[:, 3 * hid_half :]
        out_other = swap_cores(out_own)
        own, other = whole_rows(pieces_w), whole_rows(swap_cores(pieces_w))
        att_rows = to_owners(attended)
        middle, normed_ffn, out_full = out_project(att_rows, out_own, out_other, rows_low, gain_f, info)
        result = middle
        inner = []
        for share in (own, other):
            result, silu, slope, activated = ffn_forward(normed_ffn, result, share, hid_all)
            inner.append((silu, slope, activated))
        flat = [part for piece in pieces for part in piece]
        kept_items = (state, flat, queries, keys, values, attended, lse, att_rows, middle, normed_ffn, inner)
        kept_items += (own, other, out_full)
        return result.astype(BF16), values, kept_items

    split = square and lax.axis_size("dp") == 4
    plain_rows = {False: pack_rows, True: pack_rows}
    if split:
        plain_rows = {False: 0, True: pack_rows // 64 * 32 + 32}

    def tied(chains, value):
        for chain in chains:
            value = chain.tie(value)
        return value

    def backward(g_result, g_first, weights, kept_items, earlier=()):
        late = len(earlier) > 0

        gain_a, gain_f, qkv_w, unused = weights
        state, pieces, queries, keys, values, attended, lse, att_rows, middle, normed_ffn, inner = kept_items[:11]
        own, other, out_full = kept_items[11:]
        g_branch = g_result.astype(BF16)
        got_normed, got_branch, got_act = swap_cores(normed_ffn), swap_cores(g_branch), swap_cores(inner[1][2])
        g_normed = None
        g_inner = []
        for (silu, slope, activated), share in zip(inner, (own, other)):
            g_normed, g_gate, g_up = ffn_backward(g_branch, g_normed, silu, slope, share)
            g_inner.append((g_gate, g_up, activated))
        got_gate, got_up = swap_cores(g_inner[1][0]), swap_cores(g_inner[1][1])
        if late:
            g_normed = tied(earlier[0], g_normed)
        g_norm, g_gain_f = normalize_back(middle, gain_f, g_normed)
        g_middle = g_result + g_norm
        g_mid_low = g_middle.astype(BF16)
        g_att_rows = mm(g_mid_low, out_full, NT).astype(BF16)
        g_att_rows, got_gate, got_up = lax.optimization_barrier((g_att_rows, got_gate, got_up))
        g_att = to_heads(g_att_rows)

        def make_packs():
            att_whole = jnp.concatenate(att_rows, axis=1)
            out_grad = mm(att_whole, g_mid_low, TN).astype(BF16).reshape(mp, 2, out_half, model)
            out_kept = lax.dynamic_index_in_dim(out_grad, core, 1, keepdims=False)
            out_sent = lax.dynamic_index_in_dim(out_grad, 1 - core, 1, keepdims=False)
            out_grad = (out_kept.astype(F32) + swap_cores(out_sent).astype(F32)).astype(BF16)
            return pack_grads(
                g_inner[0],
                (got_gate, got_up, got_act),
                normed_ffn,
                got_normed,
                g_branch,
                got_branch,
                by_distance(out_grad, place),
                plain_rows[late],
                lax.axis_index("dp") % 2,
            )

        if not late:
            hidden_packs = make_packs()
            g_att, hidden_packs = lax.optimization_barrier((g_att, hidden_packs))
        if late:
            g_att = tied(earlier[1], g_att)
        g_qkv = attend_back(queries, keys, values, lse, cosine, sine, attended, g_att, g_first, info)
        packs = hidden_packs if not late else make_packs()
        own_chains = [groups_chain(packs[0])] if len(packs) != 2 else []
        if split:
            own_chains.append(halves_chain(packs[-2], packs[-1]))
        if late:
            g_qkv = tied(earlier[2] + own_chains[:1], g_qkv)
        g_parts = [mm(part, qkv_w, NT).astype(BF16) for part in g_qkv]
        if not square:
            g_parts = [g_parts[0][i * tok_rows : (i + 1) * tok_rows] for i in range(mp)]
        g_rows = tied(earlier[3] if late else (), sum_rows_to_owner(g_parts))
        g_norm, g_gain_a = normalize_back(state, gain_a, g_rows)
        g_inputs = g_middle + g_norm
        qkv_grad = qkv_grad_sum(pieces, tied(own_chains[1:], g_qkv) if late else g_qkv)
        qkv_grad = pick_half(qkv_grad, core).astype(F32) + swap_cores(pick_half(qkv_grad, 1 - core)).astype(F32)
        qkv_grad = qkv_grad.reshape(-1, model).astype(BF16)
        if late:
            qkv_grad = plain_chain(qkv_grad)
        else:
            qkv_grad = waiting_chain(qkv_grad)
        return g_inputs, g_qkv, (own_chains, qkv_grad, g_gain_a, g_gain_f)

    layers = [
        (layer_gains[i][0], layer_gains[i][1], qkv_weights[i], all_pieces[i]) for i in range(2)
    ]
    h_first, first_values, kept_first = forward(inputs, None, layers[0], first_normed)
    h_second, unused, kept_second = forward(h_first, first_values, layers[1])
    g_second, g_qkv_second, grads_second = backward(g_top, None, layers[1], kept_second)
    chains = grads_second[0]
    g_tokens, unused, grads_first = backward(
        g_second.astype(BF16).astype(F32),
        g_qkv_second,
        layers[0],
        kept_first,
        (chains, chains + [grads_second[1]], [], chains + [grads_second[1]]),
    )

    def ended(chains):
        return jnp.concatenate([chain.end() for chain in chains], axis=0)

    totals_first = (ended(grads_first[0]), grads_first[1].end())
    totals_second = (ended(grads_second[0]), grads_second[1].end())

    def by_layer(low, high, wire):
        mine = jnp.where(is_low, low, high)
        theirs = swap_cores(jnp.where(is_low, high, low).astype(wire)).astype(mine.dtype)
        return in_order(mine, theirs)

    layer_out = jnp.stack(by_layer(h_first, h_second, BF16))
    input_grads = jnp.stack(by_layer(g_tokens, g_second, BF16))
    all_first = jnp.stack(in_order(first_values, swap_cores(first_values)))

    low, high = by_layer(totals_first[0], totals_second[0], BF16)
    qkv_low, qkv_high = by_layer(totals_first[1], totals_second[1], BF16)

    def joined(start, size):
        return jnp.concatenate([low[start : start + size], high[start : start + size]], axis=0).astype(F32)

    gate_grad = joined(0, hid_half)
    up_grad = joined(hid_half, hid_half)
    down_grad = joined(2 * hid_half, hid_half)
    out_grad = joined(3 * hid_half, out_half)
    qkv_grad = jnp.concatenate([qkv_low, qkv_high], axis=0).astype(F32).reshape(model, 3 * width)

    heads_here = width // HEAD_DIM
    first_f32 = first_values.astype(F32).reshape(seq_rows, heads_here, HEAD_DIM)
    squares = jnp.sum(first_f32 * first_f32, axis=(0, 2))
    placed = lax.dynamic_update_slice(
        jnp.zeros((micro_count, heads_here * mp), F32), squares[None], (core, place * heads_here)
    )
    sums = [grads_first[2], grads_second[2], grads_first[3], grads_second[3], placed.reshape(-1)]
    sums = sum_all(jnp.concatenate(sums))
    gain_grads = sums[: 4 * model].reshape(4, model)
    value_norms = sums[4 * model :].reshape(placed.shape)
    attn_gain_grad = lax.dynamic_slice_in_dim(gain_grads, core, 1, 0)
    ffn_gain_grad = lax.dynamic_slice_in_dim(gain_grads, 2 + core, 1, 0)
    return (
        layer_out[None],
        input_grads[None],
        all_first,
        value_norms,
        attn_gain_grad,
        qkv_grad[:, :width][None],
        qkv_grad[:, width : 2 * width][None],
        qkv_grad[:, 2 * width :][None],
        out_grad[None],
        ffn_gain_grad,
        gate_grad.T[None],
        up_grad.T[None],
        down_grad[None],
    )


def solution(mesh):
    in_specs = (
        P(None, ("dp", "mp"), None),
        P(None, "dp"),
        P(None, ("dp", "mp"), None),
        P("section", None),
        P("section", None, "mp"),
        P("section", None, "mp"),
        P("section", None, "mp"),
        P("section", "mp", None),
        P("section", None),
        P("section", None, "mp"),
        P("section", None, "mp"),
        P("section", "mp", None),
    )
    out_specs = (
        P("section", None, ("dp", "mp"), None),
        P("section", None, ("dp", "mp"), None),
        P(None, "dp", "mp"),
        P(),
        P("section", None),
        P("section", None, "mp"),
        P("section", None, "mp"),
        P("section", None, "mp"),
        P("section", "mp", None),
        P("section", None),
        P("section", None, "mp"),
        P("section", None, "mp"),
        P("section", "mp", None),
    )
    return jax.shard_map(shards, mesh=mesh, in_specs=in_specs, out_specs=out_specs, check_vma=False)
```
